128 devices in a mesh: rows: 16 (over y, z), seq: 8 (over x, core).
Axes of the slice: x: 4, y: 4, z: 4, core: 2. Of those that a mesh axis runs over, the one named last changes fastest.
Arguments:
- residual_in: bfloat16 [16, 2048, 3200], P('rows', 'seq'), may hold values from -6 to 6
- norm_gain: float32 [3200], replicated, may hold values from 0.1 to 1.9
- qkv_weight: bfloat16 [3200, 6144], P(None, 'seq')
- qk_gain: float32 [2, 2048], P(None, 'seq')
- out_weight: bfloat16 [2048, 3200], P('seq'), may hold values from -0.125 to 0.125
- layer_scale: float32 [3200], replicated, may hold values from 1 to 6
- segment_ids: int32 [16, 2048], P('rows', 'seq'), may hold values from 0 to 2, as said below
- pad_mask: int32 [16, 2048], P('rows', 'seq'), may hold values from 0 to 1, as said below
- ln_weight: float32 [12800], replicated, may hold values from 0.1 to 1.9
- ln_bias: float32 [12800], replicated, may hold values from -3 to 3
- fc_weight: bfloat16 [12800, 6144], P('rows'), may hold values from -0.0546875 to 0.0546875
- fc_bias: float32 [6144], replicated, may hold values from -3 to 3
- owner: int32 [16], replicated, may hold values from 0 to 15, each once
Outputs:
- features: bfloat16 [16, 512, 6144], P('rows', 'seq')
The draws below stay inside these ranges and needn't reach their ends.
Inputs may be any that keep to these rules, and one draw needn't show every extreme that they name: `segment_ids`: within a row, segment ids never fall and change only at multiples of 1024 tokens; picture tokens carry ids below 2, padding tokens carry 2 and stand at the end of the row; the first tile is never padding. pad_mask is 0 exactly where segment_ids equals 2. `owner`: each index of rows owns exactly one row.
All inputs are finite; a program needn't handle non-finite values.
Results may differ from the reference program's by a relative error of at most 0.025.
Values may be sent and summed in bfloat16 or wider, within the bound.
A program may use at most 128 MiB of HBM per device.

```python
import math
import jax
import jax.numpy as jnp
from jax import lax

D = 3200
HEAD_DIM = 128
HID = 6144
HEADS = 16
GRID = 32
ROW_TOK = 2048
ROWS = 16
N_ROWS = 16
N_SEQ = 8


def packing(key):
    tile_count = ROW_TOK // (GRID * GRID)
    first_key = jax.random.fold_in(key, 11)
    second_key = jax.random.fold_in(key, 12)
    third_key = jax.random.fold_in(key, 13)
    cut_bits = jax.random.randint(first_key, (ROWS, tile_count), 0, 2)
    cut_bits = cut_bits.at[:, 0].set(0)
    picture = jnp.cumsum(cut_bits, axis=1)
    pad_tiles = jax.random.randint(second_key, (ROWS,), 0, tile_count)
    chosen = jax.random.randint(third_key, (), 0, ROWS)
    pad_tiles = jnp.where(jnp.arange(ROWS) == chosen, tile_count - 1, pad_tiles)
    tile_index = jnp.arange(tile_count)
    padded = tile_index[None, :] >= (tile_count - pad_tiles)[:, None]
    seg_tile = jnp.where(padded, tile_count, picture).astype(jnp.int32)
    valid = jnp.where(padded, 0, 1).astype(jnp.int32)
    return (jnp.repeat(seg_tile, GRID * GRID, axis=1), jnp.repeat(valid, GRID * GRID, axis=1))


def draw_segment_ids(key, part):
    return packing(key)[0]


def draw_pad_mask(key, part):
    return packing(key)[1]


def draw_qkv_weight(key, part):
    base_draw = jax.random.normal(jax.random.fold_in(key, 21), (D, HEADS, 3, HEAD_DIM), jnp.float32) * D ** (-0.5)
    head_scale = 3.0 ** (jnp.arange(HEADS, dtype=jnp.float32) / max(HEADS - 1, 1))
    wobble = jnp.exp(jax.random.uniform(jax.random.fold_in(key, 22), (HEADS,), jnp.float32, -0.2, 0.2))
    factor = jnp.stack([head_scale * wobble, head_scale * wobble, jnp.ones((HEADS,), jnp.float32)], axis=1)
    weights = base_draw * factor[None, :, :, None]
    return weights.reshape(D, HEADS * 3 * HEAD_DIM).astype(jnp.bfloat16)


def draw_qk_gain(key, part):
    gain_draw = jnp.exp(jax.random.uniform(jax.random.fold_in(key, 31), (2, HEADS, HEAD_DIM), jnp.float32, math.log(0.8), math.log(2.2)))
    return gain_draw.reshape(2, HEADS * HEAD_DIM)


def block_levels(own_key, shape, cuts, low, top_value):
    factor_of, own = 1.0, jax.random.fold_in(own_key, 6)
    for dim, shards_of in cuts:
        draws = jnp.exp(jax.random.uniform(jax.random.fold_in(own, dim), (shards_of,), jnp.float32, low / len(cuts), top_value / len(cuts)))
        factor_of = factor_of * jnp.repeat(draws, shape[dim] // shards_of).reshape([-1 if axis == dim else 1 for axis in range(len(shape))])
    return factor_of


def scatter_about(stream_key, dims, scale, limit, split=(), kind=jnp.bfloat16):
    array = scale * jax.random.normal(stream_key, dims, jnp.float32)
    if split:
        array = array * block_levels(stream_key, dims, split, -0.22, 0.18)
    return jnp.clip(array, -limit, limit).astype(kind)


def setup_inputs(seed: int = 0) -> dict:
    streams_of = jax.random.split(jax.random.key(seed), 14)
    return {
        "residual_in": scatter_about(streams_of[0], (ROWS, ROW_TOK, D), 1.0, 6.0, ((0, 16), (1, 8))),
        "norm_gain": jnp.clip(1.0 + 0.18 * jax.random.normal(streams_of[1], (D,), jnp.float32), 0.1, 1.9),
        "qkv_weight": draw_qkv_weight(jax.random.fold_in(streams_of[13], 71), 0),
        "qk_gain": draw_qk_gain(jax.random.fold_in(streams_of[13], 71), 0),
        "out_weight": scatter_about(streams_of[4], (HEADS * HEAD_DIM, D), (HEADS * HEAD_DIM) ** -0.5, 0.125, ((0, 8),)),
        "layer_scale": jnp.clip(jnp.exp(jax.random.uniform(streams_of[5], (D,), jnp.float32, math.log(1.0), math.log(6.0))), 1.0, 6.0),
        "segment_ids": draw_segment_ids(jax.random.fold_in(streams_of[13], 71), 0),
        "pad_mask": draw_pad_mask(jax.random.fold_in(streams_of[13], 71), 0),
        "ln_weight": jnp.clip(1.0 + 0.18 * jax.random.normal(streams_of[8], (4 * D,), jnp.float32), 0.1, 1.9),
        "ln_bias": scatter_about(streams_of[9], (4 * D,), 0.5, 3.0, (), jnp.float32),
        "fc_weight": scatter_about(streams_of[10], (4 * D, HID), (4 * D) ** -0.5, 0.0546875, ((0, 16),)),
        "fc_bias": scatter_about(streams_of[11], (HID,), 0.5, 3.0, (), jnp.float32),
        "owner": jax.random.permutation(streams_of[12], ROWS).astype(jnp.int32),
    }


def rounded_sum(left_parts, right_parts):

    def add_group(carry, pair):
        left, right = pair
        term = jnp.dot(left, right, preferred_element_type=jnp.float32).astype(jnp.bfloat16)
        term = lax.optimization_barrier(term)
        return (carry + term.astype(jnp.float32), None)
    start = jnp.zeros((left_parts.shape[1], right_parts.shape[2]), jnp.float32)
    result, _ = lax.scan(add_group, start, (left_parts, right_parts))
    return result

def reference(residual_in, norm_gain, qkv_weight, qk_gain, out_weight, layer_scale, segment_ids, pad_mask, ln_weight, ln_bias, fc_weight, fc_bias, owner):
    row_len = ROW_TOK
    norm_width = HEADS * HEAD_DIM
    group_width = norm_width // N_SEQ
    slab_width = 4 * D // N_ROWS
    half_grid = GRID // 2
    lines = row_len // (2 * GRID)
    scale = HEAD_DIM ** (-0.5)

    def one_row(packed):
        row_x, row_seg, row_mask = packed
        tokens = row_x.astype(jnp.float32)
        normed = (tokens * lax.rsqrt(lax.optimization_barrier(jnp.mean(tokens * tokens, axis=-1, keepdims=True)) + 1e-06) * norm_gain).astype(jnp.bfloat16)
        projected = jnp.dot(normed, qkv_weight, preferred_element_type=jnp.float32).reshape(row_len, HEADS, 3, HEAD_DIM)
        query_raw = projected[:, :, 0]
        key_raw = projected[:, :, 1]
        value_half = projected[:, :, 2].astype(jnp.bfloat16)
        query_gain = qk_gain[0].reshape(HEADS, HEAD_DIM)
        key_gain = qk_gain[1].reshape(HEADS, HEAD_DIM)
        query_norm = (query_raw * lax.rsqrt(lax.optimization_barrier(jnp.mean(query_raw * query_raw, axis=(1, 2))) + 1e-06)[:, None, None] * query_gain).astype(jnp.bfloat16)
        key_norm = (key_raw * lax.rsqrt(lax.optimization_barrier(jnp.mean(key_raw * key_raw, axis=(1, 2))) + 1e-06)[:, None, None] * key_gain).astype(jnp.bfloat16)
        same_seg = row_seg[:, None] == row_seg[None, :]

        def one_head(head):
            q_head = lax.dynamic_index_in_dim(query_norm, head, 1, keepdims=False)
            k_head = lax.dynamic_index_in_dim(key_norm, head, 1, keepdims=False)
            v_head = lax.dynamic_index_in_dim(value_half, head, 1, keepdims=False)
            scores = jnp.dot(q_head, k_head.T, preferred_element_type=jnp.float32) * scale
            scores = jnp.where(same_seg, scores, -1e+30)
            peak_val = lax.optimization_barrier(jnp.max(scores, axis=-1, keepdims=True))
            exp_terms = jnp.exp(scores - peak_val)
            probs = (exp_terms / lax.optimization_barrier(jnp.sum(exp_terms, axis=-1, keepdims=True))).astype(jnp.bfloat16)
            return jnp.dot(probs, v_head, preferred_element_type=jnp.float32).astype(jnp.bfloat16)
        heads_out = lax.map(one_head, jnp.arange(HEADS, dtype=jnp.int32))
        heads_out = jnp.transpose(heads_out, (1, 0, 2)).reshape(row_len, norm_width)
        attn = rounded_sum(jnp.transpose(heads_out.reshape(row_len, N_SEQ, group_width), (1, 0, 2)), out_weight.reshape(N_SEQ, group_width, D))
        hidden = tokens + layer_scale * attn
        merged = jnp.transpose(hidden.reshape(lines, 2, half_grid, 2, D), (0, 2, 1, 3, 4)).reshape(row_len // 4, 4 * D)
        centre = merged - lax.optimization_barrier(jnp.mean(merged, axis=-1, keepdims=True))
        spread = lax.optimization_barrier(jnp.mean(centre * centre, axis=-1, keepdims=True))
        merged_norm = (centre * lax.rsqrt(spread + 1e-05) * ln_weight + ln_bias).astype(jnp.bfloat16)
        pre = rounded_sum(jnp.transpose(merged_norm.reshape(row_len // 4, N_ROWS, slab_width), (1, 0, 2)), fc_weight.reshape(N_ROWS, slab_width, HID)) + fc_bias
        merged_mask = row_mask.reshape(lines, 2, half_grid, 2)[:, 0, :, 0].reshape(row_len // 4).astype(jnp.float32)
        return (jax.nn.gelu(pre, approximate=False) * merged_mask[:, None]).astype(jnp.bfloat16)
    results = lax.map(one_row, (residual_in, segment_ids, pad_mask))
    return jnp.zeros_like(results).at[owner].set(results)
```

```python
import jax
import jax.numpy as jnp
from jax import lax
from jax.sharding import PartitionSpec as P

D = 3200
HEAD_DIM = 128
HEADS = 16
GRID = 32
MASK_SHIFT = 1e6


def attend_dense(query_norm, key_norm, value_half, row_segments, block_len, scale):
    length, heads_here = (query_norm.shape[0], query_norm.shape[1])
    block_count = length // block_len

    def one_block(packed):
        query_block, query_seg = packed
        scores = (
            jnp.einsum("qhd,khd->hqk", query_block, key_norm, preferred_element_type=jnp.float32)
            * scale
        )
        same_seg = (query_seg[:, None] == row_segments[None, :])[None]
        scores = jnp.where(same_seg, scores, -1e30)
        peak_val = jnp.max(scores, axis=-1, keepdims=True)
        exp_terms = jnp.exp(scores - peak_val)
        probs = (exp_terms / jnp.sum(exp_terms, axis=-1, keepdims=True)).astype(jnp.bfloat16)
        return jnp.einsum(
            "hqk,khd->qhd", probs, value_half, preferred_element_type=jnp.float32
        ).astype(jnp.bfloat16)

    blocks_out = lax.map(
        one_block,
        (
            query_norm.reshape(block_count, block_len, heads_here, HEAD_DIM),
            row_segments.reshape(block_count, block_len),
        ),
    )
    return blocks_out.reshape(length, heads_here * HEAD_DIM)


def per_device(
    residual_in,
    norm_gain,
    qkv_weight,
    qk_gain,
    out_weight,
    layer_scale,
    segment_ids,
    pad_mask,
    ln_weight,
    ln_bias,
    fc_weight,
    fc_bias,
    owner,
):
    seq_count = lax.axis_size("seq")
    seq_me = lax.axis_index("seq")
    tokens = residual_in[0].astype(jnp.float32)
    shard_rows = tokens.shape[0]
    normed = (
        tokens * lax.rsqrt(jnp.mean(tokens * tokens, axis=-1, keepdims=True) + 1e-06) * norm_gain
    ).astype(jnp.bfloat16)
    row_tokens = lax.all_gather(normed, "seq", axis=0, tiled=True)
    length = row_tokens.shape[0]
    heads_here = qkv_weight.shape[1] // (3 * HEAD_DIM)
    projected = jnp.dot(row_tokens, qkv_weight, preferred_element_type=jnp.float32).reshape(
        length, heads_here, 3, HEAD_DIM
    )
    query_raw = projected[:, :, 0]
    key_raw = projected[:, :, 1]
    value_half = projected[:, :, 2].astype(jnp.bfloat16)
    seg_spread = lax.dynamic_update_slice_in_dim(
        jnp.zeros((length,), jnp.float32),
        segment_ids[0].astype(jnp.float32),
        seq_me * shard_rows,
        0,
    )
    stats = lax.psum(
        jnp.stack(
            [
                jnp.sum(query_raw * query_raw, axis=(1, 2)),
                jnp.sum(key_raw * key_raw, axis=(1, 2)),
                seg_spread,
            ]
        ),
        "seq",
    )
    query_sq, key_sq, row_segments = stats[0], stats[1], stats[2]
    norm_width = HEADS * HEAD_DIM
    gain_pair = qk_gain.reshape(2, heads_here, HEAD_DIM)
    query_norm = (
        query_raw * lax.rsqrt(query_sq / norm_width + 1e-06)[:, None, None] * gain_pair[0]
    ).astype(jnp.bfloat16)
    key_norm = (
        key_raw * lax.rsqrt(key_sq / norm_width + 1e-06)[:, None, None] * gain_pair[1]
    ).astype(jnp.bfloat16)
    block_len = min(512, length)
    scale = HEAD_DIM ** (-0.5)
    attended = attend_dense(query_norm, key_norm, value_half, row_segments, block_len, scale)
    group_width = attended.shape[1]
    own_heads = lax.all_to_all(
        attended.reshape(seq_count, shard_rows, group_width), "seq", 0, 0
    )
    full_out_weight = lax.all_gather(out_weight, "seq", axis=0, tiled=False)
    group_terms = jnp.einsum(
        "gtc,gcd->gtd", own_heads, full_out_weight, preferred_element_type=jnp.float32
    ).astype(jnp.bfloat16)
    attn = jnp.sum(group_terms.astype(jnp.float32), axis=0)
    hidden = tokens + layer_scale * attn
    half_grid = GRID // 2
    lines = shard_rows // (2 * GRID)
    merged_count = shard_rows // 4
    merged = jnp.transpose(hidden.reshape(lines, 2, half_grid, 2, D), (0, 2, 1, 3, 4)).reshape(
        merged_count, 4 * D
    )
    centre = merged - jnp.mean(merged, axis=-1, keepdims=True)
    spread = jnp.mean(centre * centre, axis=-1, keepdims=True)
    merged_norm = (centre * lax.rsqrt(spread + 1e-05) * ln_weight + ln_bias).astype(jnp.bfloat16)
    merged_mask = (
        pad_mask[0]
        .reshape(lines, 2, half_grid, 2)[:, 0, :, 0]
        .reshape(merged_count)
        .astype(jnp.float32)
    )
    row_count = lax.axis_size("rows")
    row_me = lax.axis_index("rows")
    slabs = lax.all_to_all(merged_norm, "rows", split_axis=1, concat_axis=0, tiled=True)
    owner_hot = (owner[None, :] == jnp.arange(row_count, dtype=jnp.int32)[:, None]).astype(
        jnp.bfloat16
    )
    ordered = jnp.einsum(
        "jp,pms->jms",
        owner_hot,
        slabs.reshape(row_count, merged_count, -1),
        preferred_element_type=jnp.float32,
    ).astype(jnp.bfloat16)
    ordered = ordered.reshape(row_count * merged_count, -1)
    partial = jnp.dot(ordered, fc_weight, preferred_element_type=jnp.float32).reshape(
        row_count, merged_count, -1
    )
    own_slot = (jnp.arange(row_count, dtype=jnp.int32) == owner[row_me]).astype(jnp.float32)
    shift = own_slot[:, None] * ((merged_mask - 1.0) * MASK_SHIFT)[None, :]
    partial = (partial + shift[:, :, None]).astype(jnp.bfloat16)
    summed = lax.psum_scatter(
        partial.reshape(row_count * merged_count, -1),
        "rows",
        scatter_dimension=0,
        tiled=True,
    ).astype(jnp.float32)
    result = jax.nn.gelu(summed + fc_bias, approximate=False)
    return result.astype(jnp.bfloat16)[None]


def solution(mesh):
    return jax.shard_map(
        per_device,
        mesh=mesh,
        in_specs=(
            P("rows", "seq", None),
            P(),
            P(None, "seq"),
            P(None, "seq"),
            P("seq", None),
            P(),
            P("rows", "seq"),
            P("rows", "seq"),
            P(),
            P(),
            P("rows", None),
            P(),
            P(),
        ),
        out_specs=P("rows", "seq", None),
        check_vma=False,
    )
```

```python
import jax
import jax.numpy as jnp
from jax import lax
from jax.experimental import pallas as pl
from jax.experimental.pallas import tpu as pltpu
from jax.sharding import PartitionSpec as P

MESH = pl.DeviceIdType.MESH

D = 3200
HEAD_DIM = 128
HEADS = 16
GRID = 32
MASK_SHIFT = 1e6


def seq_sum_kernel(part_ref, out_ref, slots, send_sem, recv_sem):
    n = slots.shape[0]
    me = lax.axis_index("seq")
    row = lax.axis_index("rows")
    barrier = pltpu.get_barrier_semaphore()
    for k in range(1, n):
        peer = lax.rem(me + k, n)
        pl.semaphore_signal(barrier, inc=1, device_id=(row, peer), device_id_type=MESH)
    pl.semaphore_wait(barrier, n - 1)
    sends = []
    for k in range(1, n):
        peer = lax.rem(me + k, n)
        copy = pltpu.make_async_remote_copy(
            src_ref=part_ref,
            dst_ref=slots.at[me],
            send_sem=send_sem.at[k],
            recv_sem=recv_sem.at[me],
            device_id=(row, peer),
            device_id_type=MESH,
        )
        copy.start()
        sends.append(copy)
    for k in range(1, n):
        src = lax.rem(me + n - k, n)
        pltpu.make_async_remote_copy(
            src_ref=part_ref,
            dst_ref=slots.at[src],
            send_sem=send_sem.at[k],
            recv_sem=recv_sem.at[src],
            device_id=(row, src),
            device_id_type=MESH,
        ).wait_recv()
    for copy in sends:
        copy.wait_send()
    total = jnp.zeros(out_ref.shape, jnp.float32)
    for s in range(n):
        total = total + jnp.where(s == me, part_ref[...], slots[s])
    out_ref[...] = total


def seq_sum(part):
    n = lax.axis_size("seq")
    return pl.pallas_call(
        seq_sum_kernel,
        out_shape=jax.ShapeDtypeStruct(part.shape, jnp.float32),
        in_specs=[pl.BlockSpec(memory_space=pltpu.VMEM)],
        out_specs=pl.BlockSpec(memory_space=pltpu.VMEM),
        scratch_shapes=[
            pltpu.VMEM((n,) + part.shape, jnp.float32),
            pltpu.SemaphoreType.DMA((n,)),
            pltpu.SemaphoreType.DMA((n,)),
        ],
        compiler_params=pltpu.CompilerParams(collective_id=0, has_side_effects=True),
    )(part)


def attend_dense(query_norm, key_norm, value_half, row_segments, block_len, scale):
    length, heads_here = (query_norm.shape[0], query_norm.shape[1])
    block_count = length // block_len

    def one_block(packed):
        query_block, query_seg = packed
        scores = (
            jnp.einsum("qhd,khd->hqk", query_block, key_norm, preferred_element_type=jnp.float32)
            * scale
        )
        same_seg = (query_seg[:, None] == row_segments[None, :])[None]
        scores = jnp.where(same_seg, scores, -1e30)
        peak_val = jnp.max(scores, axis=-1, keepdims=True)
        exp_terms = jnp.exp(scores - peak_val)
        probs = (exp_terms / jnp.sum(exp_terms, axis=-1, keepdims=True)).astype(jnp.bfloat16)
        return jnp.einsum(
            "hqk,khd->qhd", probs, value_half, preferred_element_type=jnp.float32
        ).astype(jnp.bfloat16)

    blocks_out = lax.map(
        one_block,
        (
            query_norm.reshape(block_count, block_len, heads_here, HEAD_DIM),
            row_segments.reshape(block_count, block_len),
        ),
    )
    return blocks_out.reshape(length, heads_here * HEAD_DIM)


def per_device(
    residual_in,
    norm_gain,
    qkv_weight,
    qk_gain,
    out_weight,
    layer_scale,
    segment_ids,
    pad_mask,
    ln_weight,
    ln_bias,
    fc_weight,
    fc_bias,
    owner,
):
    seq_count = lax.axis_size("seq")
    seq_me = lax.axis_index("seq")
    tokens = residual_in[0].astype(jnp.float32)
    shard_rows = tokens.shape[0]
    normed = (
        tokens * lax.rsqrt(jnp.mean(tokens * tokens, axis=-1, keepdims=True) + 1e-06) * norm_gain
    ).astype(jnp.bfloat16)
    row_tokens = lax.all_gather(normed, "seq", axis=0, tiled=True)
    length = row_tokens.shape[0]
    heads_here = qkv_weight.shape[1] // (3 * HEAD_DIM)
    projected = jnp.dot(row_tokens, qkv_weight, preferred_element_type=jnp.float32).reshape(
        length, heads_here, 3, HEAD_DIM
    )
    query_raw = projected[:, :, 0]
    key_raw = projected[:, :, 1]
    value_half = projected[:, :, 2].astype(jnp.bfloat16)
    seg_spread = lax.dynamic_update_slice_in_dim(
        jnp.zeros((length,), jnp.float32),
        segment_ids[0].astype(jnp.float32),
        seq_me * shard_rows,
        0,
    )
    stats = seq_sum(
        jnp.stack(
            [
                jnp.sum(query_raw * query_raw, axis=(1, 2)),
                jnp.sum(key_raw * key_raw, axis=(1, 2)),
                seg_spread,
            ]
        )
    )
    query_sq, key_sq, row_segments = stats[0], stats[1], stats[2]
    norm_width = HEADS * HEAD_DIM
    gain_pair = qk_gain.reshape(2, heads_here, HEAD_DIM)
    query_norm = (
        query_raw * lax.rsqrt(query_sq / norm_width + 1e-06)[:, None, None] * gain_pair[0]
    ).astype(jnp.bfloat16)
    key_norm = (
        key_raw * lax.rsqrt(key_sq / norm_width + 1e-06)[:, None, None] * gain_pair[1]
    ).astype(jnp.bfloat16)
    block_len = min(512, length)
    scale = HEAD_DIM ** (-0.5)
    attended = attend_dense(query_norm, key_norm, value_half, row_segments, block_len, scale)
    group_width = attended.shape[1]
    own_heads = lax.all_to_all(
        attended.reshape(seq_count, shard_rows, group_width), "seq", 0, 0
    )
    full_out_weight = lax.all_gather(out_weight, "seq", axis=0, tiled=False)
    group_terms = jnp.einsum(
        "gtc,gcd->gtd", own_heads, full_out_weight, preferred_element_type=jnp.float32
    ).astype(jnp.bfloat16)
    attn = jnp.sum(group_terms.astype(jnp.float32), axis=0)
    hidden = tokens + layer_scale * attn
    half_grid = GRID // 2
    lines = shard_rows // (2 * GRID)
    merged_count = shard_rows // 4
    merged = jnp.transpose(hidden.reshape(lines, 2, half_grid, 2, D), (0, 2, 1, 3, 4)).reshape(
        merged_count, 4 * D
    )
    centre = merged - jnp.mean(merged, axis=-1, keepdims=True)
    spread = jnp.mean(centre * centre, axis=-1, keepdims=True)
    merged_norm = (centre * lax.rsqrt(spread + 1e-05) * ln_weight + ln_bias).astype(jnp.bfloat16)
    merged_mask = (
        pad_mask[0]
        .reshape(lines, 2, half_grid, 2)[:, 0, :, 0]
        .reshape(merged_count)
        .astype(jnp.float32)
    )
    row_count = lax.axis_size("rows")
    row_me = lax.axis_index("rows")
    slabs = lax.all_to_all(merged_norm, "rows", split_axis=1, concat_axis=0, tiled=True)
    owner_hot = (owner[None, :] == jnp.arange(row_count, dtype=jnp.int32)[:, None]).astype(
        jnp.bfloat16
    )
    ordered = jnp.einsum(
        "jp,pms->jms",
        owner_hot,
        slabs.reshape(row_count, merged_count, -1),
        preferred_element_type=jnp.float32,
    ).astype(jnp.bfloat16)
    ordered = ordered.reshape(row_count * merged_count, -1)
    partial = jnp.dot(ordered, fc_weight, preferred_element_type=jnp.float32).reshape(
        row_count, merged_count, -1
    )
    own_slot = (jnp.arange(row_count, dtype=jnp.int32) == owner[row_me]).astype(jnp.float32)
    shift = own_slot[:, None] * ((merged_mask - 1.0) * MASK_SHIFT)[None, :]
    partial = (partial + shift[:, :, None]).astype(jnp.bfloat16)
    summed = lax.psum_scatter(
        partial.reshape(row_count * merged_count, -1),
        "rows",
        scatter_dimension=0,
        tiled=True,
    ).astype(jnp.float32)
    result = jax.nn.gelu(summed + fc_bias, approximate=False)
    return result.astype(jnp.bfloat16)[None]


def solution(mesh):
    return jax.shard_map(
        per_device,
        mesh=mesh,
        in_specs=(
            P("rows", "seq", None),
            P(),
            P(None, "seq"),
            P(None, "seq"),
            P("seq", None),
            P(),
            P("rows", "seq"),
            P("rows", "seq"),
            P(),
            P(),
            P("rows", None),
            P(),
            P(),
        ),
        out_specs=P("rows", "seq", None),
        check_vma=False,
    )
```

```python
import jax
import jax.numpy as jnp
from jax import lax
from jax.experimental import pallas as pl
from jax.experimental.pallas import tpu as pltpu
from jax.sharding import PartitionSpec as P

MESH = pl.DeviceIdType.MESH

D = 3200
HEAD_DIM = 128
HEADS = 16
GRID = 32
MASK_SHIFT = 1e6


def seq_sum_kernel(part_ref, out_ref, slots, send_sem, recv_sem):
    n = slots.shape[0]
    me = lax.axis_index("seq")
    row = lax.axis_index("rows")
    barrier = pltpu.get_barrier_semaphore()
    for k in range(1, n):
        peer = lax.rem(me + k, n)
        pl.semaphore_signal(barrier, inc=1, device_id=(row, peer), device_id_type=MESH)
    pl.semaphore_wait(barrier, n - 1)
    sends = []
    for k in range(1, n):
        peer = lax.rem(me + k, n)
        copy = pltpu.make_async_remote_copy(
            src_ref=part_ref,
            dst_ref=slots.at[me],
            send_sem=send_sem.at[k],
            recv_sem=recv_sem.at[me],
            device_id=(row, peer),
            device_id_type=MESH,
        )
        copy.start()
        sends.append(copy)
    for k in range(1, n):
        src = lax.rem(me + n - k, n)
        pltpu.make_async_remote_copy(
            src_ref=part_ref,
            dst_ref=slots.at[src],
            send_sem=send_sem.at[k],
            recv_sem=recv_sem.at[src],
            device_id=(row, src),
            device_id_type=MESH,
        ).wait_recv()
    for copy in sends:
        copy.wait_send()
    total = jnp.zeros(out_ref.shape, jnp.float32)
    for s in range(n):
        total = total + jnp.where(s == me, part_ref[...], slots[s])
    out_ref[...] = total


def seq_sum(part):
    n = lax.axis_size("seq")
    return pl.pallas_call(
        seq_sum_kernel,
        out_shape=jax.ShapeDtypeStruct(part.shape, jnp.float32),
        in_specs=[pl.BlockSpec(memory_space=pltpu.VMEM)],
        out_specs=pl.BlockSpec(memory_space=pltpu.VMEM),
        scratch_shapes=[
            pltpu.VMEM((n,) + part.shape, jnp.float32),
            pltpu.SemaphoreType.DMA((n,)),
            pltpu.SemaphoreType.DMA((n,)),
        ],
        compiler_params=pltpu.CompilerParams(collective_id=0, has_side_effects=True),
    )(part)


def attend_dense(query_norm, query_segments, key_norm, value_half, row_segments, block_len, scale):
    length, heads_here = (query_norm.shape[0], query_norm.shape[1])
    block_count = length // block_len

    def one_block(packed):
        query_block, query_seg = packed
        scores = (
            jnp.einsum("qhd,khd->hqk", query_block, key_norm, preferred_element_type=jnp.float32)
            * scale
        )
        same_seg = (query_seg[:, None] == row_segments[None, :])[None]
        scores = jnp.where(same_seg, scores, -1e30)
        peak_val = jnp.max(scores, axis=-1, keepdims=True)
        exp_terms = jnp.exp(scores - peak_val)
        probs = (exp_terms / jnp.sum(exp_terms, axis=-1, keepdims=True)).astype(jnp.bfloat16)
        return jnp.einsum(
            "hqk,khd->qhd", probs, value_half, preferred_element_type=jnp.float32
        ).astype(jnp.bfloat16)

    blocks_out = lax.map(
        one_block,
        (
            query_norm.reshape(block_count, block_len, heads_here, HEAD_DIM),
            query_segments.reshape(block_count, block_len),
        ),
    )
    return blocks_out.reshape(length, heads_here * HEAD_DIM)


def per_device(
    residual_in,
    norm_gain,
    qkv_weight,
    qk_gain,
    out_weight,
    layer_scale,
    segment_ids,
    pad_mask,
    ln_weight,
    ln_bias,
    fc_weight,
    fc_bias,
    owner,
):
    seq_count = lax.axis_size("seq")
    seq_me = lax.axis_index("seq")
    tokens = residual_in[0].astype(jnp.float32)
    shard_rows = tokens.shape[0]
    normed = (
        tokens * lax.rsqrt(jnp.mean(tokens * tokens, axis=-1, keepdims=True) + 1e-06) * norm_gain
    ).astype(jnp.bfloat16)
    row_tokens = lax.all_gather(normed, "seq", axis=0, tiled=True)
    length = row_tokens.shape[0]
    heads_here = qkv_weight.shape[1] // (3 * HEAD_DIM)
    projected = jnp.dot(row_tokens, qkv_weight, preferred_element_type=jnp.float32).reshape(
        length, heads_here, 3, HEAD_DIM
    )
    query_raw = projected[:, :, 0]
    key_raw = projected[:, :, 1]
    value_half = projected[:, :, 2].astype(jnp.bfloat16)
    seg_spread = lax.dynamic_update_slice_in_dim(
        jnp.zeros((length,), jnp.float32),
        segment_ids[0].astype(jnp.float32),
        seq_me * shard_rows,
        0,
    )
    stats = seq_sum(
        jnp.stack(
            [
                jnp.sum(query_raw * query_raw, axis=(1, 2)),
                jnp.sum(key_raw * key_raw, axis=(1, 2)),
                seg_spread,
            ]
        )
    )
    query_sq, key_sq, row_segments = stats[0], stats[1], stats[2]
    norm_width = HEADS * HEAD_DIM
    gain_pair = qk_gain.reshape(2, heads_here, HEAD_DIM)
    query_norm = (
        query_raw * lax.rsqrt(query_sq / norm_width + 1e-06)[:, None, None] * gain_pair[0]
    ).astype(jnp.bfloat16)
    key_norm = (
        key_raw * lax.rsqrt(key_sq / norm_width + 1e-06)[:, None, None] * gain_pair[1]
    ).astype(jnp.bfloat16)
    scale = HEAD_DIM ** (-0.5)
    full_out_weight = lax.all_gather(out_weight, "seq", axis=0, tiled=False)
    row_count = lax.axis_size("rows")
    row_me = lax.axis_index("rows")
    owner_hot = (owner[None, :] == jnp.arange(row_count, dtype=jnp.int32)[:, None]).astype(
        jnp.bfloat16
    )
    own_slot = (jnp.arange(row_count, dtype=jnp.int32) == owner[row_me]).astype(jnp.float32)
    parts = 2
    part_rows = shard_rows // parts
    query_parts = query_norm.reshape(seq_count, parts, part_rows, heads_here, HEAD_DIM)
    seg_parts = row_segments.reshape(seq_count, parts, part_rows)
    token_parts = tokens.reshape(parts, part_rows, D)
    mask_parts = pad_mask[0].reshape(parts, part_rows)
    results = []
    next_queries = query_parts[:, 0]
    for part in range(parts):
        attended = attend_dense(
            next_queries.reshape(seq_count * part_rows, heads_here, HEAD_DIM),
            seg_parts[:, part].reshape(seq_count * part_rows),
            key_norm,
            value_half,
            row_segments,
            part_rows * 4,
            scale,
        )
        group_width = attended.shape[1]
        own_heads = lax.all_to_all(
            attended.reshape(seq_count, part_rows, group_width), "seq", 0, 0
        )
        group_terms = jnp.einsum(
            "gtc,gcd->gtd", own_heads, full_out_weight, preferred_element_type=jnp.float32
        ).astype(jnp.bfloat16)
        attn = jnp.sum(group_terms.astype(jnp.float32), axis=0)
        partial = project_part(
            token_parts[part] + layer_scale * attn,
            mask_parts[part],
            ln_weight,
            ln_bias,
            fc_weight,
            owner_hot,
            own_slot,
        )
        if part + 1 < parts:
            partial, next_queries = lax.optimization_barrier((partial, query_parts[:, part + 1]))
        summed = lax.psum_scatter(partial, "rows", scatter_dimension=0, tiled=True)
        results.append(
            jax.nn.gelu(summed.astype(jnp.float32) + fc_bias, approximate=False).astype(
                jnp.bfloat16
            )
        )
    return jnp.concatenate(results, axis=0)[None]


def project_part(hidden, pad_mask, ln_weight, ln_bias, fc_weight, owner_hot, own_slot):
    row_count = owner_hot.shape[0]
    token_count = hidden.shape[0]
    half_grid = GRID // 2
    lines = token_count // (2 * GRID)
    merged_count = token_count // 4
    merged = jnp.transpose(hidden.reshape(lines, 2, half_grid, 2, D), (0, 2, 1, 3, 4)).reshape(
        merged_count, 4 * D
    )
    centre = merged - jnp.mean(merged, axis=-1, keepdims=True)
    spread = jnp.mean(centre * centre, axis=-1, keepdims=True)
    merged_norm = (centre * lax.rsqrt(spread + 1e-05) * ln_weight + ln_bias).astype(jnp.bfloat16)
    merged_mask = (
        pad_mask.reshape(lines, 2, half_grid, 2)[:, 0, :, 0]
        .reshape(merged_count)
        .astype(jnp.float32)
    )
    slabs = lax.all_to_all(merged_norm, "rows", split_axis=1, concat_axis=0, tiled=True)
    ordered = jnp.einsum(
        "jp,pms->jms",
        owner_hot,
        slabs.reshape(row_count, merged_count, -1),
        preferred_element_type=jnp.float32,
    ).astype(jnp.bfloat16)
    ordered = ordered.reshape(row_count * merged_count, -1)
    partial = jnp.dot(ordered, fc_weight, preferred_element_type=jnp.float32).reshape(
        row_count, merged_count, -1
    )
    shift = own_slot[:, None] * ((merged_mask - 1.0) * MASK_SHIFT)[None, :]
    partial = (partial + shift[:, :, None]).astype(jnp.bfloat16)
    return partial.reshape(row_count * merged_count, -1)


def solution(mesh):
    return jax.shard_map(
        per_device,
        mesh=mesh,
        in_specs=(
            P("rows", "seq", None),
            P(),
            P(None, "seq"),
            P(None, "seq"),
            P("seq", None),
            P(),
            P("rows", "seq"),
            P("rows", "seq"),
            P(),
            P(),
            P("rows", None),
            P(),
            P(),
        ),
        out_specs=P("rows", "seq", None),
        check_vma=False,
    )
```

```python
import jax
import jax.numpy as jnp
from jax import lax
from jax.experimental import pallas as pl
from jax.experimental.pallas import tpu as pltpu
from jax.sharding import PartitionSpec as P

MESH = pl.DeviceIdType.MESH

D = 3200
HEAD_DIM = 128
HEADS = 16
GRID = 32
MASK_SHIFT = 1e6


def seq_sum_kernel(part_ref, out_ref, slots, send_sem, recv_sem):
    n = slots.shape[0]
    me = lax.axis_index("seq")
    row = lax.axis_index("rows")
    barrier = pltpu.get_barrier_semaphore()
    for k in range(1, n):
        peer = lax.rem(me + k, n)
        pl.semaphore_signal(barrier, inc=1, device_id=(row, peer), device_id_type=MESH)
    pl.semaphore_wait(barrier, n - 1)
    sends = []
    for k in range(1, n):
        peer = lax.rem(me + k, n)
        copy = pltpu.make_async_remote_copy(
            src_ref=part_ref,
            dst_ref=slots.at[me],
            send_sem=send_sem.at[k],
            recv_sem=recv_sem.at[me],
            device_id=(row, peer),
            device_id_type=MESH,
        )
        copy.start()
        sends.append(copy)
    for k in range(1, n):
        src = lax.rem(me + n - k, n)
        pltpu.make_async_remote_copy(
            src_ref=part_ref,
            dst_ref=slots.at[src],
            send_sem=send_sem.at[k],
            recv_sem=recv_sem.at[src],
            device_id=(row, src),
            device_id_type=MESH,
        ).wait_recv()
    for copy in sends:
        copy.wait_send()
    total = jnp.zeros(out_ref.shape, jnp.float32)
    for s in range(n):
        total = total + jnp.where(s == me, part_ref[...], slots[s])
    out_ref[...] = total


def seq_sum(part):
    n = lax.axis_size("seq")
    return pl.pallas_call(
        seq_sum_kernel,
        out_shape=jax.ShapeDtypeStruct(part.shape, jnp.float32),
        in_specs=[pl.BlockSpec(memory_space=pltpu.VMEM)],
        out_specs=pl.BlockSpec(memory_space=pltpu.VMEM),
        scratch_shapes=[
            pltpu.VMEM((n,) + part.shape, jnp.float32),
            pltpu.SemaphoreType.DMA((n,)),
            pltpu.SemaphoreType.DMA((n,)),
        ],
        compiler_params=pltpu.CompilerParams(collective_id=0, has_side_effects=True),
    )(part)


def rows_exchange_kernel(slab_ref, out_ref, send_sem, recv_sem):
    n = out_ref.shape[0]
    me = lax.axis_index("rows")
    col = lax.axis_index("seq")
    barrier = pltpu.get_barrier_semaphore()
    for k in range(1, n):
        peer = lax.rem(me + k, n)
        pl.semaphore_signal(barrier, inc=1, device_id=(peer, col), device_id_type=MESH)
    pl.semaphore_wait(barrier, n - 1)
    sends = []
    for k in range(1, n):
        peer = lax.rem(me + k, n)
        copy = pltpu.make_async_remote_copy(
            src_ref=slab_ref.at[peer],
            dst_ref=out_ref.at[me],
            send_sem=send_sem.at[k],
            recv_sem=recv_sem.at[me],
            device_id=(peer, col),
            device_id_type=MESH,
        )
        copy.start()
        sends.append(copy)
    out_ref[me] = slab_ref[me]
    for k in range(1, n):
        src = lax.rem(me + n - k, n)
        pltpu.make_async_remote_copy(
            src_ref=slab_ref.at[src],
            dst_ref=out_ref.at[src],
            send_sem=send_sem.at[k],
            recv_sem=recv_sem.at[src],
            device_id=(src, col),
            device_id_type=MESH,
        ).wait_recv()
    for copy in sends:
        copy.wait_send()


def rows_exchange(slabs):
    n = slabs.shape[0]
    return pl.pallas_call(
        rows_exchange_kernel,
        out_shape=jax.ShapeDtypeStruct(slabs.shape, slabs.dtype),
        in_specs=[pl.BlockSpec(memory_space=pltpu.VMEM)],
        out_specs=pl.BlockSpec(memory_space=pltpu.VMEM),
        scratch_shapes=[pltpu.SemaphoreType.DMA((n,)), pltpu.SemaphoreType.DMA((n,))],
        compiler_params=pltpu.CompilerParams(collective_id=1, has_side_effects=True),
    )(slabs)


def attend_dense(query_norm, key_norm, value_half, row_segments, block_len, scale):
    length, heads_here = (query_norm.shape[0], query_norm.shape[1])
    block_count = length // block_len

    def one_block(packed):
        query_block, query_seg = packed
        scores = (
            jnp.einsum("qhd,khd->hqk", query_block, key_norm, preferred_element_type=jnp.float32)
            * scale
        )
        same_seg = (query_seg[:, None] == row_segments[None, :])[None]
        scores = jnp.where(same_seg, scores, -1e30)
        peak_val = jnp.max(scores, axis=-1, keepdims=True)
        exp_terms = jnp.exp(scores - peak_val)
        probs = (exp_terms / jnp.sum(exp_terms, axis=-1, keepdims=True)).astype(jnp.bfloat16)
        return jnp.einsum(
            "hqk,khd->qhd", probs, value_half, preferred_element_type=jnp.float32
        ).astype(jnp.bfloat16)

    blocks_out = lax.map(
        one_block,
        (
            query_norm.reshape(block_count, block_len, heads_here, HEAD_DIM),
            row_segments.reshape(block_count, block_len),
        ),
    )
    return blocks_out.reshape(length, heads_here * HEAD_DIM)


def per_device(
    residual_in,
    norm_gain,
    qkv_weight,
    qk_gain,
    out_weight,
    layer_scale,
    segment_ids,
    pad_mask,
    ln_weight,
    ln_bias,
    fc_weight,
    fc_bias,
    owner,
):
    seq_count = lax.axis_size("seq")
    seq_me = lax.axis_index("seq")
    tokens = residual_in[0].astype(jnp.float32)
    shard_rows = tokens.shape[0]
    normed = (
        tokens * lax.rsqrt(jnp.mean(tokens * tokens, axis=-1, keepdims=True) + 1e-06) * norm_gain
    ).astype(jnp.bfloat16)
    row_tokens = lax.all_gather(normed, "seq", axis=0, tiled=True)
    length = row_tokens.shape[0]
    heads_here = qkv_weight.shape[1] // (3 * HEAD_DIM)
    projected = jnp.dot(row_tokens, qkv_weight, preferred_element_type=jnp.float32).reshape(
        length, heads_here, 3, HEAD_DIM
    )
    query_raw = projected[:, :, 0]
    key_raw = projected[:, :, 1]
    value_half = projected[:, :, 2].astype(jnp.bfloat16)
    seg_spread = lax.dynamic_update_slice_in_dim(
        jnp.zeros((length,), jnp.float32),
        segment_ids[0].astype(jnp.float32),
        seq_me * shard_rows,
        0,
    )
    stats = seq_sum(
        jnp.stack(
            [
                jnp.sum(query_raw * query_raw, axis=(1, 2)),
                jnp.sum(key_raw * key_raw, axis=(1, 2)),
                seg_spread,
            ]
        )
    )
    query_sq, key_sq, row_segments = stats[0], stats[1], stats[2]
    norm_width = HEADS * HEAD_DIM
    gain_pair = qk_gain.reshape(2, heads_here, HEAD_DIM)
    query_norm = (
        query_raw * lax.rsqrt(query_sq / norm_width + 1e-06)[:, None, None] * gain_pair[0]
    ).astype(jnp.bfloat16)
    key_norm = (
        key_raw * lax.rsqrt(key_sq / norm_width + 1e-06)[:, None, None] * gain_pair[1]
    ).astype(jnp.bfloat16)
    block_len = min(512, length)
    scale = HEAD_DIM ** (-0.5)
    attended = attend_dense(query_norm, key_norm, value_half, row_segments, block_len, scale)
    group_width = attended.shape[1]
    own_heads = lax.all_to_all(
        attended.reshape(seq_count, shard_rows, group_width), "seq", 0, 0
    )
    full_out_weight = lax.all_gather(out_weight, "seq", axis=0, tiled=False)
    group_terms = jnp.einsum(
        "gtc,gcd->gtd", own_heads, full_out_weight, preferred_element_type=jnp.float32
    ).astype(jnp.bfloat16)
    attn = jnp.sum(group_terms.astype(jnp.float32), axis=0)
    hidden = tokens + layer_scale * attn
    half_grid = GRID // 2
    lines = shard_rows // (2 * GRID)
    merged_count = shard_rows // 4
    merged = jnp.transpose(hidden.reshape(lines, 2, half_grid, 2, D), (0, 2, 1, 3, 4)).reshape(
        merged_count, 4 * D
    )
    centre = merged - jnp.mean(merged, axis=-1, keepdims=True)
    spread = jnp.mean(centre * centre, axis=-1, keepdims=True)
    merged_norm = (centre * lax.rsqrt(spread + 1e-05) * ln_weight + ln_bias).astype(jnp.bfloat16)
    row_count = lax.axis_size("rows")
    row_me = lax.axis_index("rows")
    merged_mask = (
        pad_mask[0]
        .reshape(lines, 2, half_grid, 2)[:, 0, :, 0]
        .reshape(merged_count)
        .astype(jnp.float32)
    )
    slabs = rows_exchange(
        jnp.transpose(merged_norm.reshape(merged_count, row_count, -1), (1, 0, 2))
    )
    owner_hot = (owner[None, :] == jnp.arange(row_count, dtype=jnp.int32)[:, None]).astype(
        jnp.bfloat16
    )
    ordered = jnp.einsum(
        "jp,pms->jms",
        owner_hot,
        slabs.reshape(row_count, merged_count, -1),
        preferred_element_type=jnp.float32,
    ).astype(jnp.bfloat16)
    ordered = ordered.reshape(row_count * merged_count, -1)
    partial = jnp.dot(ordered, fc_weight, preferred_element_type=jnp.float32).reshape(
        row_count, merged_count, -1
    )
    own_slot = (jnp.arange(row_count, dtype=jnp.int32) == owner[row_me]).astype(jnp.float32)
    shift = own_slot[:, None] * ((merged_mask - 1.0) * MASK_SHIFT)[None, :]
    partial = (partial + shift[:, :, None]).astype(jnp.bfloat16)
    summed = lax.psum_scatter(
        partial.reshape(row_count * merged_count, -1),
        "rows",
        scatter_dimension=0,
        tiled=True,
    ).astype(jnp.float32)
    result = jax.nn.gelu(summed + fc_bias, approximate=False)
    return result.astype(jnp.bfloat16)[None]


def solution(mesh):
    return jax.shard_map(
        per_device,
        mesh=mesh,
        in_specs=(
            P("rows", "seq", None),
            P(),
            P(None, "seq"),
            P(None, "seq"),
            P("seq", None),
            P(),
            P("rows", "seq"),
            P("rows", "seq"),
            P(),
            P(),
            P("rows", None),
            P(),
            P(),
        ),
        out_specs=P("rows", "seq", None),
        check_vma=False,
    )
```

```python
import functools

import jax
import jax.numpy as jnp
from jax import lax
from jax.experimental import pallas as pl
from jax.experimental.pallas import tpu as pltpu
from jax.sharding import PartitionSpec as P

MESH = pl.DeviceIdType.MESH

D = 3200
HEAD_DIM = 128
HEADS = 16
GRID = 32
MASK_SHIFT = 1e6


def seq_sum_kernel(part_ref, out_ref, slots, send_sem, recv_sem):
    n = slots.shape[0]
    me = lax.axis_index("seq")
    row = lax.axis_index("rows")
    barrier = pltpu.get_barrier_semaphore()
    for k in range(1, n):
        peer = lax.rem(me + k, n)
        pl.semaphore_signal(barrier, inc=1, device_id=(row, peer), device_id_type=MESH)
    pl.semaphore_wait(barrier, n - 1)
    sends = []
    for k in range(1, n):
        peer = lax.rem(me + k, n)
        copy = pltpu.make_async_remote_copy(
            src_ref=part_ref,
            dst_ref=slots.at[me],
            send_sem=send_sem.at[k],
            recv_sem=recv_sem.at[me],
            device_id=(row, peer),
            device_id_type=MESH,
        )
        copy.start()
        sends.append(copy)
    for k in range(1, n):
        src = lax.rem(me + n - k, n)
        pltpu.make_async_remote_copy(
            src_ref=part_ref,
            dst_ref=slots.at[src],
            send_sem=send_sem.at[k],
            recv_sem=recv_sem.at[src],
            device_id=(row, src),
            device_id_type=MESH,
        ).wait_recv()
    for copy in sends:
        copy.wait_send()
    total = jnp.zeros(out_ref.shape, jnp.float32)
    for s in range(n):
        total = total + jnp.where(s == me, part_ref[...], slots[s])
    out_ref[...] = total


def seq_sum(part):
    n = lax.axis_size("seq")
    return pl.pallas_call(
        seq_sum_kernel,
        out_shape=jax.ShapeDtypeStruct(part.shape, jnp.float32),
        in_specs=[pl.BlockSpec(memory_space=pltpu.VMEM)],
        out_specs=pl.BlockSpec(memory_space=pltpu.VMEM),
        scratch_shapes=[
            pltpu.VMEM((n,) + part.shape, jnp.float32),
            pltpu.SemaphoreType.DMA((n,)),
            pltpu.SemaphoreType.DMA((n,)),
        ],
        compiler_params=pltpu.CompilerParams(collective_id=0, has_side_effects=True),
    )(part)


def attention_kernel(scale, q_ref, k_ref, v_ref, qseg_ref, kseg_ref, o_ref):
    scores = (
        lax.dot_general(
            q_ref[...], k_ref[...], (((1,), (1,)), ((), ())), preferred_element_type=jnp.float32
        )
        * scale
    )
    scores = jnp.where(qseg_ref[...] == kseg_ref[...], scores, -1e30)
    peak_val = jnp.max(scores, axis=-1, keepdims=True)
    exp_terms = jnp.exp(scores - peak_val)
    total = jnp.sum(exp_terms, axis=-1, keepdims=True)
    probs = (exp_terms / total).astype(jnp.bfloat16)
    o_ref[...] = jnp.dot(probs, v_ref[...], preferred_element_type=jnp.float32).astype(o_ref.dtype)


def attend_kernel(query_norm, key_norm, value_half, row_segments, block_len, scale):
    length, heads_here = query_norm.shape[0], query_norm.shape[1]
    width = heads_here * HEAD_DIM
    q2, k2, v2 = (a.reshape(length, width) for a in (query_norm, key_norm, value_half))
    flops = 4 * length * length * width
    return pl.pallas_call(
        functools.partial(attention_kernel, scale),
        out_shape=jax.ShapeDtypeStruct((length, width), jnp.bfloat16),
        grid=(heads_here, length // block_len),
        in_specs=[
            pl.BlockSpec((block_len, HEAD_DIM), lambda h, i: (i, h)),
            pl.BlockSpec((length, HEAD_DIM), lambda h, i: (0, h)),
            pl.BlockSpec((length, HEAD_DIM), lambda h, i: (0, h)),
            pl.BlockSpec((block_len, 1), lambda h, i: (i, 0)),
            pl.BlockSpec((1, length), lambda h, i: (0, 0)),
        ],
        out_specs=pl.BlockSpec((block_len, HEAD_DIM), lambda h, i: (i, h)),
        cost_estimate=pl.CostEstimate(
            flops=flops, transcendentals=length * length * heads_here, bytes_accessed=8 * length * width
        ),
    )(q2, k2, v2, row_segments.reshape(length, 1), row_segments.reshape(1, length))


def per_device(
    residual_in,
    norm_gain,
    qkv_weight,
    qk_gain,
    out_weight,
    layer_scale,
    segment_ids,
    pad_mask,
    ln_weight,
    ln_bias,
    fc_weight,
    fc_bias,
    owner,
):
    seq_count = lax.axis_size("seq")
    seq_me = lax.axis_index("seq")
    tokens = residual_in[0].astype(jnp.float32)
    shard_rows = tokens.shape[0]
    normed = (
        tokens * lax.rsqrt(jnp.mean(tokens * tokens, axis=-1, keepdims=True) + 1e-06) * norm_gain
    ).astype(jnp.bfloat16)
    row_tokens = lax.all_gather(normed, "seq", axis=0, tiled=True)
    length = row_tokens.shape[0]
    heads_here = qkv_weight.shape[1] // (3 * HEAD_DIM)
    projected = jnp.dot(row_tokens, qkv_weight, preferred_element_type=jnp.float32).reshape(
        length, heads_here, 3, HEAD_DIM
    )
    query_raw = projected[:, :, 0]
    key_raw = projected[:, :, 1]
    value_half = projected[:, :, 2].astype(jnp.bfloat16)
    seg_spread = lax.dynamic_update_slice_in_dim(
        jnp.zeros((length,), jnp.float32),
        segment_ids[0].astype(jnp.float32),
        seq_me * shard_rows,
        0,
    )
    stats = seq_sum(
        jnp.stack(
            [
                jnp.sum(query_raw * query_raw, axis=(1, 2)),
                jnp.sum(key_raw * key_raw, axis=(1, 2)),
                seg_spread,
            ]
        )
    )
    query_sq, key_sq, row_segments = stats[0], stats[1], stats[2]
    norm_width = HEADS * HEAD_DIM
    gain_pair = qk_gain.reshape(2, heads_here, HEAD_DIM)
    query_norm = (
        query_raw * lax.rsqrt(query_sq / norm_width + 1e-06)[:, None, None] * gain_pair[0]
    ).astype(jnp.bfloat16)
    key_norm = (
        key_raw * lax.rsqrt(key_sq / norm_width + 1e-06)[:, None, None] * gain_pair[1]
    ).astype(jnp.bfloat16)
    scale = HEAD_DIM ** (-0.5)
    attended = attend_kernel(query_norm, key_norm, value_half, row_segments, 256, scale)
    group_width = attended.shape[1]
    own_heads = lax.all_to_all(
        attended.reshape(seq_count, shard_rows, group_width), "seq", 0, 0
    )
    full_out_weight = lax.all_gather(out_weight, "seq", axis=0, tiled=False)
    group_terms = jnp.einsum(
        "gtc,gcd->gtd", own_heads, full_out_weight, preferred_element_type=jnp.float32
    ).astype(jnp.bfloat16)
    attn = jnp.sum(group_terms.astype(jnp.float32), axis=0)
    hidden = tokens + layer_scale * attn
    half_grid = GRID // 2
    lines = shard_rows // (2 * GRID)
    merged_count = shard_rows // 4
    merged = jnp.transpose(hidden.reshape(lines, 2, half_grid, 2, D), (0, 2, 1, 3, 4)).reshape(
        merged_count, 4 * D
    )
    centre = merged - jnp.mean(merged, axis=-1, keepdims=True)
    spread = jnp.mean(centre * centre, axis=-1, keepdims=True)
    merged_norm = (centre * lax.rsqrt(spread + 1e-05) * ln_weight + ln_bias).astype(jnp.bfloat16)
    merged_mask = (
        pad_mask[0]
        .reshape(lines, 2, half_grid, 2)[:, 0, :, 0]
        .reshape(merged_count)
        .astype(jnp.float32)
    )
    row_count = lax.axis_size("rows")
    row_me = lax.axis_index("rows")
    slabs = lax.all_to_all(merged_norm, "rows", split_axis=1, concat_axis=0, tiled=True)
    owner_hot = (owner[None, :] == jnp.arange(row_count, dtype=jnp.int32)[:, None]).astype(
        jnp.bfloat16
    )
    ordered = jnp.einsum(
        "jp,pms->jms",
        owner_hot,
        slabs.reshape(row_count, merged_count, -1),
        preferred_element_type=jnp.float32,
    ).astype(jnp.bfloat16)
    ordered = ordered.reshape(row_count * merged_count, -1)
    partial = jnp.dot(ordered, fc_weight, preferred_element_type=jnp.float32).reshape(
        row_count, merged_count, -1
    )
    own_slot = (jnp.arange(row_count, dtype=jnp.int32) == owner[row_me]).astype(jnp.float32)
    shift = own_slot[:, None] * ((merged_mask - 1.0) * MASK_SHIFT)[None, :]
    partial = (partial + shift[:, :, None]).astype(jnp.bfloat16)
    summed = lax.psum_scatter(
        partial.reshape(row_count * merged_count, -1),
        "rows",
        scatter_dimension=0,
        tiled=True,
    ).astype(jnp.float32)
    result = jax.nn.gelu(summed + fc_bias, approximate=False)
    return result.astype(jnp.bfloat16)[None]


def solution(mesh):
    return jax.shard_map(
        per_device,
        mesh=mesh,
        in_specs=(
            P("rows", "seq", None),
            P(),
            P(None, "seq"),
            P(None, "seq"),
            P("seq", None),
            P(),
            P("rows", "seq"),
            P("rows", "seq"),
            P(),
            P(),
            P("rows", None),
            P(),
            P(),
        ),
        out_specs=P("rows", "seq", None),
        check_vma=False,
    )
```

```python
import functools

import jax
import jax.numpy as jnp
from jax import lax
from jax.experimental import pallas as pl
from jax.experimental.pallas import tpu as pltpu
from jax.sharding import PartitionSpec as P

MESH = pl.DeviceIdType.MESH

D = 3200
HEAD_DIM = 128
HEADS = 16
GRID = 32
MASK_SHIFT = 1e6


def seq_sum_kernel(part_ref, out_ref, slots, send_sem, recv_sem):
    n = slots.shape[0]
    me = lax.axis_index("seq")
    row = lax.axis_index("rows")
    barrier = pltpu.get_barrier_semaphore()
    for k in range(1, n):
        peer = lax.rem(me + k, n)
        pl.semaphore_signal(barrier, inc=1, device_id=(row, peer), device_id_type=MESH)
    pl.semaphore_wait(barrier, n - 1)
    sends = []
    for k in range(1, n):
        peer = lax.rem(me + k, n)
        copy = pltpu.make_async_remote_copy(
            src_ref=part_ref,
            dst_ref=slots.at[me],
            send_sem=send_sem.at[k],
            recv_sem=recv_sem.at[me],
            device_id=(row, peer),
            device_id_type=MESH,
        )
        copy.start()
        sends.append(copy)
    for k in range(1, n):
        src = lax.rem(me + n - k, n)
        pltpu.make_async_remote_copy(
            src_ref=part_ref,
            dst_ref=slots.at[src],
            send_sem=send_sem.at[k],
            recv_sem=recv_sem.at[src],
            device_id=(row, src),
            device_id_type=MESH,
        ).wait_recv()
    for copy in sends:
        copy.wait_send()
    total = jnp.zeros(out_ref.shape, jnp.float32)
    for s in range(n):
        total = total + jnp.where(s == me, part_ref[...], slots[s])
    out_ref[...] = total


def seq_sum(part):
    n = lax.axis_size("seq")
    return pl.pallas_call(
        seq_sum_kernel,
        out_shape=jax.ShapeDtypeStruct(part.shape, jnp.float32),
        in_specs=[pl.BlockSpec(memory_space=pltpu.VMEM)],
        out_specs=pl.BlockSpec(memory_space=pltpu.VMEM),
        scratch_shapes=[
            pltpu.VMEM((n,) + part.shape, jnp.float32),
            pltpu.SemaphoreType.DMA((n,)),
            pltpu.SemaphoreType.DMA((n,)),
        ],
        compiler_params=pltpu.CompilerParams(collective_id=0, has_side_effects=True),
    )(part)


def attention_kernel(scale, q_ref, k_ref, v_ref, qseg_ref, kseg_ref, o_ref):
    scores = (
        lax.dot_general(
            q_ref[...], k_ref[...], (((1,), (1,)), ((), ())), preferred_element_type=jnp.float32
        )
        * scale
    )
    scores = jnp.where(qseg_ref[...] == kseg_ref[...], scores, -1e30)
    peak_val = jnp.max(scores, axis=-1, keepdims=True)
    exp_terms = jnp.exp(scores - peak_val)
    total = jnp.sum(exp_terms, axis=-1, keepdims=True)
    probs = (exp_terms / total).astype(jnp.bfloat16)
    o_ref[...] = jnp.dot(probs, v_ref[...], preferred_element_type=jnp.float32).astype(o_ref.dtype)


def attend_kernel(query_norm, key_norm, value_half, row_segments, block_len, scale):
    length, width = query_norm.shape
    heads_here = width // HEAD_DIM
    q2, k2, v2 = query_norm, key_norm, value_half
    flops = 4 * length * length * width
    return pl.pallas_call(
        functools.partial(attention_kernel, scale),
        out_shape=jax.ShapeDtypeStruct((length, width), jnp.bfloat16),
        grid=(heads_here, length // block_len),
        in_specs=[
            pl.BlockSpec((block_len, HEAD_DIM), lambda h, i: (i, h)),
            pl.BlockSpec((length, HEAD_DIM), lambda h, i: (0, h)),
            pl.BlockSpec((length, HEAD_DIM), lambda h, i: (0, h)),
            pl.BlockSpec((block_len, 1), lambda h, i: (i, 0)),
            pl.BlockSpec((1, length), lambda h, i: (0, 0)),
        ],
        out_specs=pl.BlockSpec((block_len, HEAD_DIM), lambda h, i: (i, h)),
        cost_estimate=pl.CostEstimate(
            flops=flops, transcendentals=length * length * heads_here, bytes_accessed=8 * length * width
        ),
    )(q2, k2, v2, row_segments.reshape(length, 1), row_segments.reshape(1, length))


def per_device(
    residual_in,
    norm_gain,
    qkv_weight,
    qk_gain,
    out_weight,
    layer_scale,
    segment_ids,
    pad_mask,
    ln_weight,
    ln_bias,
    fc_weight,
    fc_bias,
    owner,
):
    seq_count = lax.axis_size("seq")
    seq_me = lax.axis_index("seq")
    tokens = residual_in[0].astype(jnp.float32)
    shard_rows = tokens.shape[0]
    normed = (
        tokens * lax.rsqrt(jnp.mean(tokens * tokens, axis=-1, keepdims=True) + 1e-06) * norm_gain
    ).astype(jnp.bfloat16)
    row_tokens = lax.all_gather(normed, "seq", axis=0, tiled=True)
    length = row_tokens.shape[0]
    heads_here = qkv_weight.shape[1] // (3 * HEAD_DIM)
    weight_parts = qkv_weight.reshape(qkv_weight.shape[0], heads_here, 3, HEAD_DIM)
    query_raw, key_raw, value_raw = (
        jnp.dot(
            row_tokens,
            weight_parts[:, :, c].reshape(qkv_weight.shape[0], heads_here * HEAD_DIM),
            preferred_element_type=jnp.float32,
        )
        for c in range(3)
    )
    value_half = value_raw.astype(jnp.bfloat16)
    seg_spread = lax.dynamic_update_slice_in_dim(
        jnp.zeros((length,), jnp.float32),
        segment_ids[0].astype(jnp.float32),
        seq_me * shard_rows,
        0,
    )
    stats = seq_sum(
        jnp.stack(
            [
                jnp.sum(query_raw * query_raw, axis=1),
                jnp.sum(key_raw * key_raw, axis=1),
                seg_spread,
            ]
        )
    )
    query_sq, key_sq, row_segments = stats[0], stats[1], stats[2]
    norm_width = HEADS * HEAD_DIM
    query_norm = (
        query_raw * lax.rsqrt(query_sq / norm_width + 1e-06)[:, None] * qk_gain[0]
    ).astype(jnp.bfloat16)
    key_norm = (
        key_raw * lax.rsqrt(key_sq / norm_width + 1e-06)[:, None] * qk_gain[1]
    ).astype(jnp.bfloat16)
    scale = HEAD_DIM ** (-0.5)
    attended = attend_kernel(query_norm, key_norm, value_half, row_segments, 256, scale)
    group_width = attended.shape[1]
    own_heads = lax.all_to_all(
        attended.reshape(seq_count, shard_rows, group_width), "seq", 0, 0
    )
    full_out_weight = lax.all_gather(out_weight, "seq", axis=0, tiled=False)
    group_terms = jnp.einsum(
        "gtc,gcd->gtd", own_heads, full_out_weight, preferred_element_type=jnp.float32
    ).astype(jnp.bfloat16)
    attn = jnp.sum(group_terms.astype(jnp.float32), axis=0)
    hidden = tokens + layer_scale * attn
    half_grid = GRID // 2
    lines = shard_rows // (2 * GRID)
    merged_count = shard_rows // 4
    merged = jnp.transpose(hidden.reshape(lines, 2, half_grid, 2, D), (0, 2, 1, 3, 4)).reshape(
        merged_count, 4 * D
    )
    centre = merged - jnp.mean(merged, axis=-1, keepdims=True)
    spread = jnp.mean(centre * centre, axis=-1, keepdims=True)
    merged_norm = (centre * lax.rsqrt(spread + 1e-05) * ln_weight + ln_bias).astype(jnp.bfloat16)
    merged_mask = (
        pad_mask[0]
        .reshape(lines, 2, half_grid, 2)[:, 0, :, 0]
        .reshape(merged_count)
        .astype(jnp.float32)
    )
    row_count = lax.axis_size("rows")
    row_me = lax.axis_index("rows")
    slabs = lax.all_to_all(merged_norm, "rows", split_axis=1, concat_axis=0, tiled=True)
    owner_hot = (owner[None, :] == jnp.arange(row_count, dtype=jnp.int32)[:, None]).astype(
        jnp.bfloat16
    )
    ordered = jnp.einsum(
        "jp,pms->jms",
        owner_hot,
        slabs.reshape(row_count, merged_count, -1),
        preferred_element_type=jnp.float32,
    ).astype(jnp.bfloat16)
    ordered = ordered.reshape(row_count * merged_count, -1)
    partial = jnp.dot(ordered, fc_weight, preferred_element_type=jnp.float32).reshape(
        row_count, merged_count, -1
    )
    own_slot = (jnp.arange(row_count, dtype=jnp.int32) == owner[row_me]).astype(jnp.float32)
    shift = own_slot[:, None] * ((merged_mask - 1.0) * MASK_SHIFT)[None, :]
    partial = (partial + shift[:, :, None]).astype(jnp.bfloat16)
    summed = lax.psum_scatter(
        partial.reshape(row_count * merged_count, -1),
        "rows",
        scatter_dimension=0,
        tiled=True,
    ).astype(jnp.float32)
    result = jax.nn.gelu(summed + fc_bias, approximate=False)
    return result.astype(jnp.bfloat16)[None]


def solution(mesh):
    return jax.shard_map(
        per_device,
        mesh=mesh,
        in_specs=(
            P("rows", "seq", None),
            P(),
            P(None, "seq"),
            P(None, "seq"),
            P("seq", None),
            P(),
            P("rows", "seq"),
            P("rows", "seq"),
            P(),
            P(),
            P("rows", None),
            P(),
            P(),
        ),
        out_specs=P("rows", "seq", None),
        check_vma=False,
    )
```

```python
import functools

import jax
import jax.numpy as jnp
from jax import lax
from jax.experimental import pallas as pl
from jax.experimental.pallas import tpu as pltpu
from jax.sharding import PartitionSpec as P

MESH = pl.DeviceIdType.MESH

D = 3200
HEAD_DIM = 128
HEADS = 16
GRID = 32
MASK_SHIFT = 1e6


def seq_sum_kernel(part_ref, out_ref, slots, send_sem, recv_sem):
    n = slots.shape[0]
    me = lax.axis_index("seq")
    row = lax.axis_index("rows")
    barrier = pltpu.get_barrier_semaphore()
    for k in range(1, n):
        peer = lax.rem(me + k, n)
        pl.semaphore_signal(barrier, inc=1, device_id=(row, peer), device_id_type=MESH)
    pl.semaphore_wait(barrier, n - 1)
    sends = []
    for k in range(1, n):
        peer = lax.rem(me + k, n)
        copy = pltpu.make_async_remote_copy(
            src_ref=part_ref,
            dst_ref=slots.at[me],
            send_sem=send_sem.at[k],
            recv_sem=recv_sem.at[me],
            device_id=(row, peer),
            device_id_type=MESH,
        )
        copy.start()
        sends.append(copy)
    for k in range(1, n):
        src = lax.rem(me + n - k, n)
        pltpu.make_async_remote_copy(
            src_ref=part_ref,
            dst_ref=slots.at[src],
            send_sem=send_sem.at[k],
            recv_sem=recv_sem.at[src],
            device_id=(row, src),
            device_id_type=MESH,
        ).wait_recv()
    for copy in sends:
        copy.wait_send()
    total = jnp.zeros(out_ref.shape, jnp.float32)
    for s in range(n):
        total = total + jnp.where(s == me, part_ref[...], slots[s])
    out_ref[...] = total


def seq_sum(part):
    n = lax.axis_size("seq")
    return pl.pallas_call(
        seq_sum_kernel,
        out_shape=jax.ShapeDtypeStruct(part.shape, jnp.float32),
        in_specs=[pl.BlockSpec(memory_space=pltpu.VMEM)],
        out_specs=pl.BlockSpec(memory_space=pltpu.VMEM),
        scratch_shapes=[
            pltpu.VMEM((n,) + part.shape, jnp.float32),
            pltpu.SemaphoreType.DMA((n,)),
            pltpu.SemaphoreType.DMA((n,)),
        ],
        compiler_params=pltpu.CompilerParams(collective_id=0, has_side_effects=True),
    )(part)


def attention_kernel(scale, q_ref, k_ref, v_ref, qseg_ref, kseg_ref, o_ref):
    scores = (
        lax.dot_general(
            q_ref[...], k_ref[...], (((1,), (1,)), ((), ())), preferred_element_type=jnp.float32
        )
        * scale
    )
    scores = jnp.where(qseg_ref[...] == kseg_ref[...], scores, -1e30)
    peak_val = jnp.max(scores, axis=-1, keepdims=True)
    exp_terms = jnp.exp(scores - peak_val)
    total = jnp.sum(exp_terms, axis=-1, keepdims=True)
    probs = (exp_terms / total).astype(jnp.bfloat16)
    o_ref[...] = jnp.dot(probs, v_ref[...], preferred_element_type=jnp.float32).astype(o_ref.dtype)


def attend_kernel(query_norm, key_norm, value_half, row_segments, block_len, scale):
    length, width = query_norm.shape
    heads_here = width // HEAD_DIM
    q2, k2, v2 = query_norm, key_norm, value_half
    flops = 4 * length * length * width
    return pl.pallas_call(
        functools.partial(attention_kernel, scale),
        out_shape=jax.ShapeDtypeStruct((length, width), jnp.bfloat16),
        grid=(heads_here, length // block_len),
        in_specs=[
            pl.BlockSpec((block_len, HEAD_DIM), lambda h, i: (i, h)),
            pl.BlockSpec((length, HEAD_DIM), lambda h, i: (0, h)),
            pl.BlockSpec((length, HEAD_DIM), lambda h, i: (0, h)),
            pl.BlockSpec((block_len, 1), lambda h, i: (i, 0)),
            pl.BlockSpec((1, length), lambda h, i: (0, 0)),
        ],
        out_specs=pl.BlockSpec((block_len, HEAD_DIM), lambda h, i: (i, h)),
        cost_estimate=pl.CostEstimate(
            flops=flops, transcendentals=length * length * heads_here, bytes_accessed=8 * length * width
        ),
    )(q2, k2, v2, row_segments.reshape(length, 1), row_segments.reshape(1, length))


def per_device(
    residual_in,
    norm_gain,
    qkv_weight,
    qk_gain,
    out_weight,
    layer_scale,
    segment_ids,
    pad_mask,
    ln_weight,
    ln_bias,
    fc_weight,
    fc_bias,
    owner,
):
    seq_count = lax.axis_size("seq")
    seq_me = lax.axis_index("seq")
    tokens = residual_in[0].astype(jnp.float32)
    shard_rows = tokens.shape[0]
    normed = (
        tokens * lax.rsqrt(jnp.mean(tokens * tokens, axis=-1, keepdims=True) + 1e-06) * norm_gain
    ).astype(jnp.bfloat16)
    row_tokens = lax.all_gather(normed, "seq", axis=0, tiled=True)
    length = row_tokens.shape[0]
    heads_here = qkv_weight.shape[1] // (3 * HEAD_DIM)
    weight_parts = qkv_weight.reshape(qkv_weight.shape[0], heads_here, 3, HEAD_DIM)
    query_raw, key_raw, value_raw = (
        jnp.dot(
            row_tokens,
            weight_parts[:, :, c].reshape(qkv_weight.shape[0], heads_here * HEAD_DIM),
            preferred_element_type=jnp.float32,
        )
        for c in range(3)
    )
    value_half = value_raw.astype(jnp.bfloat16)
    seg_spread = lax.dynamic_update_slice_in_dim(
        jnp.zeros((length,), jnp.float32),
        segment_ids[0].astype(jnp.float32),
        seq_me * shard_rows,
        0,
    )
    stats = seq_sum(
        jnp.stack(
            [
                jnp.sum(query_raw * query_raw, axis=1),
                jnp.sum(key_raw * key_raw, axis=1),
                seg_spread,
            ]
        )
    )
    query_sq, key_sq, row_segments = stats[0], stats[1], stats[2]
    norm_width = HEADS * HEAD_DIM
    query_norm = (
        query_raw * lax.rsqrt(query_sq / norm_width + 1e-06)[:, None] * qk_gain[0]
    ).astype(jnp.bfloat16)
    key_norm = (
        key_raw * lax.rsqrt(key_sq / norm_width + 1e-06)[:, None] * qk_gain[1]
    ).astype(jnp.bfloat16)
    scale = HEAD_DIM ** (-0.5)
    attended = attend_kernel(query_norm, key_norm, value_half, row_segments, 256, scale)
    group_width = attended.shape[1]
    own_heads = lax.all_to_all(
        attended.reshape(seq_count, shard_rows, group_width), "seq", 0, 0
    )
    full_out_weight = lax.all_gather(out_weight, "seq", axis=0, tiled=False)
    group_terms = jnp.einsum(
        "gtc,gcd->gtd", own_heads, full_out_weight, preferred_element_type=jnp.float32
    ).astype(jnp.bfloat16)
    attn = jnp.sum(group_terms.astype(jnp.float32), axis=0)
    hidden = tokens + layer_scale * attn
    half_grid = GRID // 2
    lines = shard_rows // (2 * GRID)
    merged_count = shard_rows // 4
    merged = jnp.transpose(hidden.reshape(lines, 2, half_grid, 2, D), (0, 2, 1, 3, 4)).reshape(
        merged_count, 4 * D
    )
    centre = merged - jnp.mean(merged, axis=-1, keepdims=True)
    spread = jnp.mean(centre * centre, axis=-1, keepdims=True)
    merged_norm = (centre * lax.rsqrt(spread + 1e-05) * ln_weight + ln_bias).astype(jnp.bfloat16)
    merged_mask = (
        pad_mask[0]
        .reshape(lines, 2, half_grid, 2)[:, 0, :, 0]
        .reshape(merged_count)
        .astype(jnp.float32)
    )
    row_count = lax.axis_size("rows")
    row_me = lax.axis_index("rows")
    owner_hot = (owner[None, :] == jnp.arange(row_count, dtype=jnp.int32)[:, None]).astype(
        jnp.bfloat16
    )
    halves = 2
    half_count = merged_count // halves
    norm_halves = merged_norm.reshape(halves, half_count, -1)
    own_slot = (jnp.arange(row_count, dtype=jnp.int32) == owner[row_me]).astype(jnp.float32)
    shift = own_slot[:, None] * ((merged_mask - 1.0) * MASK_SHIFT)[None, :]
    shift_halves = shift.reshape(row_count, halves, half_count)
    partial_halves = []
    for half in range(halves):
        slabs = lax.all_to_all(norm_halves[half], "rows", split_axis=1, concat_axis=0, tiled=True)
        ordered = jnp.einsum(
            "jp,pms->jms",
            owner_hot,
            slabs.reshape(row_count, half_count, -1),
            preferred_element_type=jnp.float32,
        ).astype(jnp.bfloat16)
        product = jnp.dot(
            ordered.reshape(row_count * half_count, -1),
            fc_weight,
            preferred_element_type=jnp.float32,
        ).reshape(row_count, half_count, -1)
        partial_halves.append(
            (product + shift_halves[:, half, :, None]).astype(jnp.bfloat16)
        )
    partial = jnp.concatenate(partial_halves, axis=1)
    summed = lax.psum_scatter(
        partial.reshape(row_count * merged_count, -1),
        "rows",
        scatter_dimension=0,
        tiled=True,
    ).astype(jnp.float32)
    result = jax.nn.gelu(summed + fc_bias, approximate=False)
    return result.astype(jnp.bfloat16)[None]


def solution(mesh):
    return jax.shard_map(
        per_device,
        mesh=mesh,
        in_specs=(
            P("rows", "seq", None),
            P(),
            P(None, "seq"),
            P(None, "seq"),
            P("seq", None),
            P(),
            P("rows", "seq"),
            P("rows", "seq"),
            P(),
            P(),
            P("rows", None),
            P(),
            P(),
        ),
        out_specs=P("rows", "seq", None),
        check_vma=False,
    )
```

```python
import functools

import jax
import jax.numpy as jnp
from jax import lax
from jax.experimental import pallas as pl
from jax.experimental.pallas import tpu as pltpu
from jax.sharding import PartitionSpec as P

MESH = pl.DeviceIdType.MESH

D = 3200
HEAD_DIM = 128
HEADS = 16
GRID = 32
MASK_SHIFT = 1e6


def seq_sum_kernel(part_ref, out_ref, slots, send_sem, recv_sem):
    n = slots.shape[0]
    me = lax.axis_index("seq")
    row = lax.axis_index("rows")
    barrier = pltpu.get_barrier_semaphore()
    for k in range(1, n):
        peer = lax.rem(me + k, n)
        pl.semaphore_signal(barrier, inc=1, device_id=(row, peer), device_id_type=MESH)
    pl.semaphore_wait(barrier, n - 1)
    sends = []
    for k in range(1, n):
        peer = lax.rem(me + k, n)
        copy = pltpu.make_async_remote_copy(
            src_ref=part_ref,
            dst_ref=slots.at[me],
            send_sem=send_sem.at[k],
            recv_sem=recv_sem.at[me],
            device_id=(row, peer),
            device_id_type=MESH,
        )
        copy.start()
        sends.append(copy)
    for k in range(1, n):
        src = lax.rem(me + n - k, n)
        pltpu.make_async_remote_copy(
            src_ref=part_ref,
            dst_ref=slots.at[src],
            send_sem=send_sem.at[k],
            recv_sem=recv_sem.at[src],
            device_id=(row, src),
            device_id_type=MESH,
        ).wait_recv()
    for copy in sends:
        copy.wait_send()
    total = jnp.zeros(out_ref.shape, jnp.float32)
    for s in range(n):
        total = total + jnp.where(s == me, part_ref[...], slots[s])
    out_ref[...] = total


def seq_sum(part):
    n = lax.axis_size("seq")
    return pl.pallas_call(
        seq_sum_kernel,
        out_shape=jax.ShapeDtypeStruct(part.shape, jnp.float32),
        in_specs=[pl.BlockSpec(memory_space=pltpu.VMEM)],
        out_specs=pl.BlockSpec(memory_space=pltpu.VMEM),
        scratch_shapes=[
            pltpu.VMEM((n,) + part.shape, jnp.float32),
            pltpu.SemaphoreType.DMA((n,)),
            pltpu.SemaphoreType.DMA((n,)),
        ],
        compiler_params=pltpu.CompilerParams(collective_id=0, has_side_effects=True),
    )(part)


def attention_kernel(scale, q_ref, k_ref, v_ref, qrs_ref, krs_ref, qg_ref, kg_ref, qseg_ref,
                     kseg_ref, o_ref, key_norm):
    @pl.when(pl.program_id(1) == 0)
    def _():
        key_norm[...] = jnp.transpose(
            (k_ref[...] * krs_ref[...] * kg_ref[...]).astype(jnp.bfloat16)
        )

    query_norm = jnp.transpose((q_ref[...] * qrs_ref[...] * qg_ref[...]).astype(jnp.bfloat16))
    scores = (
        lax.dot_general(
            query_norm, key_norm[...], (((1,), (1,)), ((), ())), preferred_element_type=jnp.float32
        )
        * scale
    )
    scores = jnp.where(qseg_ref[...] == kseg_ref[...], scores, -1e30)
    peak_val = jnp.max(scores, axis=-1, keepdims=True)
    exp_terms = jnp.exp(scores - peak_val)
    total = jnp.sum(exp_terms, axis=-1, keepdims=True)
    probs = (exp_terms / total).astype(jnp.bfloat16)
    o_ref[...] = jnp.dot(probs, v_ref[...], preferred_element_type=jnp.float32).astype(o_ref.dtype)


def attend_kernel(query_raw, key_raw, value_half, query_rs, key_rs, qk_gain, row_segments,
                  block_len, scale):
    length, width = query_raw.shape
    heads_here = width // HEAD_DIM
    flops = 4 * length * length * width
    gain_block = pl.BlockSpec((HEAD_DIM, 1), lambda h, i: (h, 0))
    return pl.pallas_call(
        functools.partial(attention_kernel, scale),
        out_shape=jax.ShapeDtypeStruct((length, width), jnp.bfloat16),
        grid=(heads_here, length // block_len),
        in_specs=[
            pl.BlockSpec((HEAD_DIM, block_len), lambda h, i: (h, i)),
            pl.BlockSpec((HEAD_DIM, length), lambda h, i: (h, 0)),
            pl.BlockSpec((length, HEAD_DIM), lambda h, i: (0, h)),
            pl.BlockSpec((1, block_len), lambda h, i: (0, i)),
            pl.BlockSpec((1, length), lambda h, i: (0, 0)),
            gain_block,
            gain_block,
            pl.BlockSpec((block_len, 1), lambda h, i: (i, 0)),
            pl.BlockSpec((1, length), lambda h, i: (0, 0)),
        ],
        out_specs=pl.BlockSpec((block_len, HEAD_DIM), lambda h, i: (i, h)),
        scratch_shapes=[pltpu.VMEM((length, HEAD_DIM), jnp.bfloat16)],
        cost_estimate=pl.CostEstimate(
            flops=flops, transcendentals=length * length * heads_here, bytes_accessed=12 * length * width
        ),
    )(
        query_raw.T,
        key_raw.T,
        value_half,
        query_rs.reshape(1, length),
        key_rs.reshape(1, length),
        qk_gain[0].reshape(width, 1),
        qk_gain[1].reshape(width, 1),
        row_segments.reshape(length, 1),
        row_segments.reshape(1, length),
    )


def per_device(
    residual_in,
    norm_gain,
    qkv_weight,
    qk_gain,
    out_weight,
    layer_scale,
    segment_ids,
    pad_mask,
    ln_weight,
    ln_bias,
    fc_weight,
    fc_bias,
    owner,
):
    seq_count = lax.axis_size("seq")
    seq_me = lax.axis_index("seq")
    tokens = residual_in[0].astype(jnp.float32)
    shard_rows = tokens.shape[0]
    normed = (
        tokens * lax.rsqrt(jnp.mean(tokens * tokens, axis=-1, keepdims=True) + 1e-06) * norm_gain
    ).astype(jnp.bfloat16)
    row_tokens = lax.all_gather(normed, "seq", axis=0, tiled=True)
    length = row_tokens.shape[0]
    heads_here = qkv_weight.shape[1] // (3 * HEAD_DIM)
    weight_parts = qkv_weight.reshape(qkv_weight.shape[0], heads_here, 3, HEAD_DIM)
    query_raw, key_raw, value_raw = (
        jnp.dot(
            row_tokens,
            weight_parts[:, :, c].reshape(qkv_weight.shape[0], heads_here * HEAD_DIM),
            preferred_element_type=jnp.float32,
        )
        for c in range(3)
    )
    value_half = value_raw.astype(jnp.bfloat16)
    seg_spread = lax.dynamic_update_slice_in_dim(
        jnp.zeros((length,), jnp.float32),
        segment_ids[0].astype(jnp.float32),
        seq_me * shard_rows,
        0,
    )
    stats = seq_sum(
        jnp.stack(
            [
                jnp.sum(query_raw * query_raw, axis=1),
                jnp.sum(key_raw * key_raw, axis=1),
                seg_spread,
            ]
        )
    )
    query_sq, key_sq, row_segments = stats[0], stats[1], stats[2]
    norm_width = HEADS * HEAD_DIM
    scale = HEAD_DIM ** (-0.5)
    attended = attend_kernel(
        query_raw,
        key_raw,
        value_half,
        lax.rsqrt(query_sq / norm_width + 1e-06),
        lax.rsqrt(key_sq / norm_width + 1e-06),
        qk_gain,
        row_segments,
        256,
        scale,
    )
    group_width = attended.shape[1]
    own_heads = lax.all_to_all(
        attended.reshape(seq_count, shard_rows, group_width), "seq", 0, 0
    )
    full_out_weight = lax.all_gather(out_weight, "seq", axis=0, tiled=False)
    group_terms = jnp.einsum(
        "gtc,gcd->gtd", own_heads, full_out_weight, preferred_element_type=jnp.float32
    ).astype(jnp.bfloat16)
    attn = jnp.sum(group_terms.astype(jnp.float32), axis=0)
    hidden = tokens + layer_scale * attn
    half_grid = GRID // 2
    lines = shard_rows // (2 * GRID)
    merged_count = shard_rows // 4
    merged = jnp.transpose(hidden.reshape(lines, 2, half_grid, 2, D), (0, 2, 1, 3, 4)).reshape(
        merged_count, 4 * D
    )
    centre = merged - jnp.mean(merged, axis=-1, keepdims=True)
    spread = jnp.mean(centre * centre, axis=-1, keepdims=True)
    merged_norm = (centre * lax.rsqrt(spread + 1e-05) * ln_weight + ln_bias).astype(jnp.bfloat16)
    merged_mask = (
        pad_mask[0]
        .reshape(lines, 2, half_grid, 2)[:, 0, :, 0]
        .reshape(merged_count)
        .astype(jnp.float32)
    )
    row_count = lax.axis_size("rows")
    row_me = lax.axis_index("rows")
    slabs = lax.all_to_all(merged_norm, "rows", split_axis=1, concat_axis=0, tiled=True)
    owner_hot = (owner[None, :] == jnp.arange(row_count, dtype=jnp.int32)[:, None]).astype(
        jnp.bfloat16
    )
    ordered = jnp.einsum(
        "jp,pms->jms",
        owner_hot,
        slabs.reshape(row_count, merged_count, -1),
        preferred_element_type=jnp.float32,
    ).astype(jnp.bfloat16)
    ordered = ordered.reshape(row_count * merged_count, -1)
    partial = jnp.dot(ordered, fc_weight, preferred_element_type=jnp.float32).reshape(
        row_count, merged_count, -1
    )
    own_slot = (jnp.arange(row_count, dtype=jnp.int32) == owner[row_me]).astype(jnp.float32)
    shift = own_slot[:, None] * ((merged_mask - 1.0) * MASK_SHIFT)[None, :]
    partial = (partial + shift[:, :, None]).astype(jnp.bfloat16)
    summed = lax.psum_scatter(
        partial.reshape(row_count * merged_count, -1),
        "rows",
        scatter_dimension=0,
        tiled=True,
    ).astype(jnp.float32)
    result = jax.nn.gelu(summed + fc_bias, approximate=False)
    return result.astype(jnp.bfloat16)[None]


def solution(mesh):
    return jax.shard_map(
        per_device,
        mesh=mesh,
        in_specs=(
            P("rows", "seq", None),
            P(),
            P(None, "seq"),
            P(None, "seq"),
            P("seq", None),
            P(),
            P("rows", "seq"),
            P("rows", "seq"),
            P(),
            P(),
            P("rows", None),
            P(),
            P(),
        ),
        out_specs=P("rows", "seq", None),
        check_vma=False,
    )
```

```python
import functools

import jax
import jax.numpy as jnp
from jax import lax
from jax.experimental import pallas as pl
from jax.experimental.pallas import tpu as pltpu
from jax.sharding import PartitionSpec as P

MESH = pl.DeviceIdType.MESH

D = 3200
HEAD_DIM = 128
HEADS = 16
GRID = 32
MASK_SHIFT = 1e6


def seq_sum_kernel(part_ref, out_ref, slots, send_sem, recv_sem):
    n = slots.shape[0]
    me = lax.axis_index("seq")
    row = lax.axis_index("rows")
    barrier = pltpu.get_barrier_semaphore()
    for k in range(1, n):
        peer = lax.rem(me + k, n)
        pl.semaphore_signal(barrier, inc=1, device_id=(row, peer), device_id_type=MESH)
    pl.semaphore_wait(barrier, n - 1)
    sends = []
    for k in range(1, n):
        peer = lax.rem(me + k, n)
        copy = pltpu.make_async_remote_copy(
            src_ref=part_ref,
            dst_ref=slots.at[me],
            send_sem=send_sem.at[k],
            recv_sem=recv_sem.at[me],
            device_id=(row, peer),
            device_id_type=MESH,
        )
        copy.start()
        sends.append(copy)
    for k in range(1, n):
        src = lax.rem(me + n - k, n)
        pltpu.make_async_remote_copy(
            src_ref=part_ref,
            dst_ref=slots.at[src],
            send_sem=send_sem.at[k],
            recv_sem=recv_sem.at[src],
            device_id=(row, src),
            device_id_type=MESH,
        ).wait_recv()
    for copy in sends:
        copy.wait_send()
    total = jnp.zeros(out_ref.shape, jnp.float32)
    for s in range(n):
        total = total + jnp.where(s == me, part_ref[...], slots[s])
    out_ref[...] = total


def seq_sum(part):
    n = lax.axis_size("seq")
    return pl.pallas_call(
        seq_sum_kernel,
        out_shape=jax.ShapeDtypeStruct(part.shape, jnp.float32),
        in_specs=[pl.BlockSpec(memory_space=pltpu.VMEM)],
        out_specs=pl.BlockSpec(memory_space=pltpu.VMEM),
        scratch_shapes=[
            pltpu.VMEM((n,) + part.shape, jnp.float32),
            pltpu.SemaphoreType.DMA((n,)),
            pltpu.SemaphoreType.DMA((n,)),
        ],
        compiler_params=pltpu.CompilerParams(collective_id=0, has_side_effects=True),
    )(part)


def attention_kernel(scale, q_ref, k_ref, v_ref, qrs_ref, krs_ref, qg_ref, kg_ref, qseg_ref,
                     kseg_ref, o_ref, key_norm, slots, landing, send_sem, recv_sem, local_sem):
    head, block = pl.program_id(0), pl.program_id(1)
    blocks = pl.num_programs(1)
    heads = pl.num_programs(0)
    me = lax.axis_index("seq")
    row = lax.axis_index("rows")

    @pl.when((head == 0) & (block == 0))
    def _():
        barrier = pltpu.get_barrier_semaphore()
        for k in range(1, o_ref.shape[0]):
            peer = lax.rem(me + k, o_ref.shape[0])
            pl.semaphore_signal(barrier, inc=1, device_id=(row, peer), device_id_type=MESH)
        pl.semaphore_wait(barrier, o_ref.shape[0] - 1)

    @pl.when(block == 0)
    def _():
        key_norm[...] = jnp.transpose(
            (k_ref[...] * krs_ref[...] * kg_ref[...]).astype(jnp.bfloat16)
        )

    query_norm = jnp.transpose((q_ref[...] * qrs_ref[...] * qg_ref[...]).astype(jnp.bfloat16))
    scores = (
        lax.dot_general(
            query_norm, key_norm[...], (((1,), (1,)), ((), ())), preferred_element_type=jnp.float32
        )
        * scale
    )
    scores = jnp.where(qseg_ref[...] == kseg_ref[...], scores, -1e30)
    peak_val = jnp.max(scores, axis=-1, keepdims=True)
    exp_terms = jnp.exp(scores - peak_val)
    total = jnp.sum(exp_terms, axis=-1, keepdims=True)
    probs = (exp_terms / total).astype(jnp.bfloat16)
    step = head * blocks + block
    slots[step] = jnp.dot(probs, v_ref[...], preferred_element_type=jnp.float32).astype(
        slots.dtype
    )

    def remote(h, i):
        return pltpu.make_async_remote_copy(
            src_ref=slots.at[h * blocks + i],
            dst_ref=landing.at[me, h],
            send_sem=send_sem.at[h * blocks + i],
            recv_sem=recv_sem.at[me, h],
            device_id=(row, i),
            device_id_type=MESH,
        )

    def local(h):
        return pltpu.make_async_copy(
            slots.at[h * blocks + me], landing.at[me, h], local_sem.at[h]
        )

    @pl.when(block != me)
    def _():
        remote(head, block).start()

    @pl.when(block == me)
    def _():
        local(head).start()

    @pl.when(step == heads * blocks - 1)
    def _():
        for h in range(slots.shape[0] // o_ref.shape[0]):
            local(h).wait()
            for i in range(o_ref.shape[0]):
                @pl.when(i != me)
                def _():
                    remote(h, i).wait_send()
                    pltpu.make_async_remote_copy(
                        src_ref=slots.at[h * blocks + i],
                        dst_ref=landing.at[i, h],
                        send_sem=send_sem.at[h * blocks + i],
                        recv_sem=recv_sem.at[i, h],
                        device_id=(row, i),
                        device_id_type=MESH,
                    ).wait_recv()
        o_ref[...] = landing[...]


def attend_kernel(query_raw, key_raw, value_half, query_rs, key_rs, qk_gain, row_segments,
                  block_len, scale):
    length, width = query_raw.shape
    heads_here = width // HEAD_DIM
    blocks = length // block_len
    flops = 4 * length * length * width
    gain_block = pl.BlockSpec((HEAD_DIM, 1), lambda h, i: (h, 0))
    return pl.pallas_call(
        functools.partial(attention_kernel, scale),
        out_shape=jax.ShapeDtypeStruct((blocks, heads_here, block_len, HEAD_DIM), jnp.bfloat16),
        grid=(heads_here, blocks),
        in_specs=[
            pl.BlockSpec((HEAD_DIM, block_len), lambda h, i: (h, i)),
            pl.BlockSpec((HEAD_DIM, length), lambda h, i: (h, 0)),
            pl.BlockSpec((length, HEAD_DIM), lambda h, i: (0, h)),
            pl.BlockSpec((1, block_len), lambda h, i: (0, i)),
            pl.BlockSpec((1, length), lambda h, i: (0, 0)),
            gain_block,
            gain_block,
            pl.BlockSpec((block_len, 1), lambda h, i: (i, 0)),
            pl.BlockSpec((1, length), lambda h, i: (0, 0)),
        ],
        out_specs=pl.BlockSpec(memory_space=pltpu.VMEM),
        scratch_shapes=[
            pltpu.VMEM((length, HEAD_DIM), jnp.bfloat16),
            pltpu.VMEM((heads_here * blocks, block_len, HEAD_DIM), jnp.bfloat16),
            pltpu.VMEM((blocks, heads_here, block_len, HEAD_DIM), jnp.bfloat16),
            pltpu.SemaphoreType.DMA((heads_here * blocks,)),
            pltpu.SemaphoreType.DMA((blocks, heads_here)),
            pltpu.SemaphoreType.DMA((heads_here,)),
        ],
        compiler_params=pltpu.CompilerParams(collective_id=2, has_side_effects=True),
        cost_estimate=pl.CostEstimate(
            flops=flops, transcendentals=length * length * heads_here, bytes_accessed=12 * length * width
        ),
    )(
        query_raw.T,
        key_raw.T,
        value_half,
        query_rs.reshape(1, length),
        key_rs.reshape(1, length),
        qk_gain[0].reshape(width, 1),
        qk_gain[1].reshape(width, 1),
        row_segments.reshape(length, 1),
        row_segments.reshape(1, length),
    )


def per_device(
    residual_in,
    norm_gain,
    qkv_weight,
    qk_gain,
    out_weight,
    layer_scale,
    segment_ids,
    pad_mask,
    ln_weight,
    ln_bias,
    fc_weight,
    fc_bias,
    owner,
):
    seq_count = lax.axis_size("seq")
    seq_me = lax.axis_index("seq")
    tokens = residual_in[0].astype(jnp.float32)
    shard_rows = tokens.shape[0]
    normed = (
        tokens * lax.rsqrt(jnp.mean(tokens * tokens, axis=-1, keepdims=True) + 1e-06) * norm_gain
    ).astype(jnp.bfloat16)
    row_tokens = lax.all_gather(normed, "seq", axis=0, tiled=True)
    length = row_tokens.shape[0]
    heads_here = qkv_weight.shape[1] // (3 * HEAD_DIM)
    weight_parts = qkv_weight.reshape(qkv_weight.shape[0], heads_here, 3, HEAD_DIM)
    query_raw, key_raw, value_raw = (
        jnp.dot(
            row_tokens,
            weight_parts[:, :, c].reshape(qkv_weight.shape[0], heads_here * HEAD_DIM),
            preferred_element_type=jnp.float32,
        )
        for c in range(3)
    )
    value_half = value_raw.astype(jnp.bfloat16)
    seg_spread = lax.dynamic_update_slice_in_dim(
        jnp.zeros((length,), jnp.float32),
        segment_ids[0].astype(jnp.float32),
        seq_me * shard_rows,
        0,
    )
    stats = seq_sum(
        jnp.stack(
            [
                jnp.sum(query_raw * query_raw, axis=1),
                jnp.sum(key_raw * key_raw, axis=1),
                seg_spread,
            ]
        )
    )
    query_sq, key_sq, row_segments = stats[0], stats[1], stats[2]
    norm_width = HEADS * HEAD_DIM
    scale = HEAD_DIM ** (-0.5)
    attended = attend_kernel(
        query_raw,
        key_raw,
        value_half,
        lax.rsqrt(query_sq / norm_width + 1e-06),
        lax.rsqrt(key_sq / norm_width + 1e-06),
        qk_gain,
        row_segments,
        256,
        scale,
    )
    full_out_weight = lax.all_gather(out_weight, "seq", axis=0, tiled=False)
    group_terms = jnp.einsum(
        "ghtd,ghdo->gto",
        attended,
        full_out_weight.reshape(seq_count, heads_here, HEAD_DIM, -1),
        preferred_element_type=jnp.float32,
    ).astype(jnp.bfloat16)
    attn = jnp.sum(group_terms.astype(jnp.float32), axis=0)
    hidden = tokens + layer_scale * attn
    half_grid = GRID // 2
    lines = shard_rows // (2 * GRID)
    merged_count = shard_rows // 4
    merged = jnp.transpose(hidden.reshape(lines, 2, half_grid, 2, D), (0, 2, 1, 3, 4)).reshape(
        merged_count, 4 * D
    )
    centre = merged - jnp.mean(merged, axis=-1, keepdims=True)
    spread = jnp.mean(centre * centre, axis=-1, keepdims=True)
    merged_norm = (centre * lax.rsqrt(spread + 1e-05) * ln_weight + ln_bias).astype(jnp.bfloat16)
    merged_mask = (
        pad_mask[0]
        .reshape(lines, 2, half_grid, 2)[:, 0, :, 0]
        .reshape(merged_count)
        .astype(jnp.float32)
    )
    row_count = lax.axis_size("rows")
    row_me = lax.axis_index("rows")
    slabs = lax.all_to_all(merged_norm, "rows", split_axis=1, concat_axis=0, tiled=True)
    owner_hot = (owner[None, :] == jnp.arange(row_count, dtype=jnp.int32)[:, None]).astype(
        jnp.bfloat16
    )
    ordered = jnp.einsum(
        "jp,pms->jms",
        owner_hot,
        slabs.reshape(row_count, merged_count, -1),
        preferred_element_type=jnp.float32,
    ).astype(jnp.bfloat16)
    ordered = ordered.reshape(row_count * merged_count, -1)
    partial = jnp.dot(ordered, fc_weight, preferred_element_type=jnp.float32).reshape(
        row_count, merged_count, -1
    )
    own_slot = (jnp.arange(row_count, dtype=jnp.int32) == owner[row_me]).astype(jnp.float32)
    shift = own_slot[:, None] * ((merged_mask - 1.0) * MASK_SHIFT)[None, :]
    partial = (partial + shift[:, :, None]).astype(jnp.bfloat16)
    summed = lax.psum_scatter(
        partial.reshape(row_count * merged_count, -1),
        "rows",
        scatter_dimension=0,
        tiled=True,
    ).astype(jnp.float32)
    result = jax.nn.gelu(summed + fc_bias, approximate=False)
    return result.astype(jnp.bfloat16)[None]


def solution(mesh):
    return jax.shard_map(
        per_device,
        mesh=mesh,
        in_specs=(
            P("rows", "seq", None),
            P(),
            P(None, "seq"),
            P(None, "seq"),
            P("seq", None),
            P(),
            P("rows", "seq"),
            P("rows", "seq"),
            P(),
            P(),
            P("rows", None),
            P(),
            P(),
        ),
        out_specs=P("rows", "seq", None),
        check_vma=False,
    )
```

```python
import functools

import jax
import jax.numpy as jnp
from jax import lax
from jax.experimental import pallas as pl
from jax.experimental.pallas import tpu as pltpu
from jax.sharding import PartitionSpec as P

MESH = pl.DeviceIdType.MESH

D = 3200
HEAD_DIM = 128
HEADS = 16
GRID = 32
MASK_SHIFT = 1e6


def seq_sum_kernel(part_ref, out_ref, slots, send_sem, recv_sem):
    n = slots.shape[0]
    me = lax.axis_index("seq")
    row = lax.axis_index("rows")
    barrier = pltpu.get_barrier_semaphore()
    for k in range(1, n):
        peer = lax.rem(me + k, n)
        pl.semaphore_signal(barrier, inc=1, device_id=(row, peer), device_id_type=MESH)
    pl.semaphore_wait(barrier, n - 1)
    sends = []
    for k in range(1, n):
        peer = lax.rem(me + k, n)
        copy = pltpu.make_async_remote_copy(
            src_ref=part_ref,
            dst_ref=slots.at[me],
            send_sem=send_sem.at[k],
            recv_sem=recv_sem.at[me],
            device_id=(row, peer),
            device_id_type=MESH,
        )
        copy.start()
        sends.append(copy)
    for k in range(1, n):
        src = lax.rem(me + n - k, n)
        pltpu.make_async_remote_copy(
            src_ref=part_ref,
            dst_ref=slots.at[src],
            send_sem=send_sem.at[k],
            recv_sem=recv_sem.at[src],
            device_id=(row, src),
            device_id_type=MESH,
        ).wait_recv()
    for copy in sends:
        copy.wait_send()
    total = jnp.zeros(out_ref.shape, jnp.float32)
    for s in range(n):
        total = total + jnp.where(s == me, part_ref[...], slots[s])
    out_ref[...] = total


def seq_sum(part):
    n = lax.axis_size("seq")
    return pl.pallas_call(
        seq_sum_kernel,
        out_shape=jax.ShapeDtypeStruct(part.shape, jnp.float32),
        in_specs=[pl.BlockSpec(memory_space=pltpu.VMEM)],
        out_specs=pl.BlockSpec(memory_space=pltpu.VMEM),
        scratch_shapes=[
            pltpu.VMEM((n,) + part.shape, jnp.float32),
            pltpu.SemaphoreType.DMA((n,)),
            pltpu.SemaphoreType.DMA((n,)),
        ],
        compiler_params=pltpu.CompilerParams(collective_id=0, has_side_effects=True),
    )(part)


def attention_kernel(scale, q_ref, k_ref, v_ref, qrs_ref, krs_ref, qg_ref, kg_ref, qseg_ref,
                     kseg_ref, o_ref, key_norm, slots, landing, send_sem, recv_sem, local_sem):
    head, block = pl.program_id(0), pl.program_id(1)
    blocks = pl.num_programs(1)
    heads = pl.num_programs(0)
    me = lax.axis_index("seq")
    row = lax.axis_index("rows")

    @pl.when((head == 0) & (block == 0))
    def _():
        barrier = pltpu.get_barrier_semaphore()
        for k in range(1, o_ref.shape[0]):
            peer = lax.rem(me + k, o_ref.shape[0])
            pl.semaphore_signal(barrier, inc=1, device_id=(row, peer), device_id_type=MESH)
        pl.semaphore_wait(barrier, o_ref.shape[0] - 1)

    @pl.when(block == 0)
    def _():
        key_norm[...] = jnp.transpose(
            (k_ref[...] * krs_ref[...] * kg_ref[...]).astype(jnp.bfloat16)
        )

    query_norm = jnp.transpose((q_ref[...] * qrs_ref[...] * qg_ref[...]).astype(jnp.bfloat16))
    scores = (
        lax.dot_general(
            query_norm, key_norm[...], (((1,), (1,)), ((), ())), preferred_element_type=jnp.float32
        )
        * scale
    )
    scores = jnp.where(qseg_ref[...] == kseg_ref[...], scores, -1e30)
    peak_val = jnp.max(scores, axis=-1, keepdims=True)
    exp_terms = jnp.exp(scores - peak_val)
    total = jnp.sum(exp_terms, axis=-1, keepdims=True)
    probs = (exp_terms / total).astype(jnp.bfloat16)
    step = head * blocks + block
    slots[step] = jnp.dot(probs, v_ref[...], preferred_element_type=jnp.float32).astype(
        slots.dtype
    )

    def remote(h, i):
        return pltpu.make_async_remote_copy(
            src_ref=slots.at[h * blocks + i],
            dst_ref=landing.at[me, h],
            send_sem=send_sem.at[h * blocks + i],
            recv_sem=recv_sem.at[me, h],
            device_id=(row, i),
            device_id_type=MESH,
        )

    def local(h):
        return pltpu.make_async_copy(
            slots.at[h * blocks + me], landing.at[me, h], local_sem.at[h]
        )

    @pl.when(block != me)
    def _():
        remote(head, block).start()

    @pl.when(block == me)
    def _():
        local(head).start()

    @pl.when(step == heads * blocks - 1)
    def _():
        for h in range(slots.shape[0] // o_ref.shape[0]):
            local(h).wait()
            for i in range(o_ref.shape[0]):
                @pl.when(i != me)
                def _():
                    remote(h, i).wait_send()
                    pltpu.make_async_remote_copy(
                        src_ref=slots.at[h * blocks + i],
                        dst_ref=landing.at[i, h],
                        send_sem=send_sem.at[h * blocks + i],
                        recv_sem=recv_sem.at[i, h],
                        device_id=(row, i),
                        device_id_type=MESH,
                    ).wait_recv()
        o_ref[...] = landing[...]


def attend_kernel(query_raw, key_raw, value_half, query_rs, key_rs, qk_gain, row_segments,
                  block_len, scale):
    length, width = query_raw.shape
    heads_here = width // HEAD_DIM
    blocks = length // block_len
    flops = 4 * length * length * width
    gain_block = pl.BlockSpec((HEAD_DIM, 1), lambda h, i: (h, 0))
    return pl.pallas_call(
        functools.partial(attention_kernel, scale),
        out_shape=jax.ShapeDtypeStruct((blocks, heads_here, block_len, HEAD_DIM), jnp.bfloat16),
        grid=(heads_here, blocks),
        in_specs=[
            pl.BlockSpec((HEAD_DIM, block_len), lambda h, i: (h, i)),
            pl.BlockSpec((HEAD_DIM, length), lambda h, i: (h, 0)),
            pl.BlockSpec((length, HEAD_DIM), lambda h, i: (0, h)),
            pl.BlockSpec((1, block_len), lambda h, i: (0, i)),
            pl.BlockSpec((1, length), lambda h, i: (0, 0)),
            gain_block,
            gain_block,
            pl.BlockSpec((block_len, 1), lambda h, i: (i, 0)),
            pl.BlockSpec((1, length), lambda h, i: (0, 0)),
        ],
        out_specs=pl.BlockSpec(memory_space=pltpu.VMEM),
        scratch_shapes=[
            pltpu.VMEM((length, HEAD_DIM), jnp.bfloat16),
            pltpu.VMEM((heads_here * blocks, block_len, HEAD_DIM), jnp.bfloat16),
            pltpu.VMEM((blocks, heads_here, block_len, HEAD_DIM), jnp.bfloat16),
            pltpu.SemaphoreType.DMA((heads_here * blocks,)),
            pltpu.SemaphoreType.DMA((blocks, heads_here)),
            pltpu.SemaphoreType.DMA((heads_here,)),
        ],
        compiler_params=pltpu.CompilerParams(collective_id=2, has_side_effects=True),
        cost_estimate=pl.CostEstimate(
            flops=flops, transcendentals=length * length * heads_here, bytes_accessed=12 * length * width
        ),
    )(
        query_raw.T,
        key_raw.T,
        value_half,
        query_rs.reshape(1, length),
        key_rs.reshape(1, length),
        qk_gain[0].reshape(width, 1),
        qk_gain[1].reshape(width, 1),
        row_segments.reshape(length, 1),
        row_segments.reshape(1, length),
    )


def out_proj_kernel(att_ref, w_ref, res_ref, ls_ref, o_ref):
    total = jnp.zeros(o_ref.shape, jnp.float32)
    for g in range(att_ref.shape[0]):
        term = jnp.dot(att_ref[g, 0], w_ref[g, 0], preferred_element_type=jnp.float32)
        term = term + jnp.dot(att_ref[g, 1], w_ref[g, 1], preferred_element_type=jnp.float32)
        total = total + term.astype(jnp.bfloat16).astype(jnp.float32)
    o_ref[...] = res_ref[...].astype(jnp.float32) + ls_ref[...] * total


def out_proj(attended, out_weight_groups, residual, layer_scale, tile=640):
    groups, heads_here, tokens, _ = attended.shape
    width = out_weight_groups.shape[-1]
    return pl.pallas_call(
        out_proj_kernel,
        out_shape=jax.ShapeDtypeStruct((tokens, width), jnp.float32),
        grid=(width // tile,),
        in_specs=[
            pl.BlockSpec(attended.shape, lambda j: (0, 0, 0, 0)),
            pl.BlockSpec((groups, heads_here, HEAD_DIM, tile), lambda j: (0, 0, 0, j)),
            pl.BlockSpec((tokens, tile), lambda j: (0, j)),
            pl.BlockSpec((1, tile), lambda j: (0, j)),
        ],
        out_specs=pl.BlockSpec((tokens, tile), lambda j: (0, j)),
        cost_estimate=pl.CostEstimate(
            flops=2 * tokens * groups * heads_here * HEAD_DIM * width,
            transcendentals=0,
            bytes_accessed=groups * heads_here * HEAD_DIM * width * 2 + tokens * width * 6,
        ),
    )(attended, out_weight_groups, residual, layer_scale.reshape(1, width))


def per_device(
    residual_in,
    norm_gain,
    qkv_weight,
    qk_gain,
    out_weight,
    layer_scale,
    segment_ids,
    pad_mask,
    ln_weight,
    ln_bias,
    fc_weight,
    fc_bias,
    owner,
):
    seq_count = lax.axis_size("seq")
    seq_me = lax.axis_index("seq")
    tokens = residual_in[0].astype(jnp.float32)
    shard_rows = tokens.shape[0]
    normed = (
        tokens * lax.rsqrt(jnp.mean(tokens * tokens, axis=-1, keepdims=True) + 1e-06) * norm_gain
    ).astype(jnp.bfloat16)
    row_tokens = lax.all_gather(normed, "seq", axis=0, tiled=True)
    length = row_tokens.shape[0]
    heads_here = qkv_weight.shape[1] // (3 * HEAD_DIM)
    weight_parts = qkv_weight.reshape(qkv_weight.shape[0], heads_here, 3, HEAD_DIM)
    query_raw, key_raw, value_raw = (
        jnp.dot(
            row_tokens,
            weight_parts[:, :, c].reshape(qkv_weight.shape[0], heads_here * HEAD_DIM),
            preferred_element_type=jnp.float32,
        )
        for c in range(3)
    )
    value_half = value_raw.astype(jnp.bfloat16)
    seg_spread = lax.dynamic_update_slice_in_dim(
        jnp.zeros((length,), jnp.float32),
        segment_ids[0].astype(jnp.float32),
        seq_me * shard_rows,
        0,
    )
    stats = seq_sum(
        jnp.stack(
            [
                jnp.sum(query_raw * query_raw, axis=1),
                jnp.sum(key_raw * key_raw, axis=1),
                seg_spread,
            ]
        )
    )
    query_sq, key_sq, row_segments = stats[0], stats[1], stats[2]
    norm_width = HEADS * HEAD_DIM
    scale = HEAD_DIM ** (-0.5)
    attended = attend_kernel(
        query_raw,
        key_raw,
        value_half,
        lax.rsqrt(query_sq / norm_width + 1e-06),
        lax.rsqrt(key_sq / norm_width + 1e-06),
        qk_gain,
        row_segments,
        256,
        scale,
    )
    full_out_weight = lax.all_gather(out_weight, "seq", axis=0, tiled=False)
    hidden = out_proj(
        attended,
        full_out_weight.reshape(seq_count, heads_here, HEAD_DIM, -1),
        residual_in[0],
        layer_scale,
    )
    half_grid = GRID // 2
    lines = shard_rows // (2 * GRID)
    merged_count = shard_rows // 4
    merged = jnp.transpose(hidden.reshape(lines, 2, half_grid, 2, D), (0, 2, 1, 3, 4)).reshape(
        merged_count, 4 * D
    )
    centre = merged - jnp.mean(merged, axis=-1, keepdims=True)
    spread = jnp.mean(centre * centre, axis=-1, keepdims=True)
    merged_norm = (centre * lax.rsqrt(spread + 1e-05) * ln_weight + ln_bias).astype(jnp.bfloat16)
    merged_mask = (
        pad_mask[0]
        .reshape(lines, 2, half_grid, 2)[:, 0, :, 0]
        .reshape(merged_count)
        .astype(jnp.float32)
    )
    row_count = lax.axis_size("rows")
    row_me = lax.axis_index("rows")
    slabs = lax.all_to_all(merged_norm, "rows", split_axis=1, concat_axis=0, tiled=True)
    owner_hot = (owner[None, :] == jnp.arange(row_count, dtype=jnp.int32)[:, None]).astype(
        jnp.bfloat16
    )
    ordered = jnp.einsum(
        "jp,pms->jms",
        owner_hot,
        slabs.reshape(row_count, merged_count, -1),
        preferred_element_type=jnp.float32,
    ).astype(jnp.bfloat16)
    ordered = ordered.reshape(row_count * merged_count, -1)
    partial = jnp.dot(ordered, fc_weight, preferred_element_type=jnp.float32).reshape(
        row_count, merged_count, -1
    )
    own_slot = (jnp.arange(row_count, dtype=jnp.int32) == owner[row_me]).astype(jnp.float32)
    shift = own_slot[:, None] * ((merged_mask - 1.0) * MASK_SHIFT)[None, :]
    partial = (partial + shift[:, :, None]).astype(jnp.bfloat16)
    summed = lax.psum_scatter(
        partial.reshape(row_count * merged_count, -1),
        "rows",
        scatter_dimension=0,
        tiled=True,
    ).astype(jnp.float32)
    result = jax.nn.gelu(summed + fc_bias, approximate=False)
    return result.astype(jnp.bfloat16)[None]


def solution(mesh):
    return jax.shard_map(
        per_device,
        mesh=mesh,
        in_specs=(
            P("rows", "seq", None),
            P(),
            P(None, "seq"),
            P(None, "seq"),
            P("seq", None),
            P(),
            P("rows", "seq"),
            P("rows", "seq"),
            P(),
            P(),
            P("rows", None),
            P(),
            P(),
        ),
        out_specs=P("rows", "seq", None),
        check_vma=False,
    )
```

```python
import functools

import jax
import jax.numpy as jnp
from jax import lax
from jax.experimental import pallas as pl
from jax.experimental.pallas import tpu as pltpu
from jax.sharding import PartitionSpec as P

MESH = pl.DeviceIdType.MESH

D = 3200
HEAD_DIM = 128
HEADS = 16
GRID = 32
MASK_SHIFT = 1e6


def seq_sum_kernel(part_ref, out_ref, slots, send_sem, recv_sem):
    n = slots.shape[0]
    me = lax.axis_index("seq")
    row = lax.axis_index("rows")
    barrier = pltpu.get_barrier_semaphore()
    for k in range(1, n):
        peer = lax.rem(me + k, n)
        pl.semaphore_signal(barrier, inc=1, device_id=(row, peer), device_id_type=MESH)
    pl.semaphore_wait(barrier, n - 1)
    sends = []
    for k in range(1, n):
        peer = lax.rem(me + k, n)
        copy = pltpu.make_async_remote_copy(
            src_ref=part_ref,
            dst_ref=slots.at[me],
            send_sem=send_sem.at[k],
            recv_sem=recv_sem.at[me],
            device_id=(row, peer),
            device_id_type=MESH,
        )
        copy.start()
        sends.append(copy)
    for k in range(1, n):
        src = lax.rem(me + n - k, n)
        pltpu.make_async_remote_copy(
            src_ref=part_ref,
            dst_ref=slots.at[src],
            send_sem=send_sem.at[k],
            recv_sem=recv_sem.at[src],
            device_id=(row, src),
            device_id_type=MESH,
        ).wait_recv()
    for copy in sends:
        copy.wait_send()
    total = jnp.zeros(out_ref.shape, jnp.float32)
    for s in range(n):
        total = total + jnp.where(s == me, part_ref[...], slots[s])
    out_ref[...] = total


def seq_sum(part):
    n = lax.axis_size("seq")
    return pl.pallas_call(
        seq_sum_kernel,
        out_shape=jax.ShapeDtypeStruct(part.shape, jnp.float32),
        in_specs=[pl.BlockSpec(memory_space=pltpu.VMEM)],
        out_specs=pl.BlockSpec(memory_space=pltpu.VMEM),
        scratch_shapes=[
            pltpu.VMEM((n,) + part.shape, jnp.float32),
            pltpu.SemaphoreType.DMA((n,)),
            pltpu.SemaphoreType.DMA((n,)),
        ],
        compiler_params=pltpu.CompilerParams(collective_id=0, has_side_effects=True),
    )(part)


def attention_kernel(scale, q_ref, k_ref, v_ref, qrs_ref, krs_ref, qg_ref, kg_ref, qseg_ref,
                     kseg_ref, o_ref, key_norm, value_half, slots, landing, send_sem, recv_sem, local_sem):
    head, block = pl.program_id(0), pl.program_id(1)
    blocks = pl.num_programs(1)
    heads = pl.num_programs(0)
    me = lax.axis_index("seq")
    row = lax.axis_index("rows")

    @pl.when((head == 0) & (block == 0))
    def _():
        barrier = pltpu.get_barrier_semaphore()
        for k in range(1, o_ref.shape[0]):
            peer = lax.rem(me + k, o_ref.shape[0])
            pl.semaphore_signal(barrier, inc=1, device_id=(row, peer), device_id_type=MESH)
        pl.semaphore_wait(barrier, o_ref.shape[0] - 1)

    @pl.when(block == 0)
    def _():
        key_norm[...] = jnp.transpose(
            (k_ref[...] * krs_ref[...] * kg_ref[...]).astype(jnp.bfloat16)
        )
        value_half[...] = jnp.transpose(v_ref[...].astype(jnp.bfloat16))

    query_norm = jnp.transpose((q_ref[...] * qrs_ref[...] * qg_ref[...]).astype(jnp.bfloat16))
    scores = (
        lax.dot_general(
            query_norm, key_norm[...], (((1,), (1,)), ((), ())), preferred_element_type=jnp.float32
        )
        * scale
    )
    scores = jnp.where(qseg_ref[...] == kseg_ref[...], scores, -1e30)
    peak_val = jnp.max(scores, axis=-1, keepdims=True)
    exp_terms = jnp.exp(scores - peak_val)
    total = jnp.sum(exp_terms, axis=-1, keepdims=True)
    probs = (exp_terms / total).astype(jnp.bfloat16)
    step = head * blocks + block
    slots[step] = jnp.dot(probs, value_half[...], preferred_element_type=jnp.float32).astype(
        slots.dtype
    )

    def remote(h, i):
        return pltpu.make_async_remote_copy(
            src_ref=slots.at[h * blocks + i],
            dst_ref=landing.at[me, h],
            send_sem=send_sem.at[h * blocks + i],
            recv_sem=recv_sem.at[me, h],
            device_id=(row, i),
            device_id_type=MESH,
        )

    def local(h):
        return pltpu.make_async_copy(
            slots.at[h * blocks + me], landing.at[me, h], local_sem.at[h]
        )

    @pl.when(block != me)
    def _():
        remote(head, block).start()

    @pl.when(block == me)
    def _():
        local(head).start()

    @pl.when(step == heads * blocks - 1)
    def _():
        for h in range(slots.shape[0] // o_ref.shape[0]):
            local(h).wait()
            for i in range(o_ref.shape[0]):
                @pl.when(i != me)
                def _():
                    remote(h, i).wait_send()
                    pltpu.make_async_remote_copy(
                        src_ref=slots.at[h * blocks + i],
                        dst_ref=landing.at[i, h],
                        send_sem=send_sem.at[h * blocks + i],
                        recv_sem=recv_sem.at[i, h],
                        device_id=(row, i),
                        device_id_type=MESH,
                    ).wait_recv()
        o_ref[...] = landing[...]


def attend_kernel(projected_t, query_rs, key_rs, qk_gain, row_segments, block_len, scale):
    length = projected_t.shape[1]
    heads_here = projected_t.shape[0] // (3 * HEAD_DIM)
    width = heads_here * HEAD_DIM
    blocks = length // block_len
    flops = 4 * length * length * width
    gain_block = pl.BlockSpec((HEAD_DIM, 1), lambda h, i: (h, 0))
    return pl.pallas_call(
        functools.partial(attention_kernel, scale),
        out_shape=jax.ShapeDtypeStruct((blocks, heads_here, block_len, HEAD_DIM), jnp.bfloat16),
        grid=(heads_here, blocks),
        in_specs=[
            pl.BlockSpec((HEAD_DIM, block_len), lambda h, i: (3 * h, i)),
            pl.BlockSpec((HEAD_DIM, length), lambda h, i: (3 * h + 1, 0)),
            pl.BlockSpec((HEAD_DIM, length), lambda h, i: (3 * h + 2, 0)),
            pl.BlockSpec((1, block_len), lambda h, i: (0, i)),
            pl.BlockSpec((1, length), lambda h, i: (0, 0)),
            gain_block,
            gain_block,
            pl.BlockSpec((block_len, 1), lambda h, i: (i, 0)),
            pl.BlockSpec((1, length), lambda h, i: (0, 0)),
        ],
        out_specs=pl.BlockSpec(memory_space=pltpu.VMEM),
        scratch_shapes=[
            pltpu.VMEM((length, HEAD_DIM), jnp.bfloat16),
            pltpu.VMEM((length, HEAD_DIM), jnp.bfloat16),
            pltpu.VMEM((heads_here * blocks, block_len, HEAD_DIM), jnp.bfloat16),
            pltpu.VMEM((blocks, heads_here, block_len, HEAD_DIM), jnp.bfloat16),
            pltpu.SemaphoreType.DMA((heads_here * blocks,)),
            pltpu.SemaphoreType.DMA((blocks, heads_here)),
            pltpu.SemaphoreType.DMA((heads_here,)),
        ],
        compiler_params=pltpu.CompilerParams(collective_id=2, has_side_effects=True),
        cost_estimate=pl.CostEstimate(
            flops=flops, transcendentals=length * length * heads_here, bytes_accessed=12 * length * width
        ),
    )(
        projected_t,
        projected_t,
        projected_t,
        query_rs.reshape(1, length),
        key_rs.reshape(1, length),
        qk_gain[0].reshape(width, 1),
        qk_gain[1].reshape(width, 1),
        row_segments.reshape(length, 1),
        row_segments.reshape(1, length),
    )


def out_proj_kernel(att_ref, w_ref, res_ref, ls_ref, o_ref):
    total = jnp.zeros(o_ref.shape, jnp.float32)
    for g in range(att_ref.shape[0]):
        term = jnp.dot(att_ref[g, 0], w_ref[g, 0], preferred_element_type=jnp.float32)
        term = term + jnp.dot(att_ref[g, 1], w_ref[g, 1], preferred_element_type=jnp.float32)
        total = total + term.astype(jnp.bfloat16).astype(jnp.float32)
    o_ref[...] = res_ref[...].astype(jnp.float32) + ls_ref[...] * total


def out_proj(attended, out_weight_groups, residual, layer_scale, tile=640):
    groups, heads_here, tokens, _ = attended.shape
    width = out_weight_groups.shape[-1]
    return pl.pallas_call(
        out_proj_kernel,
        out_shape=jax.ShapeDtypeStruct((tokens, width), jnp.float32),
        grid=(width // tile,),
        in_specs=[
            pl.BlockSpec(attended.shape, lambda j: (0, 0, 0, 0)),
            pl.BlockSpec((groups, heads_here, HEAD_DIM, tile), lambda j: (0, 0, 0, j)),
            pl.BlockSpec((tokens, tile), lambda j: (0, j)),
            pl.BlockSpec((1, tile), lambda j: (0, j)),
        ],
        out_specs=pl.BlockSpec((tokens, tile), lambda j: (0, j)),
        cost_estimate=pl.CostEstimate(
            flops=2 * tokens * groups * heads_here * HEAD_DIM * width,
            transcendentals=0,
            bytes_accessed=groups * heads_here * HEAD_DIM * width * 2 + tokens * width * 6,
        ),
    )(attended, out_weight_groups, residual, layer_scale.reshape(1, width))


def per_device(
    residual_in,
    norm_gain,
    qkv_weight,
    qk_gain,
    out_weight,
    layer_scale,
    segment_ids,
    pad_mask,
    ln_weight,
    ln_bias,
    fc_weight,
    fc_bias,
    owner,
):
    seq_count = lax.axis_size("seq")
    seq_me = lax.axis_index("seq")
    tokens = residual_in[0].astype(jnp.float32)
    shard_rows = tokens.shape[0]
    normed = (
        tokens * lax.rsqrt(jnp.mean(tokens * tokens, axis=-1, keepdims=True) + 1e-06) * norm_gain
    ).astype(jnp.bfloat16)
    row_tokens = lax.all_gather(normed, "seq", axis=0, tiled=True)
    length = row_tokens.shape[0]
    heads_here = qkv_weight.shape[1] // (3 * HEAD_DIM)
    projected_t = jnp.dot(row_tokens, qkv_weight, preferred_element_type=jnp.float32).T
    parts_t = projected_t.reshape(heads_here, 3, HEAD_DIM, length)
    seg_spread = lax.dynamic_update_slice_in_dim(
        jnp.zeros((length,), jnp.float32),
        segment_ids[0].astype(jnp.float32),
        seq_me * shard_rows,
        0,
    )
    stats = seq_sum(
        jnp.stack(
            [
                jnp.sum(parts_t[:, 0] * parts_t[:, 0], axis=(0, 1)),
                jnp.sum(parts_t[:, 1] * parts_t[:, 1], axis=(0, 1)),
                seg_spread,
            ]
        )
    )
    query_sq, key_sq, row_segments = stats[0], stats[1], stats[2]
    norm_width = HEADS * HEAD_DIM
    scale = HEAD_DIM ** (-0.5)
    attended = attend_kernel(
        projected_t,
        lax.rsqrt(query_sq / norm_width + 1e-06),
        lax.rsqrt(key_sq / norm_width + 1e-06),
        qk_gain,
        row_segments,
        256,
        scale,
    )
    full_out_weight = lax.all_gather(out_weight, "seq", axis=0, tiled=False)
    hidden = out_proj(
        attended,
        full_out_weight.reshape(seq_count, heads_here, HEAD_DIM, -1),
        residual_in[0],
        layer_scale,
    )
    half_grid = GRID // 2
    lines = shard_rows // (2 * GRID)
    merged_count = shard_rows // 4
    merged = jnp.transpose(hidden.reshape(lines, 2, half_grid, 2, D), (0, 2, 1, 3, 4)).reshape(
        merged_count, 4 * D
    )
    centre = merged - jnp.mean(merged, axis=-1, keepdims=True)
    spread = jnp.mean(centre * centre, axis=-1, keepdims=True)
    merged_norm = (centre * lax.rsqrt(spread + 1e-05) * ln_weight + ln_bias).astype(jnp.bfloat16)
    merged_mask = (
        pad_mask[0]
        .reshape(lines, 2, half_grid, 2)[:, 0, :, 0]
        .reshape(merged_count)
        .astype(jnp.float32)
    )
    row_count = lax.axis_size("rows")
    row_me = lax.axis_index("rows")
    slabs = lax.all_to_all(merged_norm, "rows", split_axis=1, concat_axis=0, tiled=True)
    owner_hot = (owner[None, :] == jnp.arange(row_count, dtype=jnp.int32)[:, None]).astype(
        jnp.bfloat16
    )
    ordered = jnp.einsum(
        "jp,pms->jms",
        owner_hot,
        slabs.reshape(row_count, merged_count, -1),
        preferred_element_type=jnp.float32,
    ).astype(jnp.bfloat16)
    ordered = ordered.reshape(row_count * merged_count, -1)
    partial = jnp.dot(ordered, fc_weight, preferred_element_type=jnp.float32).reshape(
        row_count, merged_count, -1
    )
    own_slot = (jnp.arange(row_count, dtype=jnp.int32) == owner[row_me]).astype(jnp.float32)
    shift = own_slot[:, None] * ((merged_mask - 1.0) * MASK_SHIFT)[None, :]
    partial = (partial + shift[:, :, None]).astype(jnp.bfloat16)
    summed = lax.psum_scatter(
        partial.reshape(row_count * merged_count, -1),
        "rows",
        scatter_dimension=0,
        tiled=True,
    ).astype(jnp.float32)
    result = jax.nn.gelu(summed + fc_bias, approximate=False)
    return result.astype(jnp.bfloat16)[None]


def solution(mesh):
    return jax.shard_map(
        per_device,
        mesh=mesh,
        in_specs=(
            P("rows", "seq", None),
            P(),
            P(None, "seq"),
            P(None, "seq"),
            P("seq", None),
            P(),
            P("rows", "seq"),
            P("rows", "seq"),
            P(),
            P(),
            P("rows", None),
            P(),
            P(),
        ),
        out_specs=P("rows", "seq", None),
        check_vma=False,
    )
```

```python
import functools

import jax
import jax.numpy as jnp
from jax import lax
from jax.experimental import pallas as pl
from jax.experimental.pallas import tpu as pltpu
from jax.sharding import PartitionSpec as P

MESH = pl.DeviceIdType.MESH

D = 3200
HEAD_DIM = 128
HEADS = 16
GRID = 32
MASK_SHIFT = 1e6


def seq_sum_kernel(part_ref, out_ref, slots, send_sem, recv_sem):
    n = slots.shape[0]
    me = lax.axis_index("seq")
    row = lax.axis_index("rows")
    barrier = pltpu.get_barrier_semaphore()
    for k in range(1, n):
        peer = lax.rem(me + k, n)
        pl.semaphore_signal(barrier, inc=1, device_id=(row, peer), device_id_type=MESH)
    pl.semaphore_wait(barrier, n - 1)
    sends = []
    for k in range(1, n):
        peer = lax.rem(me + k, n)
        copy = pltpu.make_async_remote_copy(
            src_ref=part_ref,
            dst_ref=slots.at[me],
            send_sem=send_sem.at[k],
            recv_sem=recv_sem.at[me],
            device_id=(row, peer),
            device_id_type=MESH,
        )
        copy.start()
        sends.append(copy)
    for k in range(1, n):
        src = lax.rem(me + n - k, n)
        pltpu.make_async_remote_copy(
            src_ref=part_ref,
            dst_ref=slots.at[src],
            send_sem=send_sem.at[k],
            recv_sem=recv_sem.at[src],
            device_id=(row, src),
            device_id_type=MESH,
        ).wait_recv()
    for copy in sends:
        copy.wait_send()
    total = jnp.zeros(out_ref.shape, jnp.float32)
    for s in range(n):
        total = total + jnp.where(s == me, part_ref[...], slots[s])
    out_ref[...] = total


def seq_sum(part):
    n = lax.axis_size("seq")
    return pl.pallas_call(
        seq_sum_kernel,
        out_shape=jax.ShapeDtypeStruct(part.shape, jnp.float32),
        in_specs=[pl.BlockSpec(memory_space=pltpu.VMEM)],
        out_specs=pl.BlockSpec(memory_space=pltpu.VMEM),
        scratch_shapes=[
            pltpu.VMEM((n,) + part.shape, jnp.float32),
            pltpu.SemaphoreType.DMA((n,)),
            pltpu.SemaphoreType.DMA((n,)),
        ],
        compiler_params=pltpu.CompilerParams(collective_id=0, has_side_effects=True),
    )(part)


def attention_kernel(scale, q_ref, k_ref, v_ref, qrs_ref, krs_ref, qg_ref, kg_ref, qseg_ref,
                     kseg_ref, o_ref, key_norm, value_half, slots, landing, send_sem, recv_sem, local_sem):
    head, block = pl.program_id(0), pl.program_id(1)
    blocks = pl.num_programs(1)
    heads = pl.num_programs(0)
    me = lax.axis_index("seq")
    row = lax.axis_index("rows")

    @pl.when((head == 0) & (block == 0))
    def _():
        barrier = pltpu.get_barrier_semaphore()
        for k in range(1, o_ref.shape[0]):
            peer = lax.rem(me + k, o_ref.shape[0])
            pl.semaphore_signal(barrier, inc=1, device_id=(row, peer), device_id_type=MESH)
        pl.semaphore_wait(barrier, o_ref.shape[0] - 1)

    @pl.when(block == 0)
    def _():
        key_norm[...] = jnp.transpose(
            (k_ref[...] * krs_ref[...] * kg_ref[...]).astype(jnp.bfloat16)
        )
        value_half[...] = jnp.transpose(v_ref[...].astype(jnp.bfloat16))

    query_norm = jnp.transpose((q_ref[...] * qrs_ref[...] * qg_ref[...]).astype(jnp.bfloat16))
    scores = (
        lax.dot_general(
            query_norm, key_norm[...], (((1,), (1,)), ((), ())), preferred_element_type=jnp.float32
        )
        * scale
    )
    scores = jnp.where(qseg_ref[...] == kseg_ref[...], scores, -1e30)
    peak_val = jnp.max(scores, axis=-1, keepdims=True)
    exp_terms = jnp.exp(scores - peak_val)
    total = jnp.sum(exp_terms, axis=-1, keepdims=True)
    probs = (exp_terms / total).astype(jnp.bfloat16)
    step = head * blocks + block
    slots[step] = jnp.dot(probs, value_half[...], preferred_element_type=jnp.float32).astype(
        slots.dtype
    )

    def remote(h, i):
        return pltpu.make_async_remote_copy(
            src_ref=slots.at[h * blocks + i],
            dst_ref=landing.at[me, h],
            send_sem=send_sem.at[h * blocks + i],
            recv_sem=recv_sem.at[me, h],
            device_id=(row, i),
            device_id_type=MESH,
        )

    def local(h):
        return pltpu.make_async_copy(
            slots.at[h * blocks + me], landing.at[me, h], local_sem.at[h]
        )

    @pl.when(block != me)
    def _():
        remote(head, block).start()

    @pl.when(block == me)
    def _():
        local(head).start()

    @pl.when(step == heads * blocks - 1)
    def _():
        for h in range(slots.shape[0] // o_ref.shape[0]):
            local(h).wait()
            for i in range(o_ref.shape[0]):
                @pl.when(i != me)
                def _():
                    remote(h, i).wait_send()
                    pltpu.make_async_remote_copy(
                        src_ref=slots.at[h * blocks + i],
                        dst_ref=landing.at[i, h],
                        send_sem=send_sem.at[h * blocks + i],
                        recv_sem=recv_sem.at[i, h],
                        device_id=(row, i),
                        device_id_type=MESH,
                    ).wait_recv()
        o_ref[...] = landing[...]


def attend_kernel(projected_t, query_rs, key_rs, qk_gain, row_segments, block_len, scale):
    length = projected_t.shape[1]
    heads_here = projected_t.shape[0] // (3 * HEAD_DIM)
    width = heads_here * HEAD_DIM
    blocks = length // block_len
    flops = 4 * length * length * width
    gain_block = pl.BlockSpec((HEAD_DIM, 1), lambda h, i: (h, 0))
    return pl.pallas_call(
        functools.partial(attention_kernel, scale),
        out_shape=jax.ShapeDtypeStruct((blocks, heads_here, block_len, HEAD_DIM), jnp.bfloat16),
        grid=(heads_here, blocks),
        in_specs=[
            pl.BlockSpec((HEAD_DIM, block_len), lambda h, i: (3 * h, i)),
            pl.BlockSpec((HEAD_DIM, length), lambda h, i: (3 * h + 1, 0)),
            pl.BlockSpec((HEAD_DIM, length), lambda h, i: (3 * h + 2, 0)),
            pl.BlockSpec((1, block_len), lambda h, i: (0, i)),
            pl.BlockSpec((1, length), lambda h, i: (0, 0)),
            gain_block,
            gain_block,
            pl.BlockSpec((block_len, 1), lambda h, i: (i, 0)),
            pl.BlockSpec((1, length), lambda h, i: (0, 0)),
        ],
        out_specs=pl.BlockSpec(memory_space=pltpu.VMEM),
        scratch_shapes=[
            pltpu.VMEM((length, HEAD_DIM), jnp.bfloat16),
            pltpu.VMEM((length, HEAD_DIM), jnp.bfloat16),
            pltpu.VMEM((heads_here * blocks, block_len, HEAD_DIM), jnp.bfloat16),
            pltpu.VMEM((blocks, heads_here, block_len, HEAD_DIM), jnp.bfloat16),
            pltpu.SemaphoreType.DMA((heads_here * blocks,)),
            pltpu.SemaphoreType.DMA((blocks, heads_here)),
            pltpu.SemaphoreType.DMA((heads_here,)),
        ],
        compiler_params=pltpu.CompilerParams(collective_id=2, has_side_effects=True),
        cost_estimate=pl.CostEstimate(
            flops=flops, transcendentals=length * length * heads_here, bytes_accessed=12 * length * width
        ),
    )(
        projected_t,
        projected_t,
        projected_t,
        query_rs.reshape(1, length),
        key_rs.reshape(1, length),
        qk_gain[0].reshape(width, 1),
        qk_gain[1].reshape(width, 1),
        row_segments.reshape(length, 1),
        row_segments.reshape(1, length),
    )


def out_proj_kernel(att_ref, w_ref, res_ref, ls_ref, o_ref):
    n = att_ref.shape[0]
    me = lax.axis_index("seq")
    total = jnp.zeros(o_ref.shape, jnp.float32)
    for k in range(n):
        g = lax.rem(me + n - k, n)
        term = jnp.dot(att_ref[g, 0], w_ref[k, 0], preferred_element_type=jnp.float32)
        term = term + jnp.dot(att_ref[g, 1], w_ref[k, 1], preferred_element_type=jnp.float32)
        total = total + term.astype(jnp.bfloat16).astype(jnp.float32)
    o_ref[...] = res_ref[...].astype(jnp.float32) + ls_ref[...] * total


def out_proj(attended, out_weight_groups, residual, layer_scale, tile=640):
    groups, heads_here, tokens, _ = attended.shape
    width = out_weight_groups.shape[-1]
    return pl.pallas_call(
        out_proj_kernel,
        out_shape=jax.ShapeDtypeStruct((tokens, width), jnp.float32),
        grid=(width // tile,),
        in_specs=[
            pl.BlockSpec(attended.shape, lambda j: (0, 0, 0, 0)),
            pl.BlockSpec((groups, heads_here, HEAD_DIM, tile), lambda j: (0, 0, 0, j)),
            pl.BlockSpec((tokens, tile), lambda j: (0, j)),
            pl.BlockSpec((1, tile), lambda j: (0, j)),
        ],
        out_specs=pl.BlockSpec((tokens, tile), lambda j: (0, j)),
        cost_estimate=pl.CostEstimate(
            flops=2 * tokens * groups * heads_here * HEAD_DIM * width,
            transcendentals=0,
            bytes_accessed=groups * heads_here * HEAD_DIM * width * 2 + tokens * width * 6,
        ),
    )(attended, out_weight_groups, residual, layer_scale.reshape(1, width))


def per_device(
    residual_in,
    norm_gain,
    qkv_weight,
    qk_gain,
    out_weight,
    layer_scale,
    segment_ids,
    pad_mask,
    ln_weight,
    ln_bias,
    fc_weight,
    fc_bias,
    owner,
):
    seq_count = lax.axis_size("seq")
    seq_me = lax.axis_index("seq")
    tokens = residual_in[0].astype(jnp.float32)
    shard_rows = tokens.shape[0]
    normed = (
        tokens * lax.rsqrt(jnp.mean(tokens * tokens, axis=-1, keepdims=True) + 1e-06) * norm_gain
    ).astype(jnp.bfloat16)
    row_tokens = lax.all_gather(normed, "seq", axis=0, tiled=True)
    length = row_tokens.shape[0]
    heads_here = qkv_weight.shape[1] // (3 * HEAD_DIM)
    projected_t = jnp.dot(row_tokens, qkv_weight, preferred_element_type=jnp.float32).T
    parts_t = projected_t.reshape(heads_here, 3, HEAD_DIM, length)
    seg_spread = lax.dynamic_update_slice_in_dim(
        jnp.zeros((length,), jnp.float32),
        segment_ids[0].astype(jnp.float32),
        seq_me * shard_rows,
        0,
    )
    stats = seq_sum(
        jnp.stack(
            [
                jnp.sum(parts_t[:, 0] * parts_t[:, 0], axis=(0, 1)),
                jnp.sum(parts_t[:, 1] * parts_t[:, 1], axis=(0, 1)),
                seg_spread,
            ]
        )
    )
    query_sq, key_sq, row_segments = stats[0], stats[1], stats[2]
    norm_width = HEADS * HEAD_DIM
    scale = HEAD_DIM ** (-0.5)
    attended = attend_kernel(
        projected_t,
        lax.rsqrt(query_sq / norm_width + 1e-06),
        lax.rsqrt(key_sq / norm_width + 1e-06),
        qk_gain,
        row_segments,
        256,
        scale,
    )
    full_out_weight = jnp.stack(
        [out_weight]
        + [
            lax.ppermute(
                out_weight, "seq", [(src, (src + k) % seq_count) for src in range(seq_count)]
            )
            for k in range(1, seq_count)
        ]
    )
    hidden = out_proj(
        attended,
        full_out_weight.reshape(seq_count, heads_here, HEAD_DIM, -1),
        residual_in[0],
        layer_scale,
    )
    half_grid = GRID // 2
    lines = shard_rows // (2 * GRID)
    merged_count = shard_rows // 4
    merged = jnp.transpose(hidden.reshape(lines, 2, half_grid, 2, D), (0, 2, 1, 3, 4)).reshape(
        merged_count, 4 * D
    )
    centre = merged - jnp.mean(merged, axis=-1, keepdims=True)
    spread = jnp.mean(centre * centre, axis=-1, keepdims=True)
    merged_norm = (centre * lax.rsqrt(spread + 1e-05) * ln_weight + ln_bias).astype(jnp.bfloat16)
    merged_mask = (
        pad_mask[0]
        .reshape(lines, 2, half_grid, 2)[:, 0, :, 0]
        .reshape(merged_count)
        .astype(jnp.float32)
    )
    row_count = lax.axis_size("rows")
    row_me = lax.axis_index("rows")
    slabs = lax.all_to_all(merged_norm, "rows", split_axis=1, concat_axis=0, tiled=True)
    owner_hot = (owner[None, :] == jnp.arange(row_count, dtype=jnp.int32)[:, None]).astype(
        jnp.bfloat16
    )
    ordered = jnp.einsum(
        "jp,pms->jms",
        owner_hot,
        slabs.reshape(row_count, merged_count, -1),
        preferred_element_type=jnp.float32,
    ).astype(jnp.bfloat16)
    ordered = ordered.reshape(row_count * merged_count, -1)
    partial = jnp.dot(ordered, fc_weight, preferred_element_type=jnp.float32).reshape(
        row_count, merged_count, -1
    )
    own_slot = (jnp.arange(row_count, dtype=jnp.int32) == owner[row_me]).astype(jnp.float32)
    shift = own_slot[:, None] * ((merged_mask - 1.0) * MASK_SHIFT)[None, :]
    partial = (partial + shift[:, :, None]).astype(jnp.bfloat16)
    summed = lax.psum_scatter(
        partial.reshape(row_count * merged_count, -1),
        "rows",
        scatter_dimension=0,
        tiled=True,
    ).astype(jnp.float32)
    result = jax.nn.gelu(summed + fc_bias, approximate=False)
    return result.astype(jnp.bfloat16)[None]


def solution(mesh):
    return jax.shard_map(
        per_device,
        mesh=mesh,
        in_specs=(
            P("rows", "seq", None),
            P(),
            P(None, "seq"),
            P(None, "seq"),
            P("seq", None),
            P(),
            P("rows", "seq"),
            P("rows", "seq"),
            P(),
            P(),
            P("rows", None),
            P(),
            P(),
        ),
        out_specs=P("rows", "seq", None),
        check_vma=False,
    )
```

```python
import functools

import jax
import jax.numpy as jnp
from jax import lax
from jax.experimental import pallas as pl
from jax.experimental.pallas import tpu as pltpu
from jax.sharding import PartitionSpec as P

MESH = pl.DeviceIdType.MESH

D = 3200
HEAD_DIM = 128
HEADS = 16
GRID = 32
MASK_SHIFT = 1e6


def seq_sum_kernel(part_ref, out_ref, slots, send_sem, recv_sem):
    n = slots.shape[0]
    me = lax.axis_index("seq")
    row = lax.axis_index("rows")
    barrier = pltpu.get_barrier_semaphore()
    for k in range(1, n):
        peer = lax.rem(me + k, n)
        pl.semaphore_signal(barrier, inc=1, device_id=(row, peer), device_id_type=MESH)
    pl.semaphore_wait(barrier, n - 1)
    sends = []
    for k in range(1, n):
        peer = lax.rem(me + k, n)
        copy = pltpu.make_async_remote_copy(
            src_ref=part_ref,
            dst_ref=slots.at[me],
            send_sem=send_sem.at[k],
            recv_sem=recv_sem.at[me],
            device_id=(row, peer),
            device_id_type=MESH,
        )
        copy.start()
        sends.append(copy)
    for k in range(1, n):
        src = lax.rem(me + n - k, n)
        pltpu.make_async_remote_copy(
            src_ref=part_ref,
            dst_ref=slots.at[src],
            send_sem=send_sem.at[k],
            recv_sem=recv_sem.at[src],
            device_id=(row, src),
            device_id_type=MESH,
        ).wait_recv()
    for copy in sends:
        copy.wait_send()
    total = jnp.zeros(out_ref.shape, jnp.float32)
    for s in range(n):
        total = total + jnp.where(s == me, part_ref[...], slots[s])
    out_ref[...] = total


def seq_sum(part):
    n = lax.axis_size("seq")
    return pl.pallas_call(
        seq_sum_kernel,
        out_shape=jax.ShapeDtypeStruct(part.shape, jnp.float32),
        in_specs=[pl.BlockSpec(memory_space=pltpu.VMEM)],
        out_specs=pl.BlockSpec(memory_space=pltpu.VMEM),
        scratch_shapes=[
            pltpu.VMEM((n,) + part.shape, jnp.float32),
            pltpu.SemaphoreType.DMA((n,)),
            pltpu.SemaphoreType.DMA((n,)),
        ],
        compiler_params=pltpu.CompilerParams(collective_id=0, has_side_effects=True),
    )(part)


def attention_kernel(scale, q_ref, k_ref, v_ref, qrs_ref, krs_ref, qg_ref, kg_ref, qseg_ref,
                     kseg_ref, o_ref, key_norm, value_half, slots, landing, send_sem, recv_sem, local_sem):
    head, block = pl.program_id(0), pl.program_id(1)
    blocks = pl.num_programs(1)
    heads = pl.num_programs(0)
    me = lax.axis_index("seq")
    row = lax.axis_index("rows")

    @pl.when((head == 0) & (block == 0))
    def _():
        barrier = pltpu.get_barrier_semaphore()
        for k in range(1, o_ref.shape[0]):
            peer = lax.rem(me + k, o_ref.shape[0])
            pl.semaphore_signal(barrier, inc=1, device_id=(row, peer), device_id_type=MESH)
        pl.semaphore_wait(barrier, o_ref.shape[0] - 1)

    @pl.when(block == 0)
    def _():
        key_norm[...] = jnp.transpose(
            (k_ref[...] * krs_ref[...] * kg_ref[...]).astype(jnp.bfloat16)
        )
        value_half[...] = jnp.transpose(v_ref[...].astype(jnp.bfloat16))

    query_norm = jnp.transpose((q_ref[...] * qrs_ref[...] * qg_ref[...]).astype(jnp.bfloat16))
    scores = (
        lax.dot_general(
            query_norm, key_norm[...], (((1,), (1,)), ((), ())), preferred_element_type=jnp.float32
        )
        * scale
    )
    scores = jnp.where(qseg_ref[...] == kseg_ref[...], scores, -1e30)
    peak_val = jnp.max(scores, axis=-1, keepdims=True)
    exp_terms = jnp.exp(scores - peak_val)
    total = jnp.sum(exp_terms, axis=-1, keepdims=True)
    probs = (exp_terms / total).astype(jnp.bfloat16)
    step = head * blocks + block
    slots[step] = jnp.dot(probs, value_half[...], preferred_element_type=jnp.float32).astype(
        slots.dtype
    )

    def remote(h, i):
        return pltpu.make_async_remote_copy(
            src_ref=slots.at[h * blocks + i],
            dst_ref=landing.at[me, h],
            send_sem=send_sem.at[h * blocks + i],
            recv_sem=recv_sem.at[me, h],
            device_id=(row, i),
            device_id_type=MESH,
        )

    def local(h):
        return pltpu.make_async_copy(
            slots.at[h * blocks + me], landing.at[me, h], local_sem.at[h]
        )

    @pl.when(block != me)
    def _():
        remote(head, block).start()

    @pl.when(block == me)
    def _():
        local(head).start()

    @pl.when(step == heads * blocks - 1)
    def _():
        for h in range(slots.shape[0] // o_ref.shape[0]):
            local(h).wait()
            for i in range(o_ref.shape[0]):
                @pl.when(i != me)
                def _():
                    remote(h, i).wait_send()
                    pltpu.make_async_remote_copy(
                        src_ref=slots.at[h * blocks + i],
                        dst_ref=landing.at[i, h],
                        send_sem=send_sem.at[h * blocks + i],
                        recv_sem=recv_sem.at[i, h],
                        device_id=(row, i),
                        device_id_type=MESH,
                    ).wait_recv()
        o_ref[...] = landing[...]


def attend_kernel(projected_t, query_rs, key_rs, qk_gain, row_segments, block_len, scale):
    length = projected_t.shape[1]
    heads_here = projected_t.shape[0] // (3 * HEAD_DIM)
    width = heads_here * HEAD_DIM
    blocks = length // block_len
    flops = 4 * length * length * width
    gain_block = pl.BlockSpec((HEAD_DIM, 1), lambda h, i: (h, 0))
    return pl.pallas_call(
        functools.partial(attention_kernel, scale),
        out_shape=jax.ShapeDtypeStruct((blocks, heads_here, block_len, HEAD_DIM), jnp.bfloat16),
        grid=(heads_here, blocks),
        in_specs=[
            pl.BlockSpec((HEAD_DIM, block_len), lambda h, i: (3 * h, i)),
            pl.BlockSpec((HEAD_DIM, length), lambda h, i: (3 * h + 1, 0)),
            pl.BlockSpec((HEAD_DIM, length), lambda h, i: (3 * h + 2, 0)),
            pl.BlockSpec((1, block_len), lambda h, i: (0, i)),
            pl.BlockSpec((1, length), lambda h, i: (0, 0)),
            gain_block,
            gain_block,
            pl.BlockSpec((block_len, 1), lambda h, i: (i, 0)),
            pl.BlockSpec((1, length), lambda h, i: (0, 0)),
        ],
        out_specs=pl.BlockSpec(memory_space=pltpu.VMEM),
        scratch_shapes=[
            pltpu.VMEM((length, HEAD_DIM), jnp.bfloat16),
            pltpu.VMEM((length, HEAD_DIM), jnp.bfloat16),
            pltpu.VMEM((heads_here * blocks, block_len, HEAD_DIM), jnp.bfloat16),
            pltpu.VMEM((blocks, heads_here, block_len, HEAD_DIM), jnp.bfloat16),
            pltpu.SemaphoreType.DMA((heads_here * blocks,)),
            pltpu.SemaphoreType.DMA((blocks, heads_here)),
            pltpu.SemaphoreType.DMA((heads_here,)),
        ],
        compiler_params=pltpu.CompilerParams(collective_id=2, has_side_effects=True),
        cost_estimate=pl.CostEstimate(
            flops=flops, transcendentals=length * length * heads_here, bytes_accessed=12 * length * width
        ),
    )(
        projected_t,
        projected_t,
        projected_t,
        query_rs.reshape(1, length),
        key_rs.reshape(1, length),
        qk_gain[0].reshape(width, 1),
        qk_gain[1].reshape(width, 1),
        row_segments.reshape(length, 1),
        row_segments.reshape(1, length),
    )


def out_proj_kernel(att_ref, w_ref, res_ref, ls_ref, o_ref):
    total = jnp.zeros(o_ref.shape, jnp.float32)
    for g in range(att_ref.shape[0]):
        term = jnp.dot(att_ref[g, 0], w_ref[g, 0], preferred_element_type=jnp.float32)
        term = term + jnp.dot(att_ref[g, 1], w_ref[g, 1], preferred_element_type=jnp.float32)
        total = total + term.astype(jnp.bfloat16).astype(jnp.float32)
    o_ref[...] = res_ref[...].astype(jnp.float32) + ls_ref[...] * total


def out_proj(attended, out_weight_groups, residual, layer_scale, tile=640):
    groups, heads_here, tokens, _ = attended.shape
    width = out_weight_groups.shape[-1]
    return pl.pallas_call(
        out_proj_kernel,
        out_shape=jax.ShapeDtypeStruct((tokens, width), jnp.float32),
        grid=(width // tile,),
        in_specs=[
            pl.BlockSpec(attended.shape, lambda j: (0, 0, 0, 0)),
            pl.BlockSpec((groups, heads_here, HEAD_DIM, tile), lambda j: (0, 0, 0, j)),
            pl.BlockSpec((tokens, tile), lambda j: (0, j)),
            pl.BlockSpec((1, tile), lambda j: (0, j)),
        ],
        out_specs=pl.BlockSpec((tokens, tile), lambda j: (0, j)),
        cost_estimate=pl.CostEstimate(
            flops=2 * tokens * groups * heads_here * HEAD_DIM * width,
            transcendentals=0,
            bytes_accessed=groups * heads_here * HEAD_DIM * width * 2 + tokens * width * 6,
        ),
    )(attended, out_weight_groups, residual, layer_scale.reshape(1, width))


def per_device(
    residual_in,
    norm_gain,
    qkv_weight,
    qk_gain,
    out_weight,
    layer_scale,
    segment_ids,
    pad_mask,
    ln_weight,
    ln_bias,
    fc_weight,
    fc_bias,
    owner,
):
    seq_count = lax.axis_size("seq")
    seq_me = lax.axis_index("seq")
    tokens = residual_in[0].astype(jnp.float32)
    shard_rows = tokens.shape[0]
    normed = (
        tokens * lax.rsqrt(jnp.mean(tokens * tokens, axis=-1, keepdims=True) + 1e-06) * norm_gain
    ).astype(jnp.bfloat16)
    row_tokens = lax.all_gather(normed, "seq", axis=0, tiled=True)
    length = row_tokens.shape[0]
    heads_here = qkv_weight.shape[1] // (3 * HEAD_DIM)
    projected_t = jnp.dot(row_tokens, qkv_weight, preferred_element_type=jnp.float32).T
    parts_t = projected_t.reshape(heads_here, 3, HEAD_DIM, length)
    seg_spread = lax.dynamic_update_slice_in_dim(
        jnp.zeros((length,), jnp.float32),
        segment_ids[0].astype(jnp.float32),
        seq_me * shard_rows,
        0,
    )
    stats = seq_sum(
        jnp.stack(
            [
                jnp.sum(parts_t[:, 0] * parts_t[:, 0], axis=(0, 1)),
                jnp.sum(parts_t[:, 1] * parts_t[:, 1], axis=(0, 1)),
                seg_spread,
            ]
        )
    )
    query_sq, key_sq, row_segments = stats[0], stats[1], stats[2]
    norm_width = HEADS * HEAD_DIM
    scale = HEAD_DIM ** (-0.5)
    attended = attend_kernel(
        projected_t,
        lax.rsqrt(query_sq / norm_width + 1e-06),
        lax.rsqrt(key_sq / norm_width + 1e-06),
        qk_gain,
        row_segments,
        256,
        scale,
    )
    full_out_weight = lax.all_gather(out_weight, "seq", axis=0, tiled=False)
    half_grid = GRID // 2
    lines = shard_rows // (2 * GRID)
    merged_count = shard_rows // 4

    def shuffle_rows(x, axis):
        shape = x.shape
        split = shape[:axis] + (lines, 2, half_grid, 2) + shape[axis + 1:]
        order = list(range(axis)) + [axis, axis + 2, axis + 1, axis + 3] + list(
            range(axis + 4, len(split))
        )
        return jnp.transpose(x.reshape(split), order).reshape(shape)

    hidden = out_proj(
        shuffle_rows(attended, 2),
        full_out_weight.reshape(seq_count, heads_here, HEAD_DIM, -1),
        shuffle_rows(residual_in[0], 0),
        layer_scale,
    )
    merged = hidden.reshape(merged_count, 4 * D)
    centre = merged - jnp.mean(merged, axis=-1, keepdims=True)
    spread = jnp.mean(centre * centre, axis=-1, keepdims=True)
    merged_norm = (centre * lax.rsqrt(spread + 1e-05) * ln_weight + ln_bias).astype(jnp.bfloat16)
    merged_mask = (
        pad_mask[0]
        .reshape(lines, 2, half_grid, 2)[:, 0, :, 0]
        .reshape(merged_count)
        .astype(jnp.float32)
    )
    row_count = lax.axis_size("rows")
    row_me = lax.axis_index("rows")
    slabs = lax.all_to_all(merged_norm, "rows", split_axis=1, concat_axis=0, tiled=True)
    owner_hot = (owner[None, :] == jnp.arange(row_count, dtype=jnp.int32)[:, None]).astype(
        jnp.bfloat16
    )
    ordered = jnp.einsum(
        "jp,pms->jms",
        owner_hot,
        slabs.reshape(row_count, merged_count, -1),
        preferred_element_type=jnp.float32,
    ).astype(jnp.bfloat16)
    ordered = ordered.reshape(row_count * merged_count, -1)
    partial = jnp.dot(ordered, fc_weight, preferred_element_type=jnp.float32).reshape(
        row_count, merged_count, -1
    )
    own_slot = (jnp.arange(row_count, dtype=jnp.int32) == owner[row_me]).astype(jnp.float32)
    shift = own_slot[:, None] * ((merged_mask - 1.0) * MASK_SHIFT)[None, :]
    partial = (partial + shift[:, :, None]).astype(jnp.bfloat16)
    summed = lax.psum_scatter(
        partial.reshape(row_count * merged_count, -1),
        "rows",
        scatter_dimension=0,
        tiled=True,
    ).astype(jnp.float32)
    result = jax.nn.gelu(summed + fc_bias, approximate=False)
    return result.astype(jnp.bfloat16)[None]


def solution(mesh):
    return jax.shard_map(
        per_device,
        mesh=mesh,
        in_specs=(
            P("rows", "seq", None),
            P(),
            P(None, "seq"),
            P(None, "seq"),
            P("seq", None),
            P(),
            P("rows", "seq"),
            P("rows", "seq"),
            P(),
            P(),
            P("rows", None),
            P(),
            P(),
        ),
        out_specs=P("rows", "seq", None),
        check_vma=False,
    )
```

```python
import functools

import jax
import jax.numpy as jnp
from jax import lax
from jax.experimental import pallas as pl
from jax.experimental.pallas import tpu as pltpu
from jax.sharding import PartitionSpec as P

MESH = pl.DeviceIdType.MESH

D = 3200
HEAD_DIM = 128
HEADS = 16
GRID = 32
MASK_SHIFT = 1e6


def seq_sum_kernel(part_ref, out_ref, slots, send_sem, recv_sem):
    n = slots.shape[0]
    me = lax.axis_index("seq")
    row = lax.axis_index("rows")
    barrier = pltpu.get_barrier_semaphore()
    for k in range(1, n):
        peer = lax.rem(me + k, n)
        pl.semaphore_signal(barrier, inc=1, device_id=(row, peer), device_id_type=MESH)
    pl.semaphore_wait(barrier, n - 1)
    sends = []
    for k in range(1, n):
        peer = lax.rem(me + k, n)
        copy = pltpu.make_async_remote_copy(
            src_ref=part_ref,
            dst_ref=slots.at[me],
            send_sem=send_sem.at[k],
            recv_sem=recv_sem.at[me],
            device_id=(row, peer),
            device_id_type=MESH,
        )
        copy.start()
        sends.append(copy)
    for k in range(1, n):
        src = lax.rem(me + n - k, n)
        pltpu.make_async_remote_copy(
            src_ref=part_ref,
            dst_ref=slots.at[src],
            send_sem=send_sem.at[k],
            recv_sem=recv_sem.at[src],
            device_id=(row, src),
            device_id_type=MESH,
        ).wait_recv()
    for copy in sends:
        copy.wait_send()
    total = jnp.zeros(out_ref.shape, jnp.float32)
    for s in range(n):
        total = total + jnp.where(s == me, part_ref[...], slots[s])
    out_ref[...] = total


def seq_sum(part):
    n = lax.axis_size("seq")
    return pl.pallas_call(
        seq_sum_kernel,
        out_shape=jax.ShapeDtypeStruct(part.shape, jnp.float32),
        in_specs=[pl.BlockSpec(memory_space=pltpu.VMEM)],
        out_specs=pl.BlockSpec(memory_space=pltpu.VMEM),
        scratch_shapes=[
            pltpu.VMEM((n,) + part.shape, jnp.float32),
            pltpu.SemaphoreType.DMA((n,)),
            pltpu.SemaphoreType.DMA((n,)),
        ],
        compiler_params=pltpu.CompilerParams(collective_id=0, has_side_effects=True),
    )(part)


def attention_kernel(scale, q_ref, k_ref, v_ref, qrs_ref, krs_ref, qg_ref, kg_ref, qseg_ref,
                     kseg_ref, o_ref, key_norm, value_half, slots, landing, send_sem, recv_sem, local_sem):
    head, block = pl.program_id(0), pl.program_id(1)
    blocks = pl.num_programs(1)
    heads = pl.num_programs(0)
    me = lax.axis_index("seq")
    row = lax.axis_index("rows")

    @pl.when((head == 0) & (block == 0))
    def _():
        barrier = pltpu.get_barrier_semaphore()
        for k in range(1, o_ref.shape[0]):
            peer = lax.rem(me + k, o_ref.shape[0])
            pl.semaphore_signal(barrier, inc=1, device_id=(row, peer), device_id_type=MESH)
        pl.semaphore_wait(barrier, o_ref.shape[0] - 1)

    @pl.when(block == 0)
    def _():
        key_norm[...] = jnp.transpose(
            (k_ref[...] * krs_ref[...] * kg_ref[...]).astype(jnp.bfloat16)
        )
        value_half[...] = jnp.transpose(v_ref[...].astype(jnp.bfloat16))

    dest = lax.rem(me + 1 + block, blocks)
    width = slots.shape[1]
    start = pl.multiple_of(dest * width, width)
    query_norm = jnp.transpose(
        (q_ref[:, pl.ds(start, width)] * qrs_ref[:, pl.ds(start, width)] * qg_ref[...]).astype(
            jnp.bfloat16
        )
    )
    scores = (
        lax.dot_general(
            query_norm, key_norm[...], (((1,), (1,)), ((), ())), preferred_element_type=jnp.float32
        )
        * scale
    )
    scores = jnp.where(qseg_ref[pl.ds(start, width), :] == kseg_ref[...], scores, -1e30)
    peak_val = jnp.max(scores, axis=-1, keepdims=True)
    exp_terms = jnp.exp(scores - peak_val)
    total = jnp.sum(exp_terms, axis=-1, keepdims=True)
    probs = (exp_terms / total).astype(jnp.bfloat16)
    step = head * blocks + block
    slots[head * blocks + dest] = jnp.dot(probs, value_half[...], preferred_element_type=jnp.float32).astype(
        slots.dtype
    )

    def remote(h, i):
        return pltpu.make_async_remote_copy(
            src_ref=slots.at[h * blocks + i],
            dst_ref=landing.at[me, h],
            send_sem=send_sem.at[h * blocks + i],
            recv_sem=recv_sem.at[me, h],
            device_id=(row, i),
            device_id_type=MESH,
        )

    def local(h):
        return pltpu.make_async_copy(
            slots.at[h * blocks + me], landing.at[me, h], local_sem.at[h]
        )

    @pl.when(dest != me)
    def _():
        remote(head, dest).start()

    @pl.when(dest == me)
    def _():
        local(head).start()

    @pl.when(step == heads * blocks - 1)
    def _():
        for h in range(slots.shape[0] // o_ref.shape[0]):
            local(h).wait()
            for i in range(o_ref.shape[0]):
                @pl.when(i != me)
                def _():
                    remote(h, i).wait_send()
                    pltpu.make_async_remote_copy(
                        src_ref=slots.at[h * blocks + i],
                        dst_ref=landing.at[i, h],
                        send_sem=send_sem.at[h * blocks + i],
                        recv_sem=recv_sem.at[i, h],
                        device_id=(row, i),
                        device_id_type=MESH,
                    ).wait_recv()
        o_ref[...] = landing[...]


def attend_kernel(projected_t, query_rs, key_rs, qk_gain, row_segments, block_len, scale):
    length = projected_t.shape[1]
    heads_here = projected_t.shape[0] // (3 * HEAD_DIM)
    width = heads_here * HEAD_DIM
    blocks = length // block_len
    flops = 4 * length * length * width
    gain_block = pl.BlockSpec((HEAD_DIM, 1), lambda h, i: (h, 0))
    return pl.pallas_call(
        functools.partial(attention_kernel, scale),
        out_shape=jax.ShapeDtypeStruct((blocks, heads_here, block_len, HEAD_DIM), jnp.bfloat16),
        grid=(heads_here, blocks),
        in_specs=[
            pl.BlockSpec((HEAD_DIM, length), lambda h, i: (3 * h, 0)),
            pl.BlockSpec((HEAD_DIM, length), lambda h, i: (3 * h + 1, 0)),
            pl.BlockSpec((HEAD_DIM, length), lambda h, i: (3 * h + 2, 0)),
            pl.BlockSpec((1, length), lambda h, i: (0, 0)),
            pl.BlockSpec((1, length), lambda h, i: (0, 0)),
            gain_block,
            gain_block,
            pl.BlockSpec((length, 1), lambda h, i: (0, 0)),
            pl.BlockSpec((1, length), lambda h, i: (0, 0)),
        ],
        out_specs=pl.BlockSpec(memory_space=pltpu.VMEM),
        scratch_shapes=[
            pltpu.VMEM((length, HEAD_DIM), jnp.bfloat16),
            pltpu.VMEM((length, HEAD_DIM), jnp.bfloat16),
            pltpu.VMEM((heads_here * blocks, block_len, HEAD_DIM), jnp.bfloat16),
            pltpu.VMEM((blocks, heads_here, block_len, HEAD_DIM), jnp.bfloat16),
            pltpu.SemaphoreType.DMA((heads_here * blocks,)),
            pltpu.SemaphoreType.DMA((blocks, heads_here)),
            pltpu.SemaphoreType.DMA((heads_here,)),
        ],
        compiler_params=pltpu.CompilerParams(collective_id=2, has_side_effects=True),
        cost_estimate=pl.CostEstimate(
            flops=flops, transcendentals=length * length * heads_here, bytes_accessed=12 * length * width
        ),
    )(
        projected_t,
        projected_t,
        projected_t,
        query_rs.reshape(1, length),
        key_rs.reshape(1, length),
        qk_gain[0].reshape(width, 1),
        qk_gain[1].reshape(width, 1),
        row_segments.reshape(length, 1),
        row_segments.reshape(1, length),
    )


def out_proj_kernel(att_ref, w_ref, res_ref, ls_ref, o_ref):
    total = jnp.zeros(o_ref.shape, jnp.float32)
    for g in range(att_ref.shape[0]):
        term = jnp.dot(att_ref[g, 0], w_ref[g, 0], preferred_element_type=jnp.float32)
        term = term + jnp.dot(att_ref[g, 1], w_ref[g, 1], preferred_element_type=jnp.float32)
        total = total + term.astype(jnp.bfloat16).astype(jnp.float32)
    o_ref[...] = res_ref[...].astype(jnp.float32) + ls_ref[...] * total


def out_proj(attended, out_weight_groups, residual, layer_scale, tile=640):
    groups, heads_here, tokens, _ = attended.shape
    width = out_weight_groups.shape[-1]
    return pl.pallas_call(
        out_proj_kernel,
        out_shape=jax.ShapeDtypeStruct((tokens, width), jnp.float32),
        grid=(width // tile,),
        in_specs=[
            pl.BlockSpec(attended.shape, lambda j: (0, 0, 0, 0)),
            pl.BlockSpec((groups, heads_here, HEAD_DIM, tile), lambda j: (0, 0, 0, j)),
            pl.BlockSpec((tokens, tile), lambda j: (0, j)),
            pl.BlockSpec((1, tile), lambda j: (0, j)),
        ],
        out_specs=pl.BlockSpec((tokens, tile), lambda j: (0, j)),
        cost_estimate=pl.CostEstimate(
            flops=2 * tokens * groups * heads_here * HEAD_DIM * width,
            transcendentals=0,
            bytes_accessed=groups * heads_here * HEAD_DIM * width * 2 + tokens * width * 6,
        ),
    )(attended, out_weight_groups, residual, layer_scale.reshape(1, width))


def per_device(
    residual_in,
    norm_gain,
    qkv_weight,
    qk_gain,
    out_weight,
    layer_scale,
    segment_ids,
    pad_mask,
    ln_weight,
    ln_bias,
    fc_weight,
    fc_bias,
    owner,
):
    seq_count = lax.axis_size("seq")
    seq_me = lax.axis_index("seq")
    tokens = residual_in[0].astype(jnp.float32)
    shard_rows = tokens.shape[0]
    normed = (
        tokens * lax.rsqrt(jnp.mean(tokens * tokens, axis=-1, keepdims=True) + 1e-06) * norm_gain
    ).astype(jnp.bfloat16)
    row_tokens = lax.all_gather(normed, "seq", axis=0, tiled=True)
    length = row_tokens.shape[0]
    heads_here = qkv_weight.shape[1] // (3 * HEAD_DIM)
    projected_t = jnp.dot(row_tokens, qkv_weight, preferred_element_type=jnp.float32).T
    parts_t = projected_t.reshape(heads_here, 3, HEAD_DIM, length)
    seg_spread = lax.dynamic_update_slice_in_dim(
        jnp.zeros((length,), jnp.float32),
        segment_ids[0].astype(jnp.float32),
        seq_me * shard_rows,
        0,
    )
    stats = seq_sum(
        jnp.stack(
            [
                jnp.sum(parts_t[:, 0] * parts_t[:, 0], axis=(0, 1)),
                jnp.sum(parts_t[:, 1] * parts_t[:, 1], axis=(0, 1)),
                seg_spread,
            ]
        )
    )
    query_sq, key_sq, row_segments = stats[0], stats[1], stats[2]
    norm_width = HEADS * HEAD_DIM
    scale = HEAD_DIM ** (-0.5)
    attended = attend_kernel(
        projected_t,
        lax.rsqrt(query_sq / norm_width + 1e-06),
        lax.rsqrt(key_sq / norm_width + 1e-06),
        qk_gain,
        row_segments,
        256,
        scale,
    )
    full_out_weight = lax.all_gather(out_weight, "seq", axis=0, tiled=False)
    half_grid = GRID // 2
    lines = shard_rows // (2 * GRID)
    merged_count = shard_rows // 4

    def shuffle_rows(x, axis):
        shape = x.shape
        split = shape[:axis] + (lines, 2, half_grid, 2) + shape[axis + 1:]
        order = list(range(axis)) + [axis, axis + 2, axis + 1, axis + 3] + list(
            range(axis + 4, len(split))
        )
        return jnp.transpose(x.reshape(split), order).reshape(shape)

    hidden = out_proj(
        shuffle_rows(attended, 2),
        full_out_weight.reshape(seq_count, heads_here, HEAD_DIM, -1),
        shuffle_rows(residual_in[0], 0),
        layer_scale,
    )
    merged = hidden.reshape(merged_count, 4 * D)
    centre = merged - jnp.mean(merged, axis=-1, keepdims=True)
    spread = jnp.mean(centre * centre, axis=-1, keepdims=True)
    merged_norm = (centre * lax.rsqrt(spread + 1e-05) * ln_weight + ln_bias).astype(jnp.bfloat16)
    merged_mask = (
        pad_mask[0]
        .reshape(lines, 2, half_grid, 2)[:, 0, :, 0]
        .reshape(merged_count)
        .astype(jnp.float32)
    )
    row_count = lax.axis_size("rows")
    row_me = lax.axis_index("rows")
    slabs = lax.all_to_all(merged_norm, "rows", split_axis=1, concat_axis=0, tiled=True)
    owner_hot = (owner[None, :] == jnp.arange(row_count, dtype=jnp.int32)[:, None]).astype(
        jnp.bfloat16
    )
    ordered = jnp.einsum(
        "jp,pms->jms",
        owner_hot,
        slabs.reshape(row_count, merged_count, -1),
        preferred_element_type=jnp.float32,
    ).astype(jnp.bfloat16)
    ordered = ordered.reshape(row_count * merged_count, -1)
    partial = jnp.dot(ordered, fc_weight, preferred_element_type=jnp.float32).reshape(
        row_count, merged_count, -1
    )
    own_slot = (jnp.arange(row_count, dtype=jnp.int32) == owner[row_me]).astype(jnp.float32)
    shift = own_slot[:, None] * ((merged_mask - 1.0) * MASK_SHIFT)[None, :]
    partial = (partial + shift[:, :, None]).astype(jnp.bfloat16)
    summed = lax.psum_scatter(
        partial.reshape(row_count * merged_count, -1),
        "rows",
        scatter_dimension=0,
        tiled=True,
    ).astype(jnp.float32)
    result = jax.nn.gelu(summed + fc_bias, approximate=False)
    return result.astype(jnp.bfloat16)[None]


def solution(mesh):
    return jax.shard_map(
        per_device,
        mesh=mesh,
        in_specs=(
            P("rows", "seq", None),
            P(),
            P(None, "seq"),
            P(None, "seq"),
            P("seq", None),
            P(),
            P("rows", "seq"),
            P("rows", "seq"),
            P(),
            P(),
            P("rows", None),
            P(),
            P(),
        ),
        out_specs=P("rows", "seq", None),
        check_vma=False,
    )
```

```python
import functools

import jax
import jax.numpy as jnp
from jax import lax
from jax.experimental import pallas as pl
from jax.experimental.pallas import tpu as pltpu
from jax.sharding import PartitionSpec as P

MESH = pl.DeviceIdType.MESH

D = 3200
HEAD_DIM = 128
HEADS = 16
GRID = 32
MASK_SHIFT = 1e6


def seq_sum_kernel(part_ref, out_ref, slots, send_sem, recv_sem):
    n = slots.shape[0]
    me = lax.axis_index("seq")
    row = lax.axis_index("rows")
    barrier = pltpu.get_barrier_semaphore()
    for k in range(1, n):
        peer = lax.rem(me + k, n)
        pl.semaphore_signal(barrier, inc=1, device_id=(row, peer), device_id_type=MESH)
    pl.semaphore_wait(barrier, n - 1)
    sends = []
    for k in range(1, n):
        peer = lax.rem(me + k, n)
        copy = pltpu.make_async_remote_copy(
            src_ref=part_ref,
            dst_ref=slots.at[me],
            send_sem=send_sem.at[k],
            recv_sem=recv_sem.at[me],
            device_id=(row, peer),
            device_id_type=MESH,
        )
        copy.start()
        sends.append(copy)
    for k in range(1, n):
        src = lax.rem(me + n - k, n)
        pltpu.make_async_remote_copy(
            src_ref=part_ref,
            dst_ref=slots.at[src],
            send_sem=send_sem.at[k],
            recv_sem=recv_sem.at[src],
            device_id=(row, src),
            device_id_type=MESH,
        ).wait_recv()
    for copy in sends:
        copy.wait_send()
    total = jnp.zeros(out_ref.shape, jnp.float32)
    for s in range(n):
        total = total + jnp.where(s == me, part_ref[...], slots[s])
    out_ref[...] = total


def seq_sum(part):
    n = lax.axis_size("seq")
    return pl.pallas_call(
        seq_sum_kernel,
        out_shape=jax.ShapeDtypeStruct(part.shape, jnp.float32),
        in_specs=[pl.BlockSpec(memory_space=pltpu.VMEM)],
        out_specs=pl.BlockSpec(memory_space=pltpu.VMEM),
        scratch_shapes=[
            pltpu.VMEM((n,) + part.shape, jnp.float32),
            pltpu.SemaphoreType.DMA((n,)),
            pltpu.SemaphoreType.DMA((n,)),
        ],
        compiler_params=pltpu.CompilerParams(collective_id=0, has_side_effects=True),
    )(part)


def attention_kernel(scale, q_ref, k_ref, v_ref, qrs_ref, krs_ref, qg_ref, kg_ref, qseg_ref,
                     kseg_ref, o_ref, key_norm, value_half, slots, landing, send_sem, recv_sem, local_sem):
    head, block = pl.program_id(0), pl.program_id(1)
    blocks = pl.num_programs(1)
    heads = pl.num_programs(0)
    me = lax.axis_index("seq")
    row = lax.axis_index("rows")

    @pl.when((head == 0) & (block == 0))
    def _():
        barrier = pltpu.get_barrier_semaphore()
        for k in range(1, o_ref.shape[0]):
            peer = lax.rem(me + k, o_ref.shape[0])
            pl.semaphore_signal(barrier, inc=1, device_id=(row, peer), device_id_type=MESH)
        pl.semaphore_wait(barrier, o_ref.shape[0] - 1)

    @pl.when(block == 0)
    def _():
        key_norm[...] = jnp.transpose(
            (k_ref[...] * krs_ref[...] * kg_ref[...]).astype(jnp.bfloat16)
        )
        value_half[...] = jnp.transpose(v_ref[...].astype(jnp.bfloat16))

    dest = lax.rem(me + 1 + block, blocks)
    width = slots.shape[1]
    start = pl.multiple_of(dest * width, width)
    query_norm = jnp.transpose(
        (q_ref[:, pl.ds(start, width)] * qrs_ref[:, pl.ds(start, width)] * qg_ref[...]).astype(
            jnp.bfloat16
        )
    )
    scores = (
        lax.dot_general(
            query_norm, key_norm[...], (((1,), (1,)), ((), ())), preferred_element_type=jnp.float32
        )
        * scale
    )
    scores = jnp.where(qseg_ref[pl.ds(start, width), :] == kseg_ref[...], scores, -1e30)
    peak_val = jnp.max(scores, axis=-1, keepdims=True)
    exp_terms = jnp.exp(scores - peak_val)
    total = jnp.sum(exp_terms, axis=-1, keepdims=True)
    probs = (exp_terms / total).astype(jnp.bfloat16)
    step = head * blocks + block
    slots[head * blocks + dest] = jnp.dot(probs, value_half[...], preferred_element_type=jnp.float32).astype(
        slots.dtype
    )

    def remote(h, i):
        return pltpu.make_async_remote_copy(
            src_ref=slots.at[h * blocks + i],
            dst_ref=landing.at[me, h],
            send_sem=send_sem.at[h * blocks + i],
            recv_sem=recv_sem.at[me, h],
            device_id=(row, i),
            device_id_type=MESH,
        )

    def local(h):
        return pltpu.make_async_copy(
            slots.at[h * blocks + me], landing.at[me, h], local_sem.at[h]
        )

    @pl.when(dest != me)
    def _():
        remote(head, dest).start()

    @pl.when(dest == me)
    def _():
        local(head).start()

    @pl.when(step == heads * blocks - 1)
    def _():
        for h in range(slots.shape[0] // o_ref.shape[0]):
            local(h).wait()
            for i in range(o_ref.shape[0]):
                @pl.when(i != me)
                def _():
                    remote(h, i).wait_send()
                    pltpu.make_async_remote_copy(
                        src_ref=slots.at[h * blocks + i],
                        dst_ref=landing.at[i, h],
                        send_sem=send_sem.at[h * blocks + i],
                        recv_sem=recv_sem.at[i, h],
                        device_id=(row, i),
                        device_id_type=MESH,
                    ).wait_recv()
        o_ref[...] = landing[...]


def attend_kernel(projected_t, query_rs, key_rs, qk_gain, row_segments, block_len, scale):
    length = projected_t.shape[1]
    heads_here = projected_t.shape[0] // (3 * HEAD_DIM)
    width = heads_here * HEAD_DIM
    blocks = length // block_len
    flops = 4 * length * length * width
    gain_block = pl.BlockSpec((HEAD_DIM, 1), lambda h, i: (h, 0))
    return pl.pallas_call(
        functools.partial(attention_kernel, scale),
        out_shape=jax.ShapeDtypeStruct((blocks, heads_here, block_len, HEAD_DIM), jnp.bfloat16),
        grid=(heads_here, blocks),
        in_specs=[
            pl.BlockSpec((HEAD_DIM, length), lambda h, i: (3 * h, 0)),
            pl.BlockSpec((HEAD_DIM, length), lambda h, i: (3 * h + 1, 0)),
            pl.BlockSpec((HEAD_DIM, length), lambda h, i: (3 * h + 2, 0)),
            pl.BlockSpec((1, length), lambda h, i: (0, 0)),
            pl.BlockSpec((1, length), lambda h, i: (0, 0)),
            gain_block,
            gain_block,
            pl.BlockSpec((length, 1), lambda h, i: (0, 0)),
            pl.BlockSpec((1, length), lambda h, i: (0, 0)),
        ],
        out_specs=pl.BlockSpec(memory_space=pltpu.VMEM),
        scratch_shapes=[
            pltpu.VMEM((length, HEAD_DIM), jnp.bfloat16),
            pltpu.VMEM((length, HEAD_DIM), jnp.bfloat16),
            pltpu.VMEM((heads_here * blocks, block_len, HEAD_DIM), jnp.bfloat16),
            pltpu.VMEM((blocks, heads_here, block_len, HEAD_DIM), jnp.bfloat16),
            pltpu.SemaphoreType.DMA((heads_here * blocks,)),
            pltpu.SemaphoreType.DMA((blocks, heads_here)),
            pltpu.SemaphoreType.DMA((heads_here,)),
        ],
        compiler_params=pltpu.CompilerParams(collective_id=2, has_side_effects=True),
        cost_estimate=pl.CostEstimate(
            flops=flops, transcendentals=length * length * heads_here, bytes_accessed=12 * length * width
        ),
    )(
        projected_t,
        projected_t,
        projected_t,
        query_rs.reshape(1, length),
        key_rs.reshape(1, length),
        qk_gain[0].reshape(width, 1),
        qk_gain[1].reshape(width, 1),
        row_segments.reshape(length, 1),
        row_segments.reshape(1, length),
    )


def out_proj_kernel(att_ref, w_ref, res_ref, ls_ref, o_ref):
    total = jnp.zeros(o_ref.shape, jnp.float32)
    for g in range(att_ref.shape[0]):
        heads = jnp.concatenate([att_ref[g, 0], att_ref[g, 1]], axis=1)
        weights = w_ref[g].reshape(2 * HEAD_DIM, w_ref.shape[-1])
        term = jnp.dot(heads, weights, preferred_element_type=jnp.float32)
        total = total + term.astype(jnp.bfloat16).astype(jnp.float32)
    o_ref[...] = res_ref[...].astype(jnp.float32) + ls_ref[...] * total


def out_proj(attended, out_weight_groups, residual, layer_scale, tile=640):
    groups, heads_here, tokens, _ = attended.shape
    width = out_weight_groups.shape[-1]
    return pl.pallas_call(
        out_proj_kernel,
        out_shape=jax.ShapeDtypeStruct((tokens, width), jnp.float32),
        grid=(width // tile,),
        in_specs=[
            pl.BlockSpec(attended.shape, lambda j: (0, 0, 0, 0)),
            pl.BlockSpec((groups, heads_here, HEAD_DIM, tile), lambda j: (0, 0, 0, j)),
            pl.BlockSpec((tokens, tile), lambda j: (0, j)),
            pl.BlockSpec((1, tile), lambda j: (0, j)),
        ],
        out_specs=pl.BlockSpec((tokens, tile), lambda j: (0, j)),
        cost_estimate=pl.CostEstimate(
            flops=2 * tokens * groups * heads_here * HEAD_DIM * width,
            transcendentals=0,
            bytes_accessed=groups * heads_here * HEAD_DIM * width * 2 + tokens * width * 6,
        ),
    )(attended, out_weight_groups, residual, layer_scale.reshape(1, width))


def per_device(
    residual_in,
    norm_gain,
    qkv_weight,
    qk_gain,
    out_weight,
    layer_scale,
    segment_ids,
    pad_mask,
    ln_weight,
    ln_bias,
    fc_weight,
    fc_bias,
    owner,
):
    seq_count = lax.axis_size("seq")
    seq_me = lax.axis_index("seq")
    tokens = residual_in[0].astype(jnp.float32)
    shard_rows = tokens.shape[0]
    normed = (
        tokens * lax.rsqrt(jnp.mean(tokens * tokens, axis=-1, keepdims=True) + 1e-06) * norm_gain
    ).astype(jnp.bfloat16)
    row_tokens = lax.all_gather(normed, "seq", axis=0, tiled=True)
    length = row_tokens.shape[0]
    heads_here = qkv_weight.shape[1] // (3 * HEAD_DIM)
    projected_t = jnp.dot(row_tokens, qkv_weight, preferred_element_type=jnp.float32).T
    parts_t = projected_t.reshape(heads_here, 3, HEAD_DIM, length)
    seg_spread = lax.dynamic_update_slice_in_dim(
        jnp.zeros((length,), jnp.float32),
        segment_ids[0].astype(jnp.float32),
        seq_me * shard_rows,
        0,
    )
    stats = seq_sum(
        jnp.stack(
            [
                jnp.sum(parts_t[:, 0] * parts_t[:, 0], axis=(0, 1)),
                jnp.sum(parts_t[:, 1] * parts_t[:, 1], axis=(0, 1)),
                seg_spread,
            ]
        )
    )
    query_sq, key_sq, row_segments = stats[0], stats[1], stats[2]
    norm_width = HEADS * HEAD_DIM
    scale = HEAD_DIM ** (-0.5)
    attended = attend_kernel(
        projected_t,
        lax.rsqrt(query_sq / norm_width + 1e-06),
        lax.rsqrt(key_sq / norm_width + 1e-06),
        qk_gain,
        row_segments,
        256,
        scale,
    )
    full_out_weight = lax.all_gather(out_weight, "seq", axis=0, tiled=False)
    half_grid = GRID // 2
    lines = shard_rows // (2 * GRID)
    merged_count = shard_rows // 4

    def shuffle_rows(x, axis):
        shape = x.shape
        split = shape[:axis] + (lines, 2, half_grid, 2) + shape[axis + 1:]
        order = list(range(axis)) + [axis, axis + 2, axis + 1, axis + 3] + list(
            range(axis + 4, len(split))
        )
        return jnp.transpose(x.reshape(split), order).reshape(shape)

    hidden = out_proj(
        shuffle_rows(attended, 2),
        full_out_weight.reshape(seq_count, heads_here, HEAD_DIM, -1),
        shuffle_rows(residual_in[0], 0),
        layer_scale,
    )
    merged = hidden.reshape(merged_count, 4 * D)
    centre = merged - jnp.mean(merged, axis=-1, keepdims=True)
    spread = jnp.mean(centre * centre, axis=-1, keepdims=True)
    merged_norm = (centre * lax.rsqrt(spread + 1e-05) * ln_weight + ln_bias).astype(jnp.bfloat16)
    merged_mask = (
        pad_mask[0]
        .reshape(lines, 2, half_grid, 2)[:, 0, :, 0]
        .reshape(merged_count)
        .astype(jnp.float32)
    )
    row_count = lax.axis_size("rows")
    row_me = lax.axis_index("rows")
    slabs = lax.all_to_all(merged_norm, "rows", split_axis=1, concat_axis=0, tiled=True)
    owner_hot = (owner[None, :] == jnp.arange(row_count, dtype=jnp.int32)[:, None]).astype(
        jnp.bfloat16
    )
    ordered = jnp.einsum(
        "jp,pms->jms",
        owner_hot,
        slabs.reshape(row_count, merged_count, -1),
        preferred_element_type=jnp.float32,
    ).astype(jnp.bfloat16)
    ordered = ordered.reshape(row_count * merged_count, -1)
    partial = jnp.dot(ordered, fc_weight, preferred_element_type=jnp.float32).reshape(
        row_count, merged_count, -1
    )
    own_slot = (jnp.arange(row_count, dtype=jnp.int32) == owner[row_me]).astype(jnp.float32)
    shift = own_slot[:, None] * ((merged_mask - 1.0) * MASK_SHIFT)[None, :]
    partial = (partial + shift[:, :, None]).astype(jnp.bfloat16)
    summed = lax.psum_scatter(
        partial.reshape(row_count * merged_count, -1),
        "rows",
        scatter_dimension=0,
        tiled=True,
    ).astype(jnp.float32)
    result = jax.nn.gelu(summed + fc_bias, approximate=False)
    return result.astype(jnp.bfloat16)[None]


def solution(mesh):
    return jax.shard_map(
        per_device,
        mesh=mesh,
        in_specs=(
            P("rows", "seq", None),
            P(),
            P(None, "seq"),
            P(None, "seq"),
            P("seq", None),
            P(),
            P("rows", "seq"),
            P("rows", "seq"),
            P(),
            P(),
            P("rows", None),
            P(),
            P(),
        ),
        out_specs=P("rows", "seq", None),
        check_vma=False,
    )
```

```python
import functools

import jax
import jax.numpy as jnp
from jax import lax
from jax.experimental import pallas as pl
from jax.experimental.pallas import tpu as pltpu
from jax.sharding import PartitionSpec as P

MESH = pl.DeviceIdType.MESH

D = 3200
HEAD_DIM = 128
HEADS = 16
GRID = 32
MASK_SHIFT = 1e6


def seq_sum_kernel(part_ref, out_ref, slots, send_sem, recv_sem):
    n = slots.shape[0]
    me = lax.axis_index("seq")
    row = lax.axis_index("rows")
    barrier = pltpu.get_barrier_semaphore()
    for k in range(1, n):
        peer = lax.rem(me + k, n)
        pl.semaphore_signal(barrier, inc=1, device_id=(row, peer), device_id_type=MESH)
    pl.semaphore_wait(barrier, n - 1)
    sends = []
    for k in range(1, n):
        peer = lax.rem(me + k, n)
        copy = pltpu.make_async_remote_copy(
            src_ref=part_ref,
            dst_ref=slots.at[me],
            send_sem=send_sem.at[k],
            recv_sem=recv_sem.at[me],
            device_id=(row, peer),
            device_id_type=MESH,
        )
        copy.start()
        sends.append(copy)
    for k in range(1, n):
        src = lax.rem(me + n - k, n)
        pltpu.make_async_remote_copy(
            src_ref=part_ref,
            dst_ref=slots.at[src],
            send_sem=send_sem.at[k],
            recv_sem=recv_sem.at[src],
            device_id=(row, src),
            device_id_type=MESH,
        ).wait_recv()
    for copy in sends:
        copy.wait_send()
    total = jnp.zeros(out_ref.shape, jnp.float32)
    for s in range(n):
        total = total + jnp.where(s == me, part_ref[...], slots[s])
    out_ref[...] = total


def seq_sum(part):
    n = lax.axis_size("seq")
    return pl.pallas_call(
        seq_sum_kernel,
        out_shape=jax.ShapeDtypeStruct(part.shape, jnp.float32),
        in_specs=[pl.BlockSpec(memory_space=pltpu.VMEM)],
        out_specs=pl.BlockSpec(memory_space=pltpu.VMEM),
        scratch_shapes=[
            pltpu.VMEM((n,) + part.shape, jnp.float32),
            pltpu.SemaphoreType.DMA((n,)),
            pltpu.SemaphoreType.DMA((n,)),
        ],
        compiler_params=pltpu.CompilerParams(collective_id=0, has_side_effects=True),
    )(part)


def attention_kernel(scale, q_ref, k_ref, v_ref, qrs_ref, krs_ref, qg_ref, kg_ref, qseg_ref,
                     kseg_ref, o_ref, key_norm, value_half, slots, landing, send_sem, recv_sem, local_sem):
    head, block = pl.program_id(0), pl.program_id(1)
    blocks = pl.num_programs(1)
    heads = pl.num_programs(0)
    me = lax.axis_index("seq")
    row = lax.axis_index("rows")

    @pl.when((head == 0) & (block == 0))
    def _():
        barrier = pltpu.get_barrier_semaphore()
        for k in range(1, o_ref.shape[0]):
            peer = lax.rem(me + k, o_ref.shape[0])
            pl.semaphore_signal(barrier, inc=1, device_id=(row, peer), device_id_type=MESH)
        pl.semaphore_wait(barrier, o_ref.shape[0] - 1)

    @pl.when(block == 0)
    def _():
        key_norm[...] = jnp.transpose(
            (k_ref[...] * krs_ref[...] * kg_ref[...]).astype(jnp.bfloat16)
        )
        value_half[...] = jnp.transpose(v_ref[...].astype(jnp.bfloat16))

    dest = lax.rem(me + 1 + block, blocks)
    width = slots.shape[1]
    start = pl.multiple_of(dest * width, width)
    query_norm = jnp.transpose(
        (q_ref[:, pl.ds(start, width)] * qrs_ref[:, pl.ds(start, width)] * qg_ref[...]).astype(
            jnp.bfloat16
        )
    )
    scores = (
        lax.dot_general(
            query_norm, key_norm[...], (((1,), (1,)), ((), ())), preferred_element_type=jnp.float32
        )
        * scale
    )
    scores = jnp.where(qseg_ref[pl.ds(start, width), :] == kseg_ref[...], scores, -1e30)
    peak_val = jnp.max(scores, axis=-1, keepdims=True)
    exp_terms = jnp.exp(scores - peak_val)
    total = jnp.sum(exp_terms, axis=-1, keepdims=True)
    probs = (exp_terms / total).astype(jnp.bfloat16)
    step = head * blocks + block
    slots[head * blocks + dest] = jnp.dot(probs, value_half[...], preferred_element_type=jnp.float32).astype(
        slots.dtype
    )

    def remote(h, i):
        return pltpu.make_async_remote_copy(
            src_ref=slots.at[h * blocks + i],
            dst_ref=landing.at[me, h],
            send_sem=send_sem.at[h * blocks + i],
            recv_sem=recv_sem.at[me, h],
            device_id=(row, i),
            device_id_type=MESH,
        )

    def local(h):
        return pltpu.make_async_copy(
            slots.at[h * blocks + me], landing.at[me, h], local_sem.at[h]
        )

    @pl.when(dest != me)
    def _():
        remote(head, dest).start()

    @pl.when(dest == me)
    def _():
        local(head).start()

    @pl.when(step == heads * blocks - 1)
    def _():
        for h in range(slots.shape[0] // o_ref.shape[0]):
            local(h).wait()
            for i in range(o_ref.shape[0]):
                @pl.when(i != me)
                def _():
                    remote(h, i).wait_send()
                    pltpu.make_async_remote_copy(
                        src_ref=slots.at[h * blocks + i],
                        dst_ref=landing.at[i, h],
                        send_sem=send_sem.at[h * blocks + i],
                        recv_sem=recv_sem.at[i, h],
                        device_id=(row, i),
                        device_id_type=MESH,
                    ).wait_recv()
        o_ref[...] = landing[...]


def attend_kernel(projected_t, query_rs, key_rs, qk_gain, row_segments, block_len, scale):
    length = projected_t.shape[1]
    heads_here = projected_t.shape[0] // (3 * HEAD_DIM)
    width = heads_here * HEAD_DIM
    blocks = length // block_len
    flops = 4 * length * length * width
    gain_block = pl.BlockSpec((HEAD_DIM, 1), lambda h, i: (h, 0))
    return pl.pallas_call(
        functools.partial(attention_kernel, scale),
        out_shape=jax.ShapeDtypeStruct((blocks, heads_here, block_len, HEAD_DIM), jnp.bfloat16),
        grid=(heads_here, blocks),
        in_specs=[
            pl.BlockSpec((HEAD_DIM, length), lambda h, i: (3 * h, 0)),
            pl.BlockSpec((HEAD_DIM, length), lambda h, i: (3 * h + 1, 0)),
            pl.BlockSpec((HEAD_DIM, length), lambda h, i: (3 * h + 2, 0)),
            pl.BlockSpec((1, length), lambda h, i: (0, 0)),
            pl.BlockSpec((1, length), lambda h, i: (0, 0)),
            gain_block,
            gain_block,
            pl.BlockSpec((length, 1), lambda h, i: (0, 0)),
            pl.BlockSpec((1, length), lambda h, i: (0, 0)),
        ],
        out_specs=pl.BlockSpec(memory_space=pltpu.VMEM),
        scratch_shapes=[
            pltpu.VMEM((length, HEAD_DIM), jnp.bfloat16),
            pltpu.VMEM((length, HEAD_DIM), jnp.bfloat16),
            pltpu.VMEM((heads_here * blocks, block_len, HEAD_DIM), jnp.bfloat16),
            pltpu.VMEM((blocks, heads_here, block_len, HEAD_DIM), jnp.bfloat16),
            pltpu.SemaphoreType.DMA((heads_here * blocks,)),
            pltpu.SemaphoreType.DMA((blocks, heads_here)),
            pltpu.SemaphoreType.DMA((heads_here,)),
        ],
        compiler_params=pltpu.CompilerParams(collective_id=2, has_side_effects=True),
        cost_estimate=pl.CostEstimate(
            flops=flops, transcendentals=length * length * heads_here, bytes_accessed=12 * length * width
        ),
    )(
        projected_t,
        projected_t,
        projected_t,
        query_rs.reshape(1, length),
        key_rs.reshape(1, length),
        qk_gain[0].reshape(width, 1),
        qk_gain[1].reshape(width, 1),
        row_segments.reshape(length, 1),
        row_segments.reshape(1, length),
    )


def out_proj_kernel(att_ref, w_ref, res_ref, ls_ref, o_ref):
    total = jnp.zeros(o_ref.shape, jnp.float32)
    for g in range(att_ref.shape[0]):
        heads = jnp.concatenate([att_ref[g, 0], att_ref[g, 1]], axis=1)
        weights = w_ref[g].reshape(2 * HEAD_DIM, w_ref.shape[-1])
        term = jnp.dot(heads, weights, preferred_element_type=jnp.float32)
        total = total + term.astype(jnp.bfloat16).astype(jnp.float32)
    o_ref[...] = res_ref[...].astype(jnp.float32) + ls_ref[...] * total


def out_proj(attended, out_weight_groups, residual, layer_scale, tile=640):
    groups, heads_here, tokens, _ = attended.shape
    width = out_weight_groups.shape[-1]
    return pl.pallas_call(
        out_proj_kernel,
        out_shape=jax.ShapeDtypeStruct((tokens, width), jnp.float32),
        grid=(width // tile,),
        in_specs=[
            pl.BlockSpec(attended.shape, lambda j: (0, 0, 0, 0)),
            pl.BlockSpec((groups, heads_here, HEAD_DIM, tile), lambda j: (0, 0, 0, j)),
            pl.BlockSpec((tokens, tile), lambda j: (0, j)),
            pl.BlockSpec((1, tile), lambda j: (0, j)),
        ],
        out_specs=pl.BlockSpec((tokens, tile), lambda j: (0, j)),
        cost_estimate=pl.CostEstimate(
            flops=2 * tokens * groups * heads_here * HEAD_DIM * width,
            transcendentals=0,
            bytes_accessed=groups * heads_here * HEAD_DIM * width * 2 + tokens * width * 6,
        ),
    )(attended, out_weight_groups, residual, layer_scale.reshape(1, width))


def per_device(
    residual_in,
    norm_gain,
    qkv_weight,
    qk_gain,
    out_weight,
    layer_scale,
    segment_ids,
    pad_mask,
    ln_weight,
    ln_bias,
    fc_weight,
    fc_bias,
    owner,
):
    seq_count = lax.axis_size("seq")
    seq_me = lax.axis_index("seq")
    tokens = residual_in[0].astype(jnp.float32)
    shard_rows = tokens.shape[0]
    normed = (
        tokens * lax.rsqrt(jnp.mean(tokens * tokens, axis=-1, keepdims=True) + 1e-06) * norm_gain
    ).astype(jnp.bfloat16)
    row_tokens = lax.all_gather(normed, "seq", axis=0, tiled=True)
    length = row_tokens.shape[0]
    heads_here = qkv_weight.shape[1] // (3 * HEAD_DIM)
    projected_t = jnp.dot(row_tokens, qkv_weight, preferred_element_type=jnp.float32).T
    parts_t = projected_t.reshape(heads_here, 3, HEAD_DIM, length)
    seg_spread = lax.dynamic_update_slice_in_dim(
        jnp.zeros((length,), jnp.float32),
        segment_ids[0].astype(jnp.float32),
        seq_me * shard_rows,
        0,
    )
    stats = seq_sum(
        jnp.stack(
            [
                jnp.sum(parts_t[:, 0] * parts_t[:, 0], axis=(0, 1)),
                jnp.sum(parts_t[:, 1] * parts_t[:, 1], axis=(0, 1)),
                seg_spread,
            ]
        )
    )
    query_sq, key_sq, row_segments = stats[0], stats[1], stats[2]
    norm_width = HEADS * HEAD_DIM
    scale = HEAD_DIM ** (-0.5)
    attended = attend_kernel(
        projected_t,
        lax.rsqrt(query_sq / norm_width + 1e-06),
        lax.rsqrt(key_sq / norm_width + 1e-06),
        qk_gain,
        row_segments,
        256,
        scale,
    )
    full_out_weight = lax.all_gather(out_weight, "seq", axis=0, tiled=False)
    half_grid = GRID // 2
    lines = shard_rows // (2 * GRID)
    merged_count = shard_rows // 4

    def shuffle_rows(x, axis):
        shape = x.shape
        split = shape[:axis] + (lines, 2, half_grid, 2) + shape[axis + 1:]
        order = list(range(axis)) + [axis, axis + 2, axis + 1, axis + 3] + list(
            range(axis + 4, len(split))
        )
        return jnp.transpose(x.reshape(split), order).reshape(shape)

    hidden = out_proj(
        shuffle_rows(attended, 2),
        full_out_weight.reshape(seq_count, heads_here, HEAD_DIM, -1),
        shuffle_rows(residual_in[0], 0),
        layer_scale,
    )
    merged = hidden.reshape(merged_count, 4 * D)
    centre = merged - jnp.mean(merged, axis=-1, keepdims=True)
    spread = jnp.mean(centre * centre, axis=-1, keepdims=True)
    merged_norm = (centre * lax.rsqrt(spread + 1e-05) * ln_weight + ln_bias).astype(jnp.bfloat16)
    merged_mask = (
        pad_mask[0]
        .reshape(lines, 2, half_grid, 2)[:, 0, :, 0]
        .reshape(merged_count)
        .astype(jnp.float32)
    )
    row_count = lax.axis_size("rows")
    row_me = lax.axis_index("rows")
    slabs = lax.all_to_all(merged_norm, "rows", split_axis=1, concat_axis=0, tiled=True)
    owner_hot = (owner[None, :] == jnp.arange(row_count, dtype=jnp.int32)[:, None]).astype(
        jnp.bfloat16
    )
    ordered = jnp.einsum(
        "jp,pms->jms",
        owner_hot,
        slabs.reshape(row_count, merged_count, -1),
        preferred_element_type=jnp.float32,
    ).astype(jnp.bfloat16)
    ordered = ordered.reshape(row_count * merged_count, -1)
    partial = jnp.dot(ordered, fc_weight, preferred_element_type=jnp.float32).reshape(
        row_count, merged_count, -1
    )
    own_slot = (jnp.arange(row_count, dtype=jnp.int32) == owner[row_me]).astype(jnp.float32)
    shift = own_slot[:, None] * ((merged_mask - 1.0) * MASK_SHIFT)[None, :]
    partial = (partial + shift[:, :, None]).astype(jnp.bfloat16)
    summed = lax.psum_scatter(
        partial.reshape(row_count * merged_count, -1),
        "rows",
        scatter_dimension=0,
        tiled=True,
    ).astype(jnp.float32)
    pre = summed + fc_bias
    result = pre * (1.0 + lax.erf(pre * (2.0 ** -0.5))) * 0.5
    return result.astype(jnp.bfloat16)[None]


def solution(mesh):
    return jax.shard_map(
        per_device,
        mesh=mesh,
        in_specs=(
            P("rows", "seq", None),
            P(),
            P(None, "seq"),
            P(None, "seq"),
            P("seq", None),
            P(),
            P("rows", "seq"),
            P("rows", "seq"),
            P(),
            P(),
            P("rows", None),
            P(),
            P(),
        ),
        out_specs=P("rows", "seq", None),
        check_vma=False,
    )
```

```python
import functools

import jax
import jax.numpy as jnp
from jax import lax
from jax.experimental import pallas as pl
from jax.experimental.pallas import tpu as pltpu
from jax.sharding import PartitionSpec as P

MESH = pl.DeviceIdType.MESH

D = 3200
HEAD_DIM = 128
HEADS = 16
GRID = 32
MASK_SHIFT = 1e6


def seq_sum_kernel(part_ref, out_ref, slots, send_sem, recv_sem):
    n = slots.shape[0]
    me = lax.axis_index("seq")
    row = lax.axis_index("rows")
    barrier = pltpu.get_barrier_semaphore()
    for k in range(1, n):
        peer = lax.rem(me + k, n)
        pl.semaphore_signal(barrier, inc=1, device_id=(row, peer), device_id_type=MESH)
    pl.semaphore_wait(barrier, n - 1)
    sends = []
    for k in range(1, n):
        peer = lax.rem(me + k, n)
        copy = pltpu.make_async_remote_copy(
            src_ref=part_ref,
            dst_ref=slots.at[me],
            send_sem=send_sem.at[k],
            recv_sem=recv_sem.at[me],
            device_id=(row, peer),
            device_id_type=MESH,
        )
        copy.start()
        sends.append(copy)
    for k in range(1, n):
        src = lax.rem(me + n - k, n)
        pltpu.make_async_remote_copy(
            src_ref=part_ref,
            dst_ref=slots.at[src],
            send_sem=send_sem.at[k],
            recv_sem=recv_sem.at[src],
            device_id=(row, src),
            device_id_type=MESH,
        ).wait_recv()
    for copy in sends:
        copy.wait_send()
    total = jnp.zeros(out_ref.shape, jnp.float32)
    for s in range(n):
        total = total + jnp.where(s == me, part_ref[...], slots[s])
    out_ref[...] = total


def seq_sum(part):
    n = lax.axis_size("seq")
    return pl.pallas_call(
        seq_sum_kernel,
        out_shape=jax.ShapeDtypeStruct(part.shape, jnp.float32),
        in_specs=[pl.BlockSpec(memory_space=pltpu.VMEM)],
        out_specs=pl.BlockSpec(memory_space=pltpu.VMEM),
        scratch_shapes=[
            pltpu.VMEM((n,) + part.shape, jnp.float32),
            pltpu.SemaphoreType.DMA((n,)),
            pltpu.SemaphoreType.DMA((n,)),
        ],
        compiler_params=pltpu.CompilerParams(collective_id=0, has_side_effects=True),
    )(part)


def attention_kernel(scale, q_ref, k_ref, v_ref, qrs_ref, krs_ref, qg_ref, kg_ref, qseg_ref,
                     kseg_ref, o_ref, key_norm, value_half, slots, landing, send_sem, recv_sem, local_sem):
    head, block = pl.program_id(0), pl.program_id(1)
    blocks = pl.num_programs(1)
    heads = pl.num_programs(0)
    me = lax.axis_index("seq")
    row = lax.axis_index("rows")

    @pl.when((head == 0) & (block == 0))
    def _():
        barrier = pltpu.get_barrier_semaphore()
        for k in range(1, o_ref.shape[0]):
            peer = lax.rem(me + k, o_ref.shape[0])
            pl.semaphore_signal(barrier, inc=1, device_id=(row, peer), device_id_type=MESH)
        pl.semaphore_wait(barrier, o_ref.shape[0] - 1)

    @pl.when(block == 0)
    def _():
        key_norm[...] = jnp.transpose(
            (k_ref[...] * krs_ref[...] * kg_ref[...]).astype(jnp.bfloat16)
        )
        value_half[...] = jnp.transpose(v_ref[...].astype(jnp.bfloat16))

    dest = lax.rem(me + 1 + block, blocks)
    width = slots.shape[1]
    start = pl.multiple_of(dest * width, width)
    query_norm = jnp.transpose(
        (q_ref[:, pl.ds(start, width)] * qrs_ref[:, pl.ds(start, width)] * qg_ref[...]).astype(
            jnp.bfloat16
        )
    )
    scores = (
        lax.dot_general(
            query_norm, key_norm[...], (((1,), (1,)), ((), ())), preferred_element_type=jnp.float32
        )
        * scale
    )
    scores = jnp.where(qseg_ref[pl.ds(start, width), :] == kseg_ref[...], scores, -1e30)
    peak_val = jnp.max(scores, axis=-1, keepdims=True)
    exp_terms = jnp.exp(scores - peak_val)
    total = jnp.sum(exp_terms, axis=-1, keepdims=True)
    probs = (exp_terms / total).astype(jnp.bfloat16)
    step = head * blocks + block
    slots[head * blocks + dest] = jnp.dot(probs, value_half[...], preferred_element_type=jnp.float32).astype(
        slots.dtype
    )

    def remote(h, i):
        return pltpu.make_async_remote_copy(
            src_ref=slots.at[h * blocks + i],
            dst_ref=landing.at[me, h],
            send_sem=send_sem.at[h * blocks + i],
            recv_sem=recv_sem.at[me, h],
            device_id=(row, i),
            device_id_type=MESH,
        )

    def local(h):
        return pltpu.make_async_copy(
            slots.at[h * blocks + me], landing.at[me, h], local_sem.at[h]
        )

    @pl.when(dest != me)
    def _():
        remote(head, dest).start()

    @pl.when(dest == me)
    def _():
        local(head).start()

    @pl.when(step == heads * blocks - 1)
    def _():
        for h in range(slots.shape[0] // o_ref.shape[0]):
            local(h).wait()
            for i in range(o_ref.shape[0]):
                @pl.when(i != me)
                def _():
                    remote(h, i).wait_send()
                    pltpu.make_async_remote_copy(
                        src_ref=slots.at[h * blocks + i],
                        dst_ref=landing.at[i, h],
                        send_sem=send_sem.at[h * blocks + i],
                        recv_sem=recv_sem.at[i, h],
                        device_id=(row, i),
                        device_id_type=MESH,
                    ).wait_recv()
        o_ref[...] = landing[...]


def attend_kernel(projected_t, query_rs, key_rs, qk_gain, row_segments, block_len, scale):
    length = projected_t.shape[1]
    heads_here = projected_t.shape[0] // (3 * HEAD_DIM)
    width = heads_here * HEAD_DIM
    blocks = length // block_len
    flops = 4 * length * length * width
    gain_block = pl.BlockSpec((HEAD_DIM, 1), lambda h, i: (h, 0))
    return pl.pallas_call(
        functools.partial(attention_kernel, scale),
        out_shape=jax.ShapeDtypeStruct((blocks, heads_here, block_len, HEAD_DIM), jnp.bfloat16),
        grid=(heads_here, blocks),
        in_specs=[
            pl.BlockSpec((HEAD_DIM, length), lambda h, i: (3 * h, 0)),
            pl.BlockSpec((HEAD_DIM, length), lambda h, i: (3 * h + 1, 0)),
            pl.BlockSpec((HEAD_DIM, length), lambda h, i: (3 * h + 2, 0)),
            pl.BlockSpec((1, length), lambda h, i: (0, 0)),
            pl.BlockSpec((1, length), lambda h, i: (0, 0)),
            gain_block,
            gain_block,
            pl.BlockSpec((length, 1), lambda h, i: (0, 0)),
            pl.BlockSpec((1, length), lambda h, i: (0, 0)),
        ],
        out_specs=pl.BlockSpec(memory_space=pltpu.VMEM),
        scratch_shapes=[
            pltpu.VMEM((length, HEAD_DIM), jnp.bfloat16),
            pltpu.VMEM((length, HEAD_DIM), jnp.bfloat16),
            pltpu.VMEM((heads_here * blocks, block_len, HEAD_DIM), jnp.bfloat16),
            pltpu.VMEM((blocks, heads_here, block_len, HEAD_DIM), jnp.bfloat16),
            pltpu.SemaphoreType.DMA((heads_here * blocks,)),
            pltpu.SemaphoreType.DMA((blocks, heads_here)),
            pltpu.SemaphoreType.DMA((heads_here,)),
        ],
        compiler_params=pltpu.CompilerParams(collective_id=2, has_side_effects=True),
        cost_estimate=pl.CostEstimate(
            flops=flops, transcendentals=length * length * heads_here, bytes_accessed=12 * length * width
        ),
    )(
        projected_t,
        projected_t,
        projected_t,
        query_rs.reshape(1, length),
        key_rs.reshape(1, length),
        qk_gain[0].reshape(width, 1),
        qk_gain[1].reshape(width, 1),
        row_segments.reshape(length, 1),
        row_segments.reshape(1, length),
    )


def out_proj_kernel(att_ref, w_ref, res_ref, ls_ref, o_ref, sum_ref):
    total = jnp.zeros(o_ref.shape, jnp.float32)
    for g in range(att_ref.shape[0]):
        heads = jnp.concatenate([att_ref[g, 0], att_ref[g, 1]], axis=1)
        weights = w_ref[g].reshape(2 * HEAD_DIM, w_ref.shape[-1])
        term = jnp.dot(heads, weights, preferred_element_type=jnp.float32)
        total = total + term.astype(jnp.bfloat16).astype(jnp.float32)
    hidden = res_ref[...].astype(jnp.float32) + ls_ref[...] * total
    o_ref[...] = hidden

    @pl.when(pl.program_id(0) == 0)
    def _():
        sum_ref[...] = jnp.zeros(sum_ref.shape, jnp.float32)

    sum_ref[...] += jnp.sum(hidden, axis=1, keepdims=True)


def out_proj(attended, out_weight_groups, residual, layer_scale, tile=640):
    groups, heads_here, tokens, _ = attended.shape
    width = out_weight_groups.shape[-1]
    return pl.pallas_call(
        out_proj_kernel,
        out_shape=(
            jax.ShapeDtypeStruct((tokens, width), jnp.float32),
            jax.ShapeDtypeStruct((tokens, 1), jnp.float32),
        ),
        grid=(width // tile,),
        in_specs=[
            pl.BlockSpec(attended.shape, lambda j: (0, 0, 0, 0)),
            pl.BlockSpec((groups, heads_here, HEAD_DIM, tile), lambda j: (0, 0, 0, j)),
            pl.BlockSpec((tokens, tile), lambda j: (0, j)),
            pl.BlockSpec((1, tile), lambda j: (0, j)),
        ],
        out_specs=(
            pl.BlockSpec((tokens, tile), lambda j: (0, j)),
            pl.BlockSpec((tokens, 1), lambda j: (0, 0)),
        ),
        cost_estimate=pl.CostEstimate(
            flops=2 * tokens * groups * heads_here * HEAD_DIM * width,
            transcendentals=0,
            bytes_accessed=groups * heads_here * HEAD_DIM * width * 2 + tokens * width * 6,
        ),
    )(attended, out_weight_groups, residual, layer_scale.reshape(1, width))


def per_device(
    residual_in,
    norm_gain,
    qkv_weight,
    qk_gain,
    out_weight,
    layer_scale,
    segment_ids,
    pad_mask,
    ln_weight,
    ln_bias,
    fc_weight,
    fc_bias,
    owner,
):
    seq_count = lax.axis_size("seq")
    seq_me = lax.axis_index("seq")
    tokens = residual_in[0].astype(jnp.float32)
    shard_rows = tokens.shape[0]
    normed = (
        tokens * lax.rsqrt(jnp.mean(tokens * tokens, axis=-1, keepdims=True) + 1e-06) * norm_gain
    ).astype(jnp.bfloat16)
    row_tokens = lax.all_gather(normed, "seq", axis=0, tiled=True)
    length = row_tokens.shape[0]
    heads_here = qkv_weight.shape[1] // (3 * HEAD_DIM)
    projected_t = jnp.dot(row_tokens, qkv_weight, preferred_element_type=jnp.float32).T
    parts_t = projected_t.reshape(heads_here, 3, HEAD_DIM, length)
    seg_spread = lax.dynamic_update_slice_in_dim(
        jnp.zeros((length,), jnp.float32),
        segment_ids[0].astype(jnp.float32),
        seq_me * shard_rows,
        0,
    )
    stats = seq_sum(
        jnp.stack(
            [
                jnp.sum(parts_t[:, 0] * parts_t[:, 0], axis=(0, 1)),
                jnp.sum(parts_t[:, 1] * parts_t[:, 1], axis=(0, 1)),
                seg_spread,
            ]
        )
    )
    query_sq, key_sq, row_segments = stats[0], stats[1], stats[2]
    norm_width = HEADS * HEAD_DIM
    scale = HEAD_DIM ** (-0.5)
    attended = attend_kernel(
        projected_t,
        lax.rsqrt(query_sq / norm_width + 1e-06),
        lax.rsqrt(key_sq / norm_width + 1e-06),
        qk_gain,
        row_segments,
        256,
        scale,
    )
    full_out_weight = lax.all_gather(out_weight, "seq", axis=0, tiled=False)
    half_grid = GRID // 2
    lines = shard_rows // (2 * GRID)
    merged_count = shard_rows // 4

    def shuffle_rows(x, axis):
        shape = x.shape
        split = shape[:axis] + (lines, 2, half_grid, 2) + shape[axis + 1:]
        order = list(range(axis)) + [axis, axis + 2, axis + 1, axis + 3] + list(
            range(axis + 4, len(split))
        )
        return jnp.transpose(x.reshape(split), order).reshape(shape)

    hidden, row_sums = out_proj(
        shuffle_rows(attended, 2),
        full_out_weight.reshape(seq_count, heads_here, HEAD_DIM, -1),
        shuffle_rows(residual_in[0], 0),
        layer_scale,
    )
    merged = hidden.reshape(merged_count, 4 * D)
    centre = merged - jnp.sum(row_sums.reshape(merged_count, 4), axis=1, keepdims=True) / (4 * D)
    spread = jnp.mean(centre * centre, axis=-1, keepdims=True)
    merged_norm = (centre * lax.rsqrt(spread + 1e-05) * ln_weight + ln_bias).astype(jnp.bfloat16)
    merged_mask = (
        pad_mask[0]
        .reshape(lines, 2, half_grid, 2)[:, 0, :, 0]
        .reshape(merged_count)
        .astype(jnp.float32)
    )
    row_count = lax.axis_size("rows")
    row_me = lax.axis_index("rows")
    slabs = lax.all_to_all(merged_norm, "rows", split_axis=1, concat_axis=0, tiled=True)
    owner_hot = (owner[None, :] == jnp.arange(row_count, dtype=jnp.int32)[:, None]).astype(
        jnp.bfloat16
    )
    ordered = jnp.einsum(
        "jp,pms->jms",
        owner_hot,
        slabs.reshape(row_count, merged_count, -1),
        preferred_element_type=jnp.float32,
    ).astype(jnp.bfloat16)
    ordered = ordered.reshape(row_count * merged_count, -1)
    partial = jnp.dot(ordered, fc_weight, preferred_element_type=jnp.float32).reshape(
        row_count, merged_count, -1
    )
    own_slot = (jnp.arange(row_count, dtype=jnp.int32) == owner[row_me]).astype(jnp.float32)
    shift = own_slot[:, None] * ((merged_mask - 1.0) * MASK_SHIFT)[None, :]
    partial = (partial + shift[:, :, None]).astype(jnp.bfloat16)
    summed = lax.psum_scatter(
        partial.reshape(row_count * merged_count, -1),
        "rows",
        scatter_dimension=0,
        tiled=True,
    ).astype(jnp.float32)
    pre = summed + fc_bias
    result = pre * (1.0 + lax.erf(pre * (2.0 ** -0.5))) * 0.5
    return result.astype(jnp.bfloat16)[None]


def solution(mesh):
    return jax.shard_map(
        per_device,
        mesh=mesh,
        in_specs=(
            P("rows", "seq", None),
            P(),
            P(None, "seq"),
            P(None, "seq"),
            P("seq", None),
            P(),
            P("rows", "seq"),
            P("rows", "seq"),
            P(),
            P(),
            P("rows", None),
            P(),
            P(),
        ),
        out_specs=P("rows", "seq", None),
        check_vma=False,
    )
```

```python
import functools

import jax
import jax.numpy as jnp
from jax import lax
from jax.experimental import pallas as pl
from jax.experimental.pallas import tpu as pltpu
from jax.sharding import PartitionSpec as P

MESH = pl.DeviceIdType.MESH

D = 3200
HEAD_DIM = 128
HEADS = 16
GRID = 32
MASK_SHIFT = 1e6


def seq_sum_kernel(part_ref, out_ref, slots, send_sem, recv_sem):
    n = slots.shape[0]
    me = lax.axis_index("seq")
    row = lax.axis_index("rows")
    barrier = pltpu.get_barrier_semaphore()
    for k in range(1, n):
        peer = lax.rem(me + k, n)
        pl.semaphore_signal(barrier, inc=1, device_id=(row, peer), device_id_type=MESH)
    pl.semaphore_wait(barrier, n - 1)
    sends = []
    for k in range(1, n):
        peer = lax.rem(me + k, n)
        copy = pltpu.make_async_remote_copy(
            src_ref=part_ref,
            dst_ref=slots.at[me],
            send_sem=send_sem.at[k],
            recv_sem=recv_sem.at[me],
            device_id=(row, peer),
            device_id_type=MESH,
        )
        copy.start()
        sends.append(copy)
    for k in range(1, n):
        src = lax.rem(me + n - k, n)
        pltpu.make_async_remote_copy(
            src_ref=part_ref,
            dst_ref=slots.at[src],
            send_sem=send_sem.at[k],
            recv_sem=recv_sem.at[src],
            device_id=(row, src),
            device_id_type=MESH,
        ).wait_recv()
    for copy in sends:
        copy.wait_send()
    total = jnp.zeros(out_ref.shape, jnp.float32)
    for s in range(n):
        total = total + jnp.where(s == me, part_ref[...], slots[s])
    out_ref[...] = total


def seq_sum(part):
    n = lax.axis_size("seq")
    return pl.pallas_call(
        seq_sum_kernel,
        out_shape=jax.ShapeDtypeStruct(part.shape, jnp.float32),
        in_specs=[pl.BlockSpec(memory_space=pltpu.VMEM)],
        out_specs=pl.BlockSpec(memory_space=pltpu.VMEM),
        scratch_shapes=[
            pltpu.VMEM((n,) + part.shape, jnp.float32),
            pltpu.SemaphoreType.DMA((n,)),
            pltpu.SemaphoreType.DMA((n,)),
        ],
        compiler_params=pltpu.CompilerParams(collective_id=0, has_side_effects=True),
    )(part)


def attention_kernel(scale, q_ref, k_ref, v_ref, qrs_ref, krs_ref, qg_ref, kg_ref, qseg_ref,
                     kseg_ref, o_ref, key_norm, value_half, slots, landing, send_sem, recv_sem, local_sem):
    head, block = pl.program_id(0), pl.program_id(1)
    blocks = pl.num_programs(1)
    heads = pl.num_programs(0)
    me = lax.axis_index("seq")
    row = lax.axis_index("rows")

    @pl.when((head == 0) & (block == 0))
    def _():
        barrier = pltpu.get_barrier_semaphore()
        for k in range(1, o_ref.shape[0]):
            peer = lax.rem(me + k, o_ref.shape[0])
            pl.semaphore_signal(barrier, inc=1, device_id=(row, peer), device_id_type=MESH)
        pl.semaphore_wait(barrier, o_ref.shape[0] - 1)

    @pl.when(block == 0)
    def _():
        key_norm[...] = jnp.transpose(
            (k_ref[...] * krs_ref[...] * kg_ref[...]).astype(jnp.bfloat16)
        )
        value_half[...] = jnp.transpose(v_ref[...].astype(jnp.bfloat16))

    dest = lax.rem(me + 1 + block, blocks)
    width = slots.shape[1]
    start = pl.multiple_of(dest * width, width)
    query_norm = jnp.transpose(
        (q_ref[:, pl.ds(start, width)] * qrs_ref[:, pl.ds(start, width)] * qg_ref[...]).astype(
            jnp.bfloat16
        )
    )
    scores = (
        lax.dot_general(
            query_norm, key_norm[...], (((1,), (1,)), ((), ())), preferred_element_type=jnp.float32
        )
        * scale
    )
    scores = jnp.where(qseg_ref[pl.ds(start, width), :] == kseg_ref[...], scores, -1e30)
    peak_val = jnp.max(scores, axis=-1, keepdims=True)
    exp_terms = jnp.exp(scores - peak_val)
    total = jnp.sum(exp_terms, axis=-1, keepdims=True)
    probs = (exp_terms / total).astype(jnp.bfloat16)
    step = head * blocks + block
    slots[head * blocks + dest] = jnp.dot(probs, value_half[...], preferred_element_type=jnp.float32).astype(
        slots.dtype
    )

    def remote(h, i):
        return pltpu.make_async_remote_copy(
            src_ref=slots.at[h * blocks + i],
            dst_ref=landing.at[me, h],
            send_sem=send_sem.at[h * blocks + i],
            recv_sem=recv_sem.at[me, h],
            device_id=(row, i),
            device_id_type=MESH,
        )

    def local(h):
        return pltpu.make_async_copy(
            slots.at[h * blocks + me], landing.at[me, h], local_sem.at[h]
        )

    @pl.when(dest != me)
    def _():
        remote(head, dest).start()

    @pl.when(dest == me)
    def _():
        local(head).start()

    @pl.when(step == heads * blocks - 1)
    def _():
        for h in range(slots.shape[0] // o_ref.shape[0]):
            local(h).wait()
            for i in range(o_ref.shape[0]):
                @pl.when(i != me)
                def _():
                    remote(h, i).wait_send()
                    pltpu.make_async_remote_copy(
                        src_ref=slots.at[h * blocks + i],
                        dst_ref=landing.at[i, h],
                        send_sem=send_sem.at[h * blocks + i],
                        recv_sem=recv_sem.at[i, h],
                        device_id=(row, i),
                        device_id_type=MESH,
                    ).wait_recv()
        o_ref[...] = landing[...]


def attend_kernel(projected_t, query_rs, key_rs, qk_gain, row_segments, block_len, scale):
    length = projected_t.shape[1]
    heads_here = projected_t.shape[0] // (3 * HEAD_DIM)
    width = heads_here * HEAD_DIM
    blocks = length // block_len
    flops = 4 * length * length * width
    gain_block = pl.BlockSpec((HEAD_DIM, 1), lambda h, i: (h, 0))
    return pl.pallas_call(
        functools.partial(attention_kernel, scale),
        out_shape=jax.ShapeDtypeStruct((blocks, heads_here, block_len, HEAD_DIM), jnp.bfloat16),
        grid=(heads_here, blocks),
        in_specs=[
            pl.BlockSpec((HEAD_DIM, length), lambda h, i: (3 * h, 0)),
            pl.BlockSpec((HEAD_DIM, length), lambda h, i: (3 * h + 1, 0)),
            pl.BlockSpec((HEAD_DIM, length), lambda h, i: (3 * h + 2, 0)),
            pl.BlockSpec((1, length), lambda h, i: (0, 0)),
            pl.BlockSpec((1, length), lambda h, i: (0, 0)),
            gain_block,
            gain_block,
            pl.BlockSpec((length, 1), lambda h, i: (0, 0)),
            pl.BlockSpec((1, length), lambda h, i: (0, 0)),
        ],
        out_specs=pl.BlockSpec(memory_space=pltpu.VMEM),
        scratch_shapes=[
            pltpu.VMEM((length, HEAD_DIM), jnp.bfloat16),
            pltpu.VMEM((length, HEAD_DIM), jnp.bfloat16),
            pltpu.VMEM((heads_here * blocks, block_len, HEAD_DIM), jnp.bfloat16),
            pltpu.VMEM((blocks, heads_here, block_len, HEAD_DIM), jnp.bfloat16),
            pltpu.SemaphoreType.DMA((heads_here * blocks,)),
            pltpu.SemaphoreType.DMA((blocks, heads_here)),
            pltpu.SemaphoreType.DMA((heads_here,)),
        ],
        compiler_params=pltpu.CompilerParams(collective_id=2, has_side_effects=True),
        cost_estimate=pl.CostEstimate(
            flops=flops, transcendentals=length * length * heads_here, bytes_accessed=12 * length * width
        ),
    )(
        projected_t,
        projected_t,
        projected_t,
        query_rs.reshape(1, length),
        key_rs.reshape(1, length),
        qk_gain[0].reshape(width, 1),
        qk_gain[1].reshape(width, 1),
        row_segments.reshape(length, 1),
        row_segments.reshape(1, length),
    )


def out_proj_kernel(att_ref, w_ref, res_ref, ls_ref, o_ref, sum_ref):
    total = jnp.zeros(o_ref.shape, jnp.float32)
    for g in range(att_ref.shape[0]):
        heads = jnp.concatenate([att_ref[g, 0], att_ref[g, 1]], axis=1)
        weights = w_ref[g].reshape(2 * HEAD_DIM, w_ref.shape[-1])
        term = jnp.dot(heads, weights, preferred_element_type=jnp.float32)
        total = total + term.astype(jnp.bfloat16).astype(jnp.float32)
    hidden = res_ref[...].astype(jnp.float32) + ls_ref[...] * total
    o_ref[...] = hidden

    @pl.when(pl.program_id(0) == 0)
    def _():
        sum_ref[...] = jnp.zeros(sum_ref.shape, jnp.float32)

    sum_ref[...] += jnp.sum(hidden, axis=1, keepdims=True)


def out_proj(attended, out_weight_groups, residual, layer_scale, tile=640):
    groups, heads_here, tokens, _ = attended.shape
    width = out_weight_groups.shape[-1]
    return pl.pallas_call(
        out_proj_kernel,
        out_shape=(
            jax.ShapeDtypeStruct((tokens, width), jnp.float32),
            jax.ShapeDtypeStruct((tokens, 1), jnp.float32),
        ),
        grid=(width // tile,),
        in_specs=[
            pl.BlockSpec(attended.shape, lambda j: (0, 0, 0, 0)),
            pl.BlockSpec((groups, heads_here, HEAD_DIM, tile), lambda j: (0, 0, 0, j)),
            pl.BlockSpec((tokens, tile), lambda j: (0, j)),
            pl.BlockSpec((1, tile), lambda j: (0, j)),
        ],
        out_specs=(
            pl.BlockSpec((tokens, tile), lambda j: (0, j)),
            pl.BlockSpec((tokens, 1), lambda j: (0, 0)),
        ),
        cost_estimate=pl.CostEstimate(
            flops=2 * tokens * groups * heads_here * HEAD_DIM * width,
            transcendentals=0,
            bytes_accessed=groups * heads_here * HEAD_DIM * width * 2 + tokens * width * 6,
        ),
    )(attended, out_weight_groups, residual, layer_scale.reshape(1, width))


def per_device(
    residual_in,
    norm_gain,
    qkv_weight,
    qk_gain,
    out_weight,
    layer_scale,
    segment_ids,
    pad_mask,
    ln_weight,
    ln_bias,
    fc_weight,
    fc_bias,
    owner,
):
    seq_count = lax.axis_size("seq")
    seq_me = lax.axis_index("seq")
    tokens = residual_in[0].astype(jnp.float32)
    shard_rows = tokens.shape[0]
    normed = (
        tokens * lax.rsqrt(jnp.mean(tokens * tokens, axis=-1, keepdims=True) + 1e-06) * norm_gain
    ).astype(jnp.bfloat16)
    row_tokens = lax.all_gather(normed, "seq", axis=0, tiled=True)
    length = row_tokens.shape[0]
    heads_here = qkv_weight.shape[1] // (3 * HEAD_DIM)
    projected_t = jnp.dot(row_tokens, qkv_weight, preferred_element_type=jnp.float32).T
    parts_t = projected_t.reshape(heads_here, 3, HEAD_DIM, length)
    seg_spread = lax.dynamic_update_slice_in_dim(
        jnp.zeros((length,), jnp.float32),
        segment_ids[0].astype(jnp.float32),
        seq_me * shard_rows,
        0,
    )
    stats = seq_sum(
        jnp.stack(
            [
                jnp.sum(parts_t[:, 0] * parts_t[:, 0], axis=(0, 1)),
                jnp.sum(parts_t[:, 1] * parts_t[:, 1], axis=(0, 1)),
                seg_spread,
            ]
        )
    )
    query_sq, key_sq, row_segments = stats[0], stats[1], stats[2]
    norm_width = HEADS * HEAD_DIM
    scale = HEAD_DIM ** (-0.5)
    attended = attend_kernel(
        projected_t,
        lax.rsqrt(query_sq / norm_width + 1e-06),
        lax.rsqrt(key_sq / norm_width + 1e-06),
        qk_gain,
        row_segments,
        256,
        scale,
    )
    full_out_weight = lax.all_gather(out_weight, "seq", axis=0, tiled=False)
    half_grid = GRID // 2
    lines = shard_rows // (2 * GRID)
    merged_count = shard_rows // 4

    def shuffle_rows(x, axis):
        shape = x.shape
        split = shape[:axis] + (lines, 2, half_grid, 2) + shape[axis + 1:]
        order = list(range(axis)) + [axis, axis + 2, axis + 1, axis + 3] + list(
            range(axis + 4, len(split))
        )
        return jnp.transpose(x.reshape(split), order).reshape(shape)

    hidden, row_sums = out_proj(
        shuffle_rows(attended, 2),
        full_out_weight.reshape(seq_count, heads_here, HEAD_DIM, -1),
        shuffle_rows(residual_in[0], 0),
        layer_scale,
    )
    merged = hidden.reshape(merged_count, 4 * D)
    centre = merged - jnp.sum(row_sums.reshape(merged_count, 4), axis=1, keepdims=True) / (4 * D)
    spread = jnp.mean(centre * centre, axis=-1, keepdims=True)
    merged_norm = (centre * lax.rsqrt(spread + 1e-05) * ln_weight + ln_bias).astype(jnp.bfloat16)
    merged_norm = lax.optimization_barrier(merged_norm)
    merged_mask = (
        pad_mask[0]
        .reshape(lines, 2, half_grid, 2)[:, 0, :, 0]
        .reshape(merged_count)
        .astype(jnp.float32)
    )
    row_count = lax.axis_size("rows")
    row_me = lax.axis_index("rows")
    slabs = lax.all_to_all(merged_norm, "rows", split_axis=1, concat_axis=0, tiled=True)
    owner_hot = (owner[None, :] == jnp.arange(row_count, dtype=jnp.int32)[:, None]).astype(
        jnp.bfloat16
    )
    ordered = jnp.einsum(
        "jp,pms->jms",
        owner_hot,
        slabs.reshape(row_count, merged_count, -1),
        preferred_element_type=jnp.float32,
    ).astype(jnp.bfloat16)
    ordered = ordered.reshape(row_count * merged_count, -1)
    partial = jnp.dot(ordered, fc_weight, preferred_element_type=jnp.float32).reshape(
        row_count, merged_count, -1
    )
    own_slot = (jnp.arange(row_count, dtype=jnp.int32) == owner[row_me]).astype(jnp.float32)
    shift = own_slot[:, None] * ((merged_mask - 1.0) * MASK_SHIFT)[None, :]
    partial = (partial + shift[:, :, None]).astype(jnp.bfloat16)
    summed = lax.psum_scatter(
        partial.reshape(row_count * merged_count, -1),
        "rows",
        scatter_dimension=0,
        tiled=True,
    ).astype(jnp.float32)
    pre = summed + fc_bias
    result = pre * (1.0 + lax.erf(pre * (2.0 ** -0.5))) * 0.5
    return result.astype(jnp.bfloat16)[None]


def solution(mesh):
    return jax.shard_map(
        per_device,
        mesh=mesh,
        in_specs=(
            P("rows", "seq", None),
            P(),
            P(None, "seq"),
            P(None, "seq"),
            P("seq", None),
            P(),
            P("rows", "seq"),
            P("rows", "seq"),
            P(),
            P(),
            P("rows", None),
            P(),
            P(),
        ),
        out_specs=P("rows", "seq", None),
        check_vma=False,
    )
```
